32 devices in a mesh: ctx: 8 (over z, x), exp: 4 (over y, core).
Axes of the slice: x: 2, y: 2, z: 4, core: 2. Of those that a mesh axis runs over, the one named last changes fastest.
Arguments:
- tokens: bfloat16 [4, 1024, 2048], P('exp', 'ctx'), may hold values from -6 to 6
- doc_ids: int32 [4, 1024], P('exp', 'ctx'), may hold values from 0 to 3, never falling along the last dimension, each value on 1 to 512 neighbouring positions
- expert_ids: int32 [4, 1024, 8], P('exp', 'ctx'), may hold values from 0 to 15, all different within a row
- drop_order: int32 [4, 8, 128], P('exp', 'ctx'), may hold values from 0 to 127, each once within a row
- w_query: bfloat16 [2048, 2048], P(('ctx', 'exp')), may hold values from -0.125 to 0.125
- w_key: bfloat16 [2048, 2048], P(('ctx', 'exp')), may hold values from -0.125 to 0.125
- w_value: bfloat16 [2048, 2048], P(('ctx', 'exp')), may hold values from -0.125 to 0.125
- w_out: bfloat16 [2048, 2048], P(('ctx', 'exp')), may hold values from -1 to 1
- w_router: bfloat16 [2048, 16], P(('ctx', 'exp')), may hold values from -0.25 to 0.25
- gain_attn: bfloat16 [2048], P(('ctx', 'exp')), may hold values from 0.099609375 to 1.8984375
- gain_query: bfloat16 [2048], P(('ctx', 'exp')), may hold values from 0.099609375 to 1.8984375
- gain_key: bfloat16 [2048], P(('ctx', 'exp')), may hold values from 0.099609375 to 1.8984375
- gain_ffn: bfloat16 [2048], P(('ctx', 'exp')), may hold values from 0.099609375 to 1.8984375
- w_gate: bfloat16 [16, 2048, 1024], P('exp', 'ctx'), may hold values from -0.125 to 0.125
- w_up: bfloat16 [16, 2048, 1024], P('exp', 'ctx'), may hold values from -0.125 to 0.125
- w_down: bfloat16 [16, 1024, 2048], P('exp', None, 'ctx'), may hold values from -1.5 to 1.5
- cotangent: bfloat16 [4, 1024, 2048], P('exp', 'ctx'), may hold values from -6 to 6
Outputs:
- output: bfloat16 [4, 1024, 2048], P('exp', 'ctx')
- grad_tokens: float32 [4, 1024, 2048], P('exp', 'ctx')
- grad_query: float32 [2048, 2048], P(('ctx', 'exp'))
- grad_key: float32 [2048, 2048], P(('ctx', 'exp'))
- grad_value: float32 [2048, 2048], P(('ctx', 'exp'))
- grad_out: float32 [2048, 2048], P(('ctx', 'exp'))
- grad_router: float32 [2048, 16], P(('ctx', 'exp'))
- grad_gain_attn: float32 [2048], P(('ctx', 'exp'))
- grad_gain_query: float32 [2048], P(('ctx', 'exp'))
- grad_gain_key: float32 [2048], P(('ctx', 'exp'))
- grad_gain_ffn: float32 [2048], P(('ctx', 'exp'))
- grad_gate: float32 [16, 2048, 1024], P('exp', 'ctx')
- grad_up: float32 [16, 2048, 1024], P('exp', 'ctx')
- grad_down: float32 [16, 1024, 2048], P('exp', None, 'ctx')
The draws below stay inside these ranges and needn't reach their ends.
Inputs may be any that keep to these rules, and one draw needn't show every extreme that they name: `expert_ids`: each token names 8 different experts. `drop_order`: within each block of 128 positions of a sequence every number appears once. `doc_ids`: never falls along a sequence; a document has at most 1024 // 2 positions, and one has exactly that many.
All inputs are finite; a program needn't handle non-finite values.
Results may differ from the reference program's by a relative error of at most 0.02.
Values may be sent and summed in bfloat16 or wider, within the bound.
No kernel may reach another device: no remote copies, remote signals or barrier semaphores. Data moves between devices by JAX's collectives and lax.ppermute only.
A program may use at most 320 MiB of HBM per device.

```python
import math
import jax
import jax.numpy as jnp
import numpy as np
from jax import lax

D = 2048
H = 16
HD = 128
F = 1024
TOPK = 8
EXPERTS = 16
WINDOW = 1024
DOCS = 4
TOK_DEV = 128
LEN = 1024
SEQS = 4
CAP = 64
N_CTX = 8


def levels(key, extent, pieces, low, largest):
    loudness = 1.0
    for position, shards_of in pieces:
        draws = jax.random.uniform(jax.random.fold_in(jax.random.fold_in(key, 6), position), (shards_of,), jnp.float32, low / len(pieces), largest / len(pieces))
        loudness = loudness * jnp.repeat(jnp.exp(draws), extent[position] // shards_of).reshape((-1,) + (1,) * (len(extent) - 1 - position))
    return loudness


def picks_of(key, rows, number_of, top, lift):
    sequence = jax.random.permutation(jax.random.fold_in(key, 1), number_of)
    pull = sequence
    for power in range(3):
        pull = pull * pull // number_of
    pull = pull * lift // number_of
    tickets = jax.random.randint(jax.random.fold_in(key, 2), (rows, number_of), 0, 4096) + pull
    fixed_rows = jax.random.permutation(jax.random.fold_in(key, 3), rows)[jnp.arange(number_of) % rows]
    tickets = jnp.where(jnp.arange(rows)[:, None] == fixed_rows[None, :], 1 << 14, tickets)
    score = tickets * number_of + jnp.arange(number_of)
    return lax.top_k(score.astype(jnp.int32), top)[1].astype(jnp.int32)


def profile(count, total, most, lean):
    loads = [(1 << 20) // math.isqrt(rank ** lean) + 1 for rank in range(2, count + 1)]
    spare, given = total - most - (count - 1), [1] * (count - 1)
    while spare > 0:
        free = [i for i in range(count - 1) if given[i] < most]
        mass, remaining = sum([loads[i] for i in free]), spare
        for i in free:
            more = min(most - given[i], max(1, remaining * loads[i] // mass), spare)
            given[i] = given[i] + more
            spare = spare - more
    return np.array([most] + given)


def uneven(stream_key, count, total, reach, lean):
    if count == 2:
        one = jax.random.randint(stream_key, (), max(1, total - reach), min(reach, total - 1) + 1)
        return jnp.stack([one, total - one])
    lengths = jnp.asarray(profile(count, total, reach, lean), jnp.int32)
    twos = (count - 1) // 2
    source_of, taker = lengths[1:1 + 2 * twos:2], lengths[2:2 + 2 * twos:2]
    slack = jnp.minimum(source_of - 1, reach - taker)
    passed = jax.random.randint(jax.random.fold_in(stream_key, 1), (twos,), 0, 1 << 20) % (slack + 1)
    lengths = lengths.at[1:1 + 2 * twos:2].set(source_of - passed).at[2:2 + 2 * twos:2].set(taker + passed)
    return lengths[jax.random.permutation(jax.random.fold_in(stream_key, 2), count)]


def centred(stream_key, dims, spread, limit, pieces=(), kind=jnp.bfloat16):
    values = spread * jax.random.normal(stream_key, dims, jnp.float32)
    if pieces:
        values = values * levels(stream_key, dims, pieces, -0.22, 0.18)
    return jnp.clip(values, -limit, limit).astype(kind)


def setup_inputs(seed: int = 0) -> dict:
    key_list = jax.random.split(jax.random.key(seed), 18)
    return {
        "tokens": centred(key_list[0], (SEQS, LEN, D), 1.0, 6.0, ((0, 4), (1, 8))),
        "doc_ids": jax.vmap(lambda own: jnp.searchsorted(jnp.cumsum(uneven(own, DOCS, LEN, LEN // 2, 1)), jnp.arange(LEN), side="right"))(jax.random.split(key_list[1], SEQS)).reshape((SEQS, LEN)).astype(jnp.int32),
        "expert_ids": picks_of(key_list[2], SEQS * LEN, EXPERTS, TOPK, 4096).reshape((SEQS, LEN, TOPK)),
        "drop_order": jax.vmap(lambda own: jax.random.permutation(own, TOK_DEV))(jax.random.split(key_list[3], SEQS * N_CTX)).reshape((SEQS, N_CTX, TOK_DEV)).astype(jnp.int32),
        "w_query": centred(key_list[4], (D, D), D ** -0.5, 0.125, ((0, 32),)),
        "w_key": centred(key_list[5], (D, D), D ** -0.5, 0.125, ((0, 32),)),
        "w_value": centred(key_list[6], (D, D), D ** -0.5, 0.125, ((0, 32),)),
        "w_out": centred(key_list[7], (D, D), (max(D // 64, 1)) ** -0.5, 1.0, ((0, 32),)),
        "w_router": centred(key_list[8], (D, EXPERTS), (D // 4) ** -0.5, 0.25, ((0, 32),)),
        "gain_attn": jnp.clip(1.0 + 0.18 * jax.random.normal(key_list[9], (D,), jnp.float32), 0.099609375, 1.8984375).astype(jnp.bfloat16),
        "gain_query": jnp.clip(1.0 + 0.18 * jax.random.normal(key_list[10], (D,), jnp.float32), 0.099609375, 1.8984375).astype(jnp.bfloat16),
        "gain_key": jnp.clip(1.0 + 0.18 * jax.random.normal(key_list[11], (D,), jnp.float32), 0.099609375, 1.8984375).astype(jnp.bfloat16),
        "gain_ffn": jnp.clip(1.0 + 0.18 * jax.random.normal(key_list[12], (D,), jnp.float32), 0.099609375, 1.8984375).astype(jnp.bfloat16),
        "w_gate": centred(key_list[13], (EXPERTS, D, F), D ** -0.5, 0.125, ((0, 4), (1, 8))),
        "w_up": centred(key_list[14], (EXPERTS, D, F), D ** -0.5, 0.125, ((0, 4), (1, 8))),
        "w_down": centred(key_list[15], (EXPERTS, F, D), (max(F // 64, 1)) ** -0.5, 1.5, ((0, 4), (2, 8))),
        "cotangent": centred(key_list[16], (SEQS, LEN, D), 1.0, 6.0, ((0, 4), (1, 8))),
    }


EPS = 1e-05
NEG = -1000000000.0
HIGH = lax.Precision.HIGHEST

@jax.custom_vjp
def low(v):
    return lax.optimization_barrier(v.astype(jnp.bfloat16)).astype(jnp.float32)

@jax.custom_vjp
def low_back(v):
    return v

def low_keep(v):
    return (low(v), None)

def low_pass(kept, grad):
    return (grad,)

def back_keep(v):
    return (v, None)

def back_low(kept, grad):
    return (low(grad),)
low.defvjp(low_keep, low_pass)
low_back.defvjp(back_keep, back_low)

def matmul(left, right):
    return jnp.dot(left, right, precision=HIGH, preferred_element_type=jnp.float32)

def inv_root(values):
    return lax.rsqrt(lax.optimization_barrier(jnp.mean(values * values, axis=-1, keepdims=True)) + EPS)

def angles(positions):
    half = HD // 2
    freqs = 10000.0 ** (-2.0 * jnp.arange(half, dtype=jnp.float32) / HD)
    angle = positions.astype(jnp.float32)[:, None] * freqs[None, :]
    return (jnp.cos(angle)[:, None, :], jnp.sin(angle)[:, None, :])

def rotate(values, cosine, sine, sign):
    half = values.shape[-1] // 2
    first = values[..., :half]
    second = values[..., half:]
    return jnp.concatenate([first * cosine - sign * second * sine, second * cosine + sign * first * sine], axis=-1)

def sequence_forward(params, inputs, docs, named_ids, order):
    query_weight, key_weight, value_weight, out_weight, router_weight, attn_gain, query_gain, key_gain, ffn_gain, gate_weight, up_weight, down_weight = params
    positions = jnp.arange(LEN, dtype=jnp.int32)
    normed_first = inputs * inv_root(inputs)
    hidden_first = low(normed_first * attn_gain)
    query_raw = low_back(matmul(hidden_first, query_weight))
    key_raw = low_back(matmul(hidden_first, key_weight))
    values = low(low_back(matmul(hidden_first, value_weight)))
    cosine, sine = angles(positions)
    queries = low(rotate((query_raw * inv_root(query_raw) * query_gain).reshape(LEN, H, HD), cosine, sine, 1.0))
    keys = low(rotate((key_raw * inv_root(key_raw) * key_gain).reshape(LEN, H, HD), cosine, sine, 1.0))
    value_heads = values.reshape(LEN, H, HD)
    span = min(512, LEN)
    blocks = LEN // span

    def attend(index):
        start = index * span
        query_block = lax.dynamic_slice_in_dim(queries, start, span, 0)
        query_pos = start + jnp.arange(span, dtype=jnp.int32)
        query_docs = lax.dynamic_slice_in_dim(docs, start, span, 0)
        raw = jnp.einsum('qhd,khd->hqk', query_block, keys, precision=HIGH) * HD ** (-0.5)
        offset = query_pos[:, None] - positions[None, :]
        allowed = (offset >= 0) & (offset < WINDOW) & (query_docs[:, None] == docs[None, :])
        scores = low_back(jnp.where(allowed[None], raw, NEG))
        weights = low(jax.nn.softmax(scores, axis=-1))
        return jnp.einsum('hqk,khd->qhd', weights, value_heads, precision=HIGH).reshape(span, D)
    attended = lax.map(jax.checkpoint(attend), jnp.arange(blocks, dtype=jnp.int32)).reshape(LEN, D)
    attended = low(low_back(attended))
    resid = inputs + low_back(matmul(attended, out_weight))
    normed_second = resid * inv_root(resid)
    hidden_second = low(normed_second * ffn_gain)
    logits = low_back(matmul(hidden_second, router_weight))
    router_probs = jax.nn.softmax(logits, axis=-1)
    expert_iota = jnp.arange(EXPERTS, dtype=jnp.int32)
    named = lax.optimization_barrier(jnp.sum((named_ids[:, :, None] == expert_iota[None, None, :]).astype(jnp.int32), axis=1))
    named_blocks = named.reshape(N_CTX, TOK_DEV, EXPERTS)
    earlier = (order[:, None, :] < order[:, :, None]).astype(jnp.int32)
    slots = jnp.einsum('ntu,nue->nte', earlier, named_blocks).reshape(LEN, EXPERTS)
    kept = ((named > 0) & (slots < CAP)).astype(jnp.float32)
    combine = low(router_probs * kept)

    def expert_step(total, index):
        expert_input = low_back(hidden_second)
        gate = low_back(matmul(expert_input, gate_weight[index]))
        upper = low_back(matmul(expert_input, up_weight[index]))
        activated = low(jax.nn.silu(gate) * upper)
        expert_out = low_back(low(matmul(activated, down_weight[index])))
        weight_column = lax.dynamic_slice_in_dim(combine, index, 1, 1)
        return (total + weight_column * expert_out, None)
    mixed, unused = lax.scan(jax.checkpoint(expert_step), jnp.zeros((LEN, D), jnp.float32), jnp.arange(EXPERTS, dtype=jnp.int32))
    return resid + mixed

def reference(tokens, doc_ids, expert_ids, drop_order, w_query, w_key, w_value, w_out, w_router, gain_attn, gain_query, gain_key, gain_ffn, w_gate, w_up, w_down, cotangent):
    params = tuple((weight_item.astype(jnp.float32) for weight_item in (w_query, w_key, w_value, w_out, w_router, gain_attn, gain_query, gain_key, gain_ffn, w_gate, w_up, w_down)))
    inputs = tokens.astype(jnp.float32)

    def forward(param_set, all_inputs):

        def single_sequence(item):
            return sequence_forward(param_set, item[0], item[1], item[2], item[3])
        return lax.map(single_sequence, (all_inputs, doc_ids, expert_ids, drop_order))
    result, pullback = jax.vjp(forward, params, inputs)
    grad_params, grad_inputs = pullback(cotangent.astype(jnp.float32))
    return (result.astype(jnp.bfloat16), grad_inputs, grad_params[0], grad_params[1], grad_params[2], grad_params[3], grad_params[4], grad_params[5], grad_params[6], grad_params[7], grad_params[8], grad_params[9], grad_params[10], grad_params[11])
```

```python
import jax
import jax.numpy as jnp
from jax import lax
from jax.sharding import Mesh, PartitionSpec as P

D = 2048
H = 16
HD = 128
EXPERTS = 16
WINDOW = 1024
CAP = 64

EPS = 1e-05
NEG = -1000000000.0
HIGH = lax.Precision.HIGHEST
F32 = jnp.float32
BF16 = jnp.bfloat16

CTX = ("a", "b")
GROUP = ("a", "exp")
ALL = ("a", "b", "exp")


def dot(left, right):
    return jnp.dot(left, right, preferred_element_type=F32)


def ein(spec, left, right):
    return jnp.einsum(spec, left, right, preferred_element_type=F32)


def exchange(block, axes):
    return lax.all_to_all(block, axes, split_axis=0, concat_axis=0, tiled=True)


def inv_root(values):
    return lax.rsqrt(jnp.mean(values * values, axis=-1, keepdims=True) + EPS)


def norm_back(grad_normed, normed, inverse, gain):
    weighted = grad_normed * gain
    return inverse * (weighted - normed * jnp.mean(weighted * normed, axis=-1, keepdims=True))


def angles(positions):
    half = HD // 2
    freqs = 10000.0 ** (-2.0 * jnp.arange(half, dtype=F32) / HD)
    angle = positions.astype(F32)[:, None] * freqs[None, :]
    return (jnp.cos(angle)[None], jnp.sin(angle)[None])


def rotate(values, cosine, sine, sign):
    half = values.shape[-1] // 2
    first = values[..., :half]
    second = values[..., half:]
    return jnp.concatenate(
        [first * cosine - sign * second * sine, second * cosine + sign * first * sine], axis=-1
    )


def heads_of(values):
    length, width = values.shape
    return values.reshape(length, width // HD, HD).transpose(1, 0, 2)


def flat_of(values):
    heads, length, _ = values.shape
    return values.transpose(1, 0, 2).reshape(length, heads * HD)


def pick(values, index, axis):
    spots = lax.broadcasted_iota(jnp.int32, values.shape, axis)
    return jnp.sum(jnp.where(spots == index, values, jnp.zeros_like(values)), axis=axis)


def shards(
    tokens,
    doc_ids,
    expert_ids,
    drop_order,
    w_query,
    w_key,
    w_value,
    w_out,
    w_router,
    gain_attn,
    gain_query,
    gain_key,
    gain_ffn,
    w_gate,
    w_up,
    w_down,
    cotangent,
):
    n_a, n_b, n_e = (lax.axis_size(name) for name in ALL)
    n_c = n_a * n_b
    n_all = n_c * n_e
    group = n_a * n_e
    length = tokens.shape[1]
    span = n_c * length
    slab = D // n_c
    rows = D // n_all
    at_a, at_b, at_e = (lax.axis_index(name) for name in ALL)
    at_c = at_a * n_b + at_b
    expert = at_e * n_a + at_a

    def to_group_order(values):
        parts = values.reshape(values.shape[0], n_a, n_b, slab).transpose(0, 2, 1, 3)
        twice = jnp.concatenate([parts, parts], axis=1)
        return lax.dynamic_slice_in_dim(twice, at_b, n_b, 1).reshape(values.shape[0], D)

    def from_group_order(values):
        parts = values.reshape(values.shape[0], n_b, n_a, slab)
        twice = jnp.concatenate([parts, parts], axis=1)
        parts = lax.dynamic_slice_in_dim(twice, n_b - at_b, n_b, 1)
        return parts.transpose(0, 2, 1, 3).reshape(values.shape[0], D)

    def from_b(block, distance):
        return lax.ppermute(block, "b", [((i + distance) % n_b, i) for i in range(n_b)])

    vectors = jnp.stack([gain_attn, gain_query, gain_key, gain_ffn])
    small = jnp.concatenate([w_router.T, vectors]).reshape(-1)
    small = jnp.concatenate([small, doc_ids[0].astype(BF16)])
    small = exchange(jnp.broadcast_to(small[None], (n_all, small.shape[0])), ALL)
    params = small[:, : (EXPERTS + 4) * rows].reshape(n_all, EXPERTS + 4, rows)
    params = params.transpose(1, 0, 2).reshape(EXPERTS + 4, D)
    router_weight = params[:EXPERTS]
    attn_gain, query_gain, key_gain, ffn_gain = params[EXPERTS:].astype(F32)
    documents = pick(small[:, (EXPERTS + 4) * rows :].reshape(n_c, n_e, length), at_e, 1)
    documents = documents.reshape(span)
    query_gain = lax.dynamic_slice_in_dim(query_gain, at_c * slab, slab)
    key_gain = lax.dynamic_slice_in_dim(key_gain, at_c * slab, slab)

    whole_tokens = lax.all_gather(tokens[0], CTX, axis=0, tiled=True)
    mine = jnp.stack([w_query, w_key, w_value]).reshape(3, rows, n_c, slab)
    mine = mine.transpose(2, 1, 0, 3).reshape(n_c, rows, 3 * slab)
    mine = exchange(mine, CTX)
    head_weight = lax.all_gather(mine, "exp", axis=1, tiled=True).reshape(D, 3 * slab)
    out_weight = lax.all_gather(w_out, ALL, axis=0, tiled=True)

    def whole_expert(weight):
        own = exchange(weight, "a")
        return [own] + [from_b(own, i) for i in range(1, n_b)]

    gate_parts = whole_expert(w_gate)
    up_parts = whole_expert(w_up)
    down_parts = whole_expert(w_down)

    expert_iota = jnp.arange(EXPERTS, dtype=jnp.int32)
    named = jnp.sum(
        (expert_ids[0][:, :, None] == expert_iota[None, None, :]).astype(F32), axis=1
    )
    order = drop_order[0, 0]
    earlier = (order[None, :] < order[:, None]).astype(F32)
    slots = jnp.dot(earlier, named, precision=HIGH, preferred_element_type=F32)
    kept = named * (slots < CAP).astype(F32)
    slot_code = jnp.where(kept > 0, slots, -1.0).astype(BF16)
    lanes = jnp.zeros((length, HD - EXPERTS), BF16)
    grad_rows_in = cotangent[0]
    grad_output = grad_rows_in.astype(F32)
    grads_all = lax.all_gather(
        jnp.concatenate([to_group_order(grad_rows_in), slot_code, lanes], axis=1), GROUP
    )

    whole_inputs = whole_tokens.astype(F32)
    hidden_first = (whole_inputs * inv_root(whole_inputs) * attn_gain).astype(BF16)
    raw = dot(hidden_first, head_weight)
    query_raw = raw[:, :slab]
    key_raw = raw[:, slab : 2 * slab]
    values = heads_of(raw[:, 2 * slab :].astype(BF16))

    def over_heads(query_sum, key_sum):
        both = jnp.stack([query_sum, key_sum]).reshape(1, 2 * span)
        both = exchange(jnp.broadcast_to(both, (n_c, 2 * span)), CTX)
        both = jnp.sum(both, axis=0).reshape(2, span, 1) / D
        return both[0], both[1]

    query_mean, key_mean = over_heads(
        jnp.sum(query_raw * query_raw, axis=-1), jnp.sum(key_raw * key_raw, axis=-1)
    )
    inv_query = lax.rsqrt(query_mean + EPS)
    inv_key = lax.rsqrt(key_mean + EPS)
    query_hat = query_raw * inv_query
    key_hat = key_raw * inv_key
    positions = jnp.arange(span, dtype=jnp.int32)
    cosine, sine = angles(positions)
    queries = rotate(heads_of(query_hat * query_gain), cosine, sine, 1.0).astype(BF16)
    keys = rotate(heads_of(key_hat * key_gain), cosine, sine, 1.0).astype(BF16)
    offset = positions[:, None] - positions[None, :]
    allowed = (offset >= 0) & (offset < WINDOW) & (documents[:, None] == documents[None, :])
    scale = HD ** (-0.5)
    scores = jnp.where(allowed[None], ein("hqd,hkd->hqk", queries, keys) * scale, NEG)
    top_score = jnp.max(scores, axis=-1, keepdims=True)
    expo = jnp.exp(scores - top_score)
    total = jnp.sum(expo, axis=-1, keepdims=True)
    probs = expo / total
    probs_low = probs.astype(BF16)
    attended = flat_of(ein("hqk,hkd->hqd", probs_low, values).astype(BF16))

    def to_tokens(block):
        block = exchange(block.reshape(n_c, length, slab), CTX)
        return block.transpose(1, 0, 2).reshape(length, D)

    def to_heads(block):
        block = block.reshape(length, n_c, slab).transpose(1, 0, 2)
        return exchange(block, CTX).reshape(span, slab)

    attended = to_tokens(attended)
    inputs = tokens[0].astype(F32)
    resid = inputs + dot(attended, out_weight)
    inv_second = inv_root(resid)
    normed_second = resid * inv_second
    hidden_second = (normed_second * ffn_gain).astype(BF16)
    logits = ein("td,ed->te", hidden_second, router_weight)
    router_probs = jax.nn.softmax(logits, axis=-1)
    combine = (router_probs * kept).astype(BF16)

    hidden_all = lax.all_gather(
        jnp.concatenate([to_group_order(hidden_second), combine, lanes], axis=1), GROUP
    )
    slot_mine = pick(grads_all[..., D : D + EXPERTS], expert, 2)
    combine_mine = pick(hidden_all[..., D : D + EXPERTS], expert, 2).astype(F32)
    slot_iota = lax.broadcasted_iota(jnp.int32, (1, CAP, 1), 1).astype(BF16)
    placing = (slot_mine[:, None, :] == slot_iota).astype(BF16)
    weighting = placing * combine_mine[:, None, :].astype(BF16)
    row_combine = jnp.sum(weighting.astype(F32), axis=2)
    received = ein("grt,gtd->grd", placing, hidden_all[..., :D]).astype(BF16)
    received = received.reshape(group * CAP, D)
    slot_grads = ein("grt,gtd->grd", placing, grads_all[..., :D])
    grad_received = (row_combine[..., None] * slot_grads).astype(BF16).reshape(group * CAP, D)
    width = D // n_b

    def pieces(block):
        return [block[:, i * width : (i + 1) * width] for i in range(n_b)]

    def into(block, parts):
        return sum(
            dot(left, part.reshape(width, -1)) for left, part in zip(pieces(block), parts)
        )

    def back(block, parts):
        return jnp.concatenate(
            [ein("rf,df->rd", block, part.reshape(width, -1)) for part in parts], axis=1
        )

    gate = into(received, gate_parts)
    upper = into(received, up_parts)
    sigmoid_gate = jax.nn.sigmoid(gate)
    silu_gate = gate * sigmoid_gate
    activated = (silu_gate * upper).astype(BF16)
    expert_out = jnp.concatenate(
        [ein("rf,afd->rad", activated, part).reshape(-1, width) for part in down_parts], axis=1
    ).astype(BF16)
    expert_out = expert_out.reshape(group, CAP, D)
    mixed = ein("grt,grd->gtd", weighting, expert_out).astype(BF16)
    mixed = lax.psum_scatter(mixed, GROUP, scatter_dimension=0, tiled=True)[0]
    slot_dots = jnp.sum(expert_out.astype(F32) * slot_grads, axis=-1)
    grad_combine = jnp.sum(placing.astype(F32) * slot_dots[:, :, None], axis=1)
    grad_combine = exchange(grad_combine, GROUP).reshape(n_a, n_e, length)
    grad_combine = grad_combine.transpose(2, 1, 0).reshape(length, EXPERTS)
    grad_act = sum(
        ein("rad,afd->rf", left.reshape(-1, n_a, slab), part)
        for left, part in zip(pieces(grad_received), down_parts)
    )
    grad_gate = (grad_act * upper * sigmoid_gate * (1.0 + gate * (1.0 - sigmoid_gate))).astype(
        BF16
    )
    grad_upper = (grad_act * silu_gate).astype(BF16)
    grad_rows = (back(grad_gate, gate_parts) + back(grad_upper, up_parts)).astype(BF16)
    grad_rows = ein("grt,grd->gtd", placing, grad_rows.reshape(group, CAP, D)).astype(BF16)
    grad_rows = lax.psum_scatter(grad_rows, GROUP, scatter_dimension=0, tiled=True)[0]
    output = (resid + from_group_order(mixed).astype(F32)).astype(BF16)

    def owners(parts):
        total = parts[0]
        for i in range(1, n_b):
            moved = lax.ppermute(
                parts[i].astype(BF16), "b", [(j, (j + i) % n_b) for j in range(n_b)]
            )
            total = total + moved.astype(F32)
        return exchange(total.astype(BF16), "a").astype(F32)

    grad_gate_sum = owners(
        [ein("rd,rf->df", left, grad_gate).reshape(n_a, slab, -1) for left in pieces(received)]
    )
    grad_up_sum = owners(
        [ein("rd,rf->df", left, grad_upper).reshape(n_a, slab, -1) for left in pieces(received)]
    )
    grad_down_sum = owners(
        [
            ein("rf,rad->afd", activated, left.reshape(-1, n_a, slab))
            for left in pieces(grad_received)
        ]
    )

    grad_router_probs = grad_combine * kept
    grad_logits = (
        router_probs
        * (grad_router_probs - jnp.sum(router_probs * grad_router_probs, axis=-1, keepdims=True))
    ).astype(BF16)
    grad_router_full = ein("td,te->de", hidden_second, grad_logits)
    grad_hidden_second = dot(grad_logits, router_weight) + from_group_order(grad_rows).astype(F32)
    grad_ffn_gain = jnp.sum(grad_hidden_second * normed_second, axis=0)
    grad_resid = grad_output + norm_back(grad_hidden_second, normed_second, inv_second, ffn_gain)
    grad_attn_out = grad_resid.astype(BF16)
    grad_attended = ein("te,de->td", grad_attn_out, out_weight).astype(BF16)
    grad_attended = heads_of(to_heads(grad_attended))
    grad_out_full = ein("td,te->de", attended, grad_attn_out).astype(BF16)
    grad_out = lax.psum_scatter(grad_out_full, ALL, scatter_dimension=0, tiled=True).astype(F32)

    grad_probs = ein("hqd,hkd->hqk", grad_attended, values)
    inner = jnp.sum(probs * grad_probs, axis=-1, keepdims=True)
    grad_scores = (probs * (grad_probs - inner)).astype(BF16)
    grad_queries = ein("hqk,hkd->hqd", grad_scores, keys) * scale
    grad_keys = ein("hqk,hqd->hkd", grad_scores, queries) * scale
    grad_values = flat_of(ein("hqk,hqd->hkd", probs_low, grad_attended).astype(BF16))
    grad_query_norm = flat_of(rotate(grad_queries, cosine, sine, -1.0))
    grad_key_norm = flat_of(rotate(grad_keys, cosine, sine, -1.0))
    grad_query_gain = jnp.sum(grad_query_norm * query_hat, axis=0)
    grad_key_gain = jnp.sum(grad_key_norm * key_hat, axis=0)
    weighted_query = grad_query_norm * query_gain
    weighted_key = grad_key_norm * key_gain
    query_mean, key_mean = over_heads(
        jnp.sum(weighted_query * query_hat, axis=-1), jnp.sum(weighted_key * key_hat, axis=-1)
    )
    grad_query_raw = (inv_query * (weighted_query - query_hat * query_mean)).astype(BF16)
    grad_key_raw = (inv_key * (weighted_key - key_hat * key_mean)).astype(BF16)
    grad_raw = jnp.concatenate([grad_query_raw, grad_key_raw, grad_values], axis=1)
    grad_hidden_first = ein("tf,df->td", grad_raw, head_weight).astype(BF16)
    grad_hidden_first = lax.psum_scatter(
        grad_hidden_first, CTX, scatter_dimension=0, tiled=True
    ).astype(F32)
    grad_heads = ein("td,tf->df", hidden_first, grad_raw).astype(BF16)
    grad_heads = lax.psum_scatter(
        grad_heads.reshape(n_c, n_e * rows, 3 * slab), "exp", scatter_dimension=1, tiled=True
    )
    grad_heads = exchange(grad_heads, CTX).reshape(n_c, rows, 3, slab)
    grad_heads = grad_heads.transpose(2, 1, 0, 3).reshape(3, rows, D).astype(F32)

    inv_first = inv_root(inputs)
    normed_first = inputs * inv_first
    grad_attn_gain = jnp.sum(grad_hidden_first * normed_first, axis=0)
    grad_inputs = grad_resid + norm_back(grad_hidden_first, normed_first, inv_first, attn_gain)

    head_gains = jnp.stack([grad_query_gain, grad_key_gain]).reshape(2, 1, n_e, rows)
    here = jnp.arange(n_c).reshape(1, n_c, 1, 1) == at_c
    head_gains = jnp.where(here, head_gains, 0.0).reshape(2, n_all, rows)
    sums = jnp.concatenate(
        [
            grad_router_full.T.reshape(EXPERTS, n_all, rows),
            grad_attn_gain.reshape(1, n_all, rows),
            head_gains,
            grad_ffn_gain.reshape(1, n_all, rows),
        ]
    )
    sums = exchange(sums.transpose(1, 0, 2).reshape(n_all, -1), ALL)
    sums = jnp.sum(sums, axis=0).reshape(EXPERTS + 4, rows)
    return (
        output[None],
        grad_inputs[None],
        grad_heads[0],
        grad_heads[1],
        grad_heads[2],
        grad_out,
        sums[:EXPERTS].T,
        sums[EXPERTS],
        sums[EXPERTS + 1],
        sums[EXPERTS + 2],
        sums[EXPERTS + 3],
        grad_gate_sum,
        grad_up_sum,
        grad_down_sum,
    )


def solution(mesh):
    n_c, n_e = mesh.shape["ctx"], mesh.shape["exp"]
    n_a = EXPERTS // n_e
    fine = Mesh(mesh.devices.reshape(n_a, n_c // n_a, n_e), ALL)
    rows, blocks = P(ALL, None), P("exp", CTX, None)
    return jax.shard_map(
        shards,
        mesh=fine,
        in_specs=(blocks, P("exp", CTX), blocks, blocks)
        + (rows,) * 5
        + (P(ALL),) * 4
        + (blocks, blocks, P("exp", None, CTX), blocks),
        out_specs=(blocks, blocks)
        + (rows,) * 5
        + (P(ALL),) * 4
        + (blocks, blocks, P("exp", None, CTX)),
        check_vma=False,
    )
```

```python
import functools

import jax
import jax.numpy as jnp
from jax import lax
from jax.experimental import pallas as pl
from jax.experimental.pallas import tpu as pltpu
from jax.sharding import Mesh, PartitionSpec as P

D = 2048
H = 16
HD = 128
EXPERTS = 16
WINDOW = 1024
CAP = 64

EPS = 1e-05
NEG = -1000000000.0
HIGH = lax.Precision.HIGHEST
F32 = jnp.float32
BF16 = jnp.bfloat16

VMEM_LIMIT = 60 * 1024 * 1024

CTX = ("a", "b")
GROUP = ("a", "exp")
ALL = ("a", "b", "exp")


def dot(left, right):
    return jnp.dot(left, right, preferred_element_type=F32)


def ein(spec, left, right):
    return jnp.einsum(spec, left, right, preferred_element_type=F32)


def exchange(block, axes):
    return lax.all_to_all(block, axes, split_axis=0, concat_axis=0, tiled=True)


def inv_root(values):
    return lax.rsqrt(jnp.mean(values * values, axis=-1, keepdims=True) + EPS)


def norm_back(grad_normed, normed, inverse, gain):
    weighted = grad_normed * gain
    return inverse * (weighted - normed * jnp.mean(weighted * normed, axis=-1, keepdims=True))


def angles(span):
    half = HD // 2
    freqs = 10000.0 ** (-2.0 * jnp.arange(half, dtype=F32) / HD)
    angle = jnp.arange(span, dtype=jnp.int32).astype(F32)[:, None] * freqs[None, :]
    cosine, sine = jnp.cos(angle), jnp.sin(angle)
    return jnp.concatenate([cosine, cosine], axis=1), jnp.concatenate([-sine, sine], axis=1)


def pick(values, index, axis):
    spots = lax.broadcasted_iota(jnp.int32, values.shape, axis)
    return jnp.sum(jnp.where(spots == index, values, jnp.zeros_like(values)), axis=axis)


def contract(left, right, dims):
    return lax.dot_general(left, right, ((dims[:1], dims[1:]), ((), ())), preferred_element_type=F32)

def expert_body(n_blocks, n_parts, where_ref, *refs):
    blocks, refs = refs[:n_blocks], refs[n_blocks:]
    parts, refs = refs[:n_parts], refs[n_parts:]
    saved_hbm, back_ref, refs = refs[:5], refs[5], refs[6:]
    saved, refs = refs[:5], refs[5:]
    rows_ref, grad_out_ref, act_ref, grad_gate_ref, grad_up_ref = saved
    hidden, weights, slot_grads, place, weigh, dots, sems = refs
    slab = parts[0].shape[1]
    fetched = [pltpu.make_async_copy(b, hidden.at[k], sems.at[0, k]) for k, b in enumerate(blocks)]
    for copy in fetched:
        copy.start()
    copies = []
    for i, part in enumerate(parts):
        spot = pl.multiple_of(where_ref[1 + i] * slab, slab)
        target = weights.at[:, pl.ds(spot, slab), :]
        copies.append(pltpu.make_async_copy(part, target, sems.at[2, i]))
        copies[-1].start()
    expert = where_ref[0]
    length = hidden.shape[1]
    pair = 2 * length
    lane = lax.broadcasted_iota(jnp.int32, (pair, HD), 1)
    slot = lax.broadcasted_iota(jnp.int32, (pair, 2 * CAP), 1)
    slot -= CAP * (lax.broadcasted_iota(jnp.int32, slot.shape, 0) // length)
    slot = jnp.where((slot >= 0) & (slot < CAP), slot, CAP).astype(F32)
    for k in range(n_blocks // 2):
        fetched[2 * k].wait()
        fetched[2 * k + 1].wait()
        rows = pl.ds(2 * k * CAP, 2 * CAP)
        two = slice(2 * k, 2 * k + 2)
        tags = hidden[two, :, D : D + HD].reshape(pair, HD).astype(F32)
        share = jnp.sum(jnp.where(lane == expert, tags, 0.0), axis=1, keepdims=True)
        codes = jnp.where(lane == expert + EXPERTS, tags, 0.0)
        codes = jnp.sum(codes, axis=1, keepdims=True)
        chosen = (codes == slot).astype(F32)
        placing = chosen.astype(BF16)
        place[k] = placing
        weigh[k] = (chosen * share).astype(BF16)
        picked = contract(placing, hidden[two, :, :D].reshape(pair, D), (0, 0))
        rows_ref[rows, :] = picked.astype(BF16)
        picked = contract(placing, hidden[two, :, D + HD :].reshape(pair, D), (0, 0))
        slot_grads[rows, :] = picked.astype(BF16)
        row_share = contract(weigh[k], jnp.ones((pair, HD), BF16), (0, 0))[:, :1]
        grad_out_ref[rows, :] = (row_share * picked).astype(BF16)
    for copy in copies:
        copy.wait()
    chunk = 512
    width = weights.shape[2]

    @pl.loop(0, width // chunk)
    def _(i):
        cols = pl.ds(pl.multiple_of(i * chunk, chunk), chunk)
        gate = jnp.dot(rows_ref[...], weights[0, :, cols], preferred_element_type=F32)
        upper = jnp.dot(rows_ref[...], weights[1, :, cols], preferred_element_type=F32)
        grad_act = jnp.dot(grad_out_ref[...], weights[2, :, cols], preferred_element_type=F32)
        sigmoid = jax.nn.sigmoid(gate)
        silu = gate * sigmoid
        act_ref[:, cols] = (silu * upper).astype(BF16)
        grad_gate_ref[:, cols] = (
            grad_act * upper * sigmoid * (1.0 + gate * (1.0 - sigmoid))
        ).astype(BF16)
        grad_up_ref[:, cols] = (grad_act * silu).astype(BF16)

    keep = [
        pltpu.make_async_copy(ours, theirs, sems.at[3, i])
        for i, (ours, theirs) in enumerate(zip(saved, saved_hbm))
    ]
    for copy in keep:
        copy.start()
    dots[...] = jnp.zeros_like(dots)

    @pl.loop(0, D // chunk)
    def _(i):
        cols = pl.ds(pl.multiple_of(i * chunk, chunk), chunk)
        out = contract(act_ref[...], weights[2, cols, :], (1, 1)).astype(BF16)
        product = out.astype(F32) * slot_grads[:, cols].astype(F32)
        for j in range(chunk // HD):
            dots[...] += product[:, j * HD : (j + 1) * HD]
        back = contract(grad_gate_ref[...], weights[0, cols, :], (1, 1))
        back += contract(grad_up_ref[...], weights[1, cols, :], (1, 1))
        back = back.astype(BF16)
        for k in range(n_blocks // 2):
            rows = slice(2 * k * CAP, 2 * (k + 1) * CAP)
            two = slice(2 * k, 2 * k + 2)
            mixed = jnp.dot(weigh[k], out[rows], preferred_element_type=F32).astype(BF16)
            back_ref[two, :, cols] = mixed.reshape(2, length, chunk)
            moved = jnp.dot(place[k], back[rows], preferred_element_type=F32).astype(BF16)
            later = pl.ds(pl.multiple_of(D + i * chunk, chunk), chunk)
            back_ref[two, :, later] = moved.reshape(2, length, chunk)

    total = jnp.sum(dots[...], axis=1, keepdims=True)
    for k in range(n_blocks // 2):
        mine = total[2 * k * CAP : 2 * (k + 1) * CAP]
        mine = jnp.broadcast_to(mine, (2 * CAP, HD)).astype(BF16)
        found = jnp.dot(place[k], mine, preferred_element_type=F32)
        found = jnp.where(lane == expert, found, 0.0).astype(BF16)
        back_ref[2 * k : 2 * k + 2, :, 2 * D :] = found.reshape(2, length, HD)
    for copy in keep:
        copy.wait()


def expert_call(where, blocks, parts):
    n_blocks, (length, wide) = len(blocks), blocks[0].shape
    rows = n_blocks * CAP
    width = parts[0].shape[2]
    saved = [(rows, D), (rows, D), (rows, width), (rows, width), (rows, width)]
    sent = (n_blocks, length, wide)
    anywhere = pl.BlockSpec(memory_space=pl.ANY)
    return pl.pallas_call(
        functools.partial(expert_body, n_blocks, len(parts)),
        out_shape=[jax.ShapeDtypeStruct(s, BF16) for s in saved + [sent]],
        grid_spec=pltpu.PrefetchScalarGridSpec(
            num_scalar_prefetch=1,
            grid=(1,),
            in_specs=[anywhere] * (n_blocks + len(parts)),
            out_specs=[anywhere] * 5
            + [pl.BlockSpec(sent, lambda *_: (0, 0, 0), pipeline_mode=pl.Buffered(1))],
            scratch_shapes=[pltpu.VMEM(s, BF16) for s in saved]
            + [
                pltpu.VMEM((n_blocks, length, wide), BF16),
                pltpu.VMEM((3, D, width), BF16),
                pltpu.VMEM((rows, D), BF16),
                pltpu.VMEM((n_blocks // 2, 2 * length, 2 * CAP), BF16),
                pltpu.VMEM((n_blocks // 2, 2 * length, 2 * CAP), BF16),
                pltpu.VMEM((rows, HD), F32),
                pltpu.SemaphoreType.DMA((4, max(n_blocks, len(parts)))),
            ],
        ),
        compiler_params=pltpu.CompilerParams(vmem_limit_bytes=VMEM_LIMIT),
        name="expert",
    )(where, *blocks, *parts)


def sums_body(n, where_ref, *refs):
    ins, outs = refs[: 5 * n], refs[5 * n :]
    rows, grad_out, act, grad_gate, grad_up = (ins[i * n : (i + 1) * n] for i in range(5))
    for i, out in enumerate(outs):

        @pl.when(pl.program_id(0) == i)
        def _():
            for j, (left, right) in enumerate(((rows, grad_gate), (rows, grad_up), (grad_out, act))):
                total = contract(left[0][...], right[0][...], (0, 0))
                for h in range(1, n):
                    total += contract(left[h][...], right[h][...], (0, 0))
                out[j] = total.astype(BF16)


def sums_call(where, saved, slab):
    n = len(saved)
    count = where.shape[0]
    length, width = saved[0][2].shape
    by_slab = pl.BlockSpec((length, slab), lambda i, ref: (0, ref[i]))
    fixed = pl.BlockSpec((length, width), lambda i, ref: (0, 0), pipeline_mode=pl.Buffered(1))
    args = [saved[h][j] for j in range(5) for h in range(n)]
    return pl.pallas_call(
        functools.partial(sums_body, n),
        out_shape=[jax.ShapeDtypeStruct((3, slab, width), BF16)] * count,
        grid_spec=pltpu.PrefetchScalarGridSpec(
            num_scalar_prefetch=1,
            grid=(count,),
            in_specs=[by_slab] * (2 * n) + [fixed] * (3 * n),
            out_specs=[
                pl.BlockSpec((3, slab, width), lambda i, ref: (0, 0, 0), pipeline_mode=pl.Buffered(1))
            ]
            * count,
        ),
        compiler_params=pltpu.CompilerParams(vmem_limit_bytes=VMEM_LIMIT),
        name="expert_sums",
    )(where, *args)


def pack_body(where_ref, gate_ref, up_ref, down_ref, *outs):
    for i, out in enumerate(outs):

        @pl.when(pl.program_id(0) == i)
        def _():
            out[0] = gate_ref[0]
            out[1] = up_ref[0]
            out[2] = down_ref[0].T


def pack_call(where, gate, up, down):
    count, slab, width = gate.shape
    upright = pl.BlockSpec((1, slab, width), lambda i, ref: (ref[i], 0, 0))
    return pl.pallas_call(
        pack_body,
        out_shape=[jax.ShapeDtypeStruct((3, slab, width), BF16)] * count,
        grid_spec=pltpu.PrefetchScalarGridSpec(
            num_scalar_prefetch=1,
            grid=(count,),
            in_specs=[upright, upright, pl.BlockSpec((1, width, slab), lambda i, ref: (ref[i], 0, 0))],
            out_specs=[pl.BlockSpec((3, slab, width), lambda i, ref: (0, 0, 0))] * count,
        ),
        compiler_params=pltpu.CompilerParams(vmem_limit_bytes=VMEM_LIMIT),
        name="pack",
    )(where, gate, up, down)


def unpack_body(where_ref, *refs):
    parts, (gate_ref, up_ref, down_ref) = refs[:-3], refs[-3:]
    for i, part in enumerate(parts):

        @pl.when(pl.program_id(0) == i)
        def _():
            gate_ref[0] = part[0].astype(F32)
            up_ref[0] = part[1].astype(F32)
            down_ref[0] = part[2].astype(F32).T


def unpack_call(where, parts):
    count = len(parts)
    _, slab, width = parts[0].shape
    upright = pl.BlockSpec((1, slab, width), lambda i, ref: (ref[i], 0, 0))
    return pl.pallas_call(
        unpack_body,
        out_shape=[jax.ShapeDtypeStruct((count, slab, width), F32)] * 2
        + [jax.ShapeDtypeStruct((count, width, slab), F32)],
        grid_spec=pltpu.PrefetchScalarGridSpec(
            num_scalar_prefetch=1,
            grid=(count,),
            in_specs=[
                pl.BlockSpec((3, slab, width), lambda i, ref: (0, 0, 0), pipeline_mode=pl.Buffered(1))
            ]
            * count,
            out_specs=[upright, upright, pl.BlockSpec((1, width, slab), lambda i, ref: (ref[i], 0, 0))],
        ),
        compiler_params=pltpu.CompilerParams(vmem_limit_bytes=VMEM_LIMIT),
        name="unpack",
    )(where, *parts)


def heads_body(n_blocks, where_ref, *refs):
    blocks, (gain_ref, weight_ref, hidden_ref, raw_ref, sums_ref, tokens, sems) = (
        refs[:n_blocks],
        refs[n_blocks:],
    )
    step = pl.program_id(0)
    copies = [pltpu.make_async_copy(b, tokens.at[k], sems.at[k]) for k, b in enumerate(blocks)]

    @pl.when(step == 0)
    def _():
        for copy in copies:
            copy.start()
        for copy in copies:
            copy.wait()

    values = tokens[step].astype(F32)
    hidden = (values * inv_root(values) * gain_ref[...]).astype(BF16)
    hidden_ref[...] = hidden
    raw = jnp.dot(hidden, weight_ref[...], preferred_element_type=F32)
    raw_ref[...] = raw
    slab = raw.shape[1] // 3
    query, key = raw[:, :slab], raw[:, slab : 2 * slab]
    sums_ref[...] = by_token(
        jnp.sum(query * query, axis=1, keepdims=True), jnp.sum(key * key, axis=1, keepdims=True)
    )


def by_token(first, second):
    lane = lax.broadcasted_iota(jnp.int32, (first.shape[0], HD), 1)
    both = jnp.where(lane == 0, first, jnp.where(lane == 1, second, 0.0))
    return both.T[:8]


def heads_call(where, blocks, gain, weight):
    count, (length, _), wide = len(blocks), blocks[0].shape, weight.shape[1]
    span = count * length
    return pl.pallas_call(
        functools.partial(heads_body, count),
        grid_spec=pltpu.PrefetchScalarGridSpec(
            num_scalar_prefetch=1,
            grid=(count,),
            in_specs=[pl.BlockSpec(memory_space=pl.ANY)] * count
            + [
                pl.BlockSpec((1, D), lambda i, ref: (0, 0)),
                pl.BlockSpec((D, wide), lambda i, ref: (0, 0), pipeline_mode=pl.Buffered(1)),
            ],
            out_specs=[
                pl.BlockSpec((length, D), lambda i, ref: (ref[i], 0)),
                pl.BlockSpec((length, wide), lambda i, ref: (ref[i], 0)),
                pl.BlockSpec((8, length), lambda i, ref: (0, ref[i])),
            ],
            scratch_shapes=[
                pltpu.VMEM((count, length, D), BF16),
                pltpu.SemaphoreType.DMA((count,)),
            ],
        ),
        out_shape=[
            jax.ShapeDtypeStruct((span, D), BF16),
            jax.ShapeDtypeStruct((span, wide), F32),
            jax.ShapeDtypeStruct((8, span), F32),
        ],
        compiler_params=pltpu.CompilerParams(vmem_limit_bytes=VMEM_LIMIT),
        name="heads",
    )(where, *blocks, gain, weight)


def project_body(order_ref, attended_ref, weight_ref, out_ref):
    out_ref[0] = jnp.dot(
        attended_ref[...], weight_ref[...], preferred_element_type=F32
    ).astype(BF16)


def project_call(order, attended, weight):
    span, slab = attended.shape
    count = order.shape[0]
    length = span // count
    return pl.pallas_call(
        project_body,
        out_shape=jax.ShapeDtypeStruct((count, length, D), BF16),
        grid_spec=pltpu.PrefetchScalarGridSpec(
            num_scalar_prefetch=1,
            grid=(count,),
            in_specs=[
                pl.BlockSpec((length, slab), lambda i, ref: (ref[i], 0)),
                pl.BlockSpec((slab, D), lambda i, ref: (0, 0), pipeline_mode=pl.Buffered(1)),
            ],
            out_specs=pl.BlockSpec((1, length, D), lambda i, ref: (i, 0, 0)),
        ),
        compiler_params=pltpu.CompilerParams(vmem_limit_bytes=VMEM_LIMIT),
        name="project",
    )(order, attended, weight)


def project_back_body(n_blocks, where_ref, *refs):
    blocks, (attended_ref, weight_ref, grad_ref, sum_ref, grads, total, sems) = (
        refs[:n_blocks],
        refs[n_blocks:],
    )
    step = pl.program_id(0)
    copies = [pltpu.make_async_copy(b, grads.at[k], sems.at[k]) for k, b in enumerate(blocks)]

    @pl.when(step == 0)
    def _():
        for copy in copies:
            copy.start()
        total[...] = jnp.zeros_like(total)
        for copy in copies:
            copy.wait()

    mine = grads[step]
    grad_ref[...] = contract(mine, weight_ref[...], (1, 1)).astype(BF16)
    total[...] += contract(attended_ref[...], mine, (0, 0))

    @pl.when(step == n_blocks - 1)
    def _():
        sum_ref[...] = total[...].astype(BF16)


def project_back_call(where, blocks, attended, weight):
    span, slab = attended.shape
    count, (length, _) = len(blocks), blocks[0].shape
    return pl.pallas_call(
        functools.partial(project_back_body, count),
        out_shape=[jax.ShapeDtypeStruct((span, slab), BF16), jax.ShapeDtypeStruct((slab, D), BF16)],
        grid_spec=pltpu.PrefetchScalarGridSpec(
            num_scalar_prefetch=1,
            grid=(count,),
            in_specs=[pl.BlockSpec(memory_space=pl.ANY)] * count
            + [
                pl.BlockSpec((length, slab), lambda i, ref: (ref[i], 0)),
                pl.BlockSpec((slab, D), lambda i, ref: (0, 0), pipeline_mode=pl.Buffered(1)),
            ],
            out_specs=[
                pl.BlockSpec((length, slab), lambda i, ref: (ref[i], 0)),
                pl.BlockSpec((slab, D), lambda i, ref: (0, 0)),
            ],
            scratch_shapes=[
                pltpu.VMEM((count, length, D), BF16),
                pltpu.VMEM((slab, D), F32),
                pltpu.SemaphoreType.DMA((count,)),
            ],
        ),
        compiler_params=pltpu.CompilerParams(vmem_limit_bytes=VMEM_LIMIT),
        name="project_back",
    )(where, *blocks, attended, weight)


def turn(values, cosine, sine, sign):
    return values * cosine + sign * pltpu.roll(values, HD // 2, 1) * sine


def ready(head, raw_ref, stats, gains_ref, cosine, sine):
    slab = raw_ref.shape[1] // 3
    cols = slice(head * HD, (head + 1) * HD)
    found = []
    for j in range(2):
        inverse = lax.rsqrt(stats[:, j : j + 1] / D + EPS)
        hat = raw_ref[:, j * slab + head * HD : j * slab + (head + 1) * HD] * inverse
        gain = gains_ref[j : j + 1, cols]
        found.append((turn(hat * gain, cosine, sine, 1.0).astype(BF16), hat, gain))
    value = raw_ref[:, 2 * slab + head * HD : 2 * slab + (head + 1) * HD].astype(BF16)
    return found[0], found[1], value


def soften(first, last, query, key_ref, stats, docs, low):
    scores = contract(query, key_ref[low:last, :], (1, 1)) * HD ** (-0.5)
    row = first + lax.broadcasted_iota(jnp.int32, scores.shape, 0)
    col = low + lax.broadcasted_iota(jnp.int32, scores.shape, 1)
    offset = row - col
    allowed = (offset >= 0) & (offset < WINDOW) & (stats[first:last, 2:3] == docs[:, low:last])
    scores = jnp.where(allowed, scores, NEG)
    expo = jnp.exp(scores - jnp.max(scores, axis=1, keepdims=True))
    return expo * (1.0 / jnp.sum(expo, axis=1, keepdims=True))


def ranges(span):
    rows, reach = 256, min(WINDOW, span // 2)
    return [(i, i + rows, max(0, (i - reach) // rows * rows)) for i in range(0, span, rows)]


def attend_body(raw_ref, rows_ref, gains_ref, cosine_ref, sine_ref, out_ref, key_ref):
    span = raw_ref.shape[0]
    stats = rows_ref[...].T
    docs = rows_ref[2:3, :]
    for head in range(out_ref.shape[1] // HD):
        (query, _, _), (key, _, _), value = ready(
            head, raw_ref, stats, gains_ref, cosine_ref[...], sine_ref[...]
        )
        key_ref[...] = key
        for first, last, low in ranges(span):
            probs = soften(first, last, query[first:last], key_ref, stats, docs, low)
            out_ref[first:last, head * HD : (head + 1) * HD] = jnp.dot(
                probs.astype(BF16), value[low:last], preferred_element_type=F32
            ).astype(BF16)


def attend_call(raw, rows, gains, cosine, sine):
    span, wide = raw.shape
    return pl.pallas_call(
        attend_body,
        out_shape=jax.ShapeDtypeStruct((span, wide // 3), BF16),
        scratch_shapes=[pltpu.VMEM((span, HD), BF16)],
        compiler_params=pltpu.CompilerParams(vmem_limit_bytes=VMEM_LIMIT),
        name="attend",
    )(raw, rows, gains, cosine, sine)


def attend_back_body(
    raw_ref,
    rows_ref,
    gains_ref,
    cosine_ref,
    sine_ref,
    grad_ref,
    weighted_ref,
    grad_values_ref,
    grad_gains_ref,
    sums_ref,
    key_ref,
    grad_query,
    grad_key,
    grad_value,
):
    span = raw_ref.shape[0]
    slab = grad_ref.shape[1]
    stats = rows_ref[...].T
    docs = rows_ref[2:3, :]
    cosine, sine = cosine_ref[...], sine_ref[...]
    grad_gains_ref[...] = jnp.zeros_like(grad_gains_ref)
    totals = [jnp.zeros((span, 1), F32), jnp.zeros((span, 1), F32)]
    for head in range(slab // HD):
        cols = slice(head * HD, (head + 1) * HD)
        (query, query_hat, query_gain), (key, key_hat, key_gain), value = ready(
            head, raw_ref, stats, gains_ref, cosine, sine
        )
        key_ref[...] = key
        grad_key[...] = jnp.zeros_like(grad_key)
        grad_value[...] = jnp.zeros_like(grad_value)
        for first, last, low in ranges(span):
            probs = soften(first, last, query[first:last], key_ref, stats, docs, low)
            grad_out = grad_ref[first:last, cols]
            grad_probs = contract(grad_out, value[low:last], (1, 1))
            inner = jnp.sum(probs * grad_probs, axis=1, keepdims=True)
            grad_scores = (probs * (grad_probs - inner)).astype(BF16)
            grad_query[first:last, :] = jnp.dot(
                grad_scores, key_ref[low:last, :], preferred_element_type=F32
            )
            grad_key[low:last, :] += contract(grad_scores, query[first:last], (0, 0))
            grad_value[low:last, :] += contract(probs.astype(BF16), grad_out, (0, 0))
        grad_values_ref[:, cols] = grad_value[...].astype(BF16)
        for j, (grad, hat, gain) in enumerate(
            ((grad_query, query_hat, query_gain), (grad_key, key_hat, key_gain))
        ):
            grad_norm = turn(grad[...] * HD ** (-0.5), cosine, sine, -1.0)
            grad_gains_ref[j : j + 1, cols] = jnp.sum(grad_norm * hat, axis=0, keepdims=True)
            weighted = grad_norm * gain
            weighted_ref[:, j * slab + head * HD : j * slab + (head + 1) * HD] = weighted
            totals[j] += jnp.sum(weighted * hat, axis=1, keepdims=True)
    sums_ref[...] = by_token(*totals)


def attend_back_call(raw, rows, gains, cosine, sine, grad):
    span, slab = grad.shape
    return pl.pallas_call(
        attend_back_body,
        out_shape=[
            jax.ShapeDtypeStruct((span, 2 * slab), F32),
            jax.ShapeDtypeStruct((span, slab), BF16),
            jax.ShapeDtypeStruct((8, slab), F32),
            jax.ShapeDtypeStruct((8, span), F32),
        ],
        scratch_shapes=[pltpu.VMEM((span, HD), BF16)] + [pltpu.VMEM((span, HD), F32)] * 3,
        compiler_params=pltpu.CompilerParams(vmem_limit_bytes=VMEM_LIMIT),
        name="attend_back",
    )(raw, rows, gains, cosine, sine, grad)


def grad_heads_body(order_ref, weighted_ref, raw_ref, rows_ref, grad_values_ref, weight_ref, raw_out_ref, hidden_out_ref):
    slab = grad_values_ref.shape[1]
    stats = rows_ref[...].T
    for j in range(2):
        cols = slice(j * slab, (j + 1) * slab)
        inverse = lax.rsqrt(stats[:, j : j + 1] / D + EPS)
        hat = raw_ref[:, cols] * inverse
        mean = stats[:, 3 + j : 4 + j] / D
        raw_out_ref[:, cols] = (inverse * (weighted_ref[:, cols] - hat * mean)).astype(BF16)
    raw_out_ref[:, 2 * slab :] = grad_values_ref[...]
    hidden_out_ref[0] = contract(raw_out_ref[...], weight_ref[...], (1, 1)).astype(BF16)


def grad_heads_call(order, weighted, raw, rows, grad_values, weight):
    span, slab = grad_values.shape
    count = order.shape[0]
    length = span // count

    def spec(width):
        return pl.BlockSpec((length, width), lambda i, ref: (ref[i], 0))

    return pl.pallas_call(
        grad_heads_body,
        out_shape=[
            jax.ShapeDtypeStruct((span, 3 * slab), BF16),
            jax.ShapeDtypeStruct((count, length, D), BF16),
        ],
        grid_spec=pltpu.PrefetchScalarGridSpec(
            num_scalar_prefetch=1,
            grid=(count,),
            in_specs=[
                spec(2 * slab),
                spec(3 * slab),
                pl.BlockSpec((8, length), lambda i, ref: (0, ref[i])),
                spec(slab),
                pl.BlockSpec((D, 3 * slab), lambda i, ref: (0, 0), pipeline_mode=pl.Buffered(1)),
            ],
            out_specs=[spec(3 * slab), pl.BlockSpec((1, length, D), lambda i, ref: (i, 0, 0))],
        ),
        compiler_params=pltpu.CompilerParams(vmem_limit_bytes=VMEM_LIMIT),
        name="grad_heads",
    )(order, weighted, raw, rows, grad_values, weight)


def tie(value, *others):
    return lax.optimization_barrier((value, others))[0]


def cycle(high, low):
    cells = [(0, j) for j in range(low)]
    for i in range(1, high):
        columns = range(low - 1, 0, -1) if i % 2 else range(1, low)
        cells += [(i, j) for j in columns]
    cells += [(i, 0) for i in range(high - 1, 0, -1)]
    return [i * low + j for i, j in cells]


class Ring:
    def __init__(self, count, groups):
        self.count = count
        self.onward, self.backward = [], []
        self.device = {}
        for members in groups:
            for i, member in enumerate(members):
                after = members[(i + 1) % count]
                self.onward.append((member, after))
                self.backward.append((after, member))
                self.device[member] = i

    def gather(self, block, waits=None, other=None):
        found, passed = {0: block}, {}
        ahead = behind = block
        fresh = [0]
        for step in range(1, self.count // 2 + 1):
            if waits and step in waits:
                behind = tie(behind, *waits[step])
            if other is not None:
                passed.update({k: other(found[k]) for k in fresh})
            held = [passed[k] for k in fresh if k in passed]
            behind = lax.ppermute(behind, ALL, self.onward)
            if step < (self.count + 1) // 2:
                ahead = lax.ppermute(ahead, ALL, self.backward)
            behind, ahead, *held = lax.optimization_barrier((behind, ahead, *held))
            for k, value in zip(fresh, held):
                passed[k] = value
            fresh = [step]
            found[step] = behind
            if step < (self.count + 1) // 2:
                found[self.count - step] = ahead
                fresh.append(self.count - step)
        found = [found[k] for k in range(self.count)]
        if other is None:
            return found
        passed.update({k: other(found[k]) for k in fresh})
        return found, [passed[k] for k in range(self.count)]

    def scatter(self, part, visit=None, waits=()):
        half = self.count // 2
        far = self.count - half - 1
        onward = backward = None
        for k in range(half, -1, -1):
            term = part(k).astype(F32) if onward is None else onward.astype(F32) + part(k).astype(F32)
            if k == 0:
                return term if backward is None else term + backward.astype(F32)
            term = term.astype(BF16)
            if waits:
                term = tie(term, *waits)
            onward = lax.ppermute(term, ALL, self.onward)
            if k <= far:
                term = part(self.count - k).astype(F32)
                if backward is not None:
                    term = term + backward.astype(F32)
                backward = lax.ppermute(term.astype(BF16), ALL, self.backward)
                onward, backward = lax.optimization_barrier((onward, backward))
            waits = visit(half - k + 1, onward) if visit is not None else ()


def shards(
    tokens,
    doc_ids,
    expert_ids,
    drop_order,
    w_query,
    w_key,
    w_value,
    w_out,
    w_router,
    gain_attn,
    gain_query,
    gain_key,
    gain_ffn,
    w_gate,
    w_up,
    w_down,
    cotangent,
):
    n_a, n_b, n_e = (lax.axis_size(name) for name in ALL)
    n_c = n_a * n_b
    n_all = n_c * n_e
    group = n_a * n_e
    length = tokens.shape[1]
    span = n_c * length
    slab = D // n_c
    rows = D // n_all
    at_a, at_b, at_e = (lax.axis_index(name) for name in ALL)
    at_c = at_a * n_b + at_b
    expert = at_e * n_a + at_a
    at_all = at_c * n_e + at_e

    walk = cycle(n_a, n_b) if n_b % 2 == 0 and n_a % 2 == 0 else list(range(n_c))
    ctx_ring = Ring(n_c, [[c * n_e + e for c in walk] for e in range(n_e)])
    n_y = n_e // 2
    n_ring = n_a * n_y
    y_walk = cycle(n_a, n_y)
    group_ring = Ring(
        n_ring,
        [
            [((w // n_y) * n_b + b) * n_e + (w % n_y) * 2 + core for w in y_walk]
            for b in range(n_b)
            for core in range(2)
        ],
    )
    swap_cores = [(i, i + 1 - 2 * (i % 2)) for i in range(n_all)]
    table = []
    for i in range(n_all):
        c, e = divmod(i, n_e)
        a, b = divmod(c, n_b)
        p, q = ctx_ring.device[i], group_ring.device[i]
        line = [walk[(p - k) % n_c] for k in range(n_c)]
        for core in (1 - e % 2, e % 2):
            for k in range(n_ring):
                w = y_walk[(q - k) % n_ring]
                line.append((w // n_y) * n_e + (w % n_y) * 2 + core)
        line += [(a + k) % n_a for k in range(n_a)] + [(a - k) % n_a for k in range(n_a)]
        line += [((a - j) % n_a) * n_b + (b + k) % n_b for k in range(n_b) for j in range(n_a)]
        line += [((a + j) % n_a) * n_b + (b + k) % n_b for k in range(n_b) for j in range(n_a)]
        table.append(line)
    line = lax.dynamic_slice_in_dim(jnp.array(table, jnp.int32), at_all, 1, 0)[0]
    cuts = [n_c, 2 * n_ring, n_a, n_a, n_c, n_c]
    ends = [sum(cuts[: i + 1]) for i in range(len(cuts))]
    ctx_spots, group_spots, onward_experts, behind_experts, weight_slabs, grad_slabs = (
        line[end - cut : end] for cut, end in zip(cuts, ends)
    )

    vectors = jnp.stack([gain_attn, gain_query, gain_key, gain_ffn])
    small = jnp.concatenate([w_router.T, vectors]).reshape(-1)
    small = jnp.concatenate([small, doc_ids[0].astype(BF16)])
    small = exchange(jnp.broadcast_to(small[None], (n_all, small.shape[0])), ALL)
    params = small[:, : (EXPERTS + 4) * rows].reshape(n_all, EXPERTS + 4, rows)
    params = params.transpose(1, 0, 2).reshape(EXPERTS + 4, D)
    router_weight = params[:EXPERTS]
    attn_gain, query_gain, key_gain, ffn_gain = params[EXPERTS:].astype(F32)
    documents = pick(small[:, (EXPERTS + 4) * rows :].reshape(n_c, n_e, length), at_e, 1)
    documents = documents.reshape(1, span)
    head_gains = jnp.stack([query_gain, key_gain])
    head_gains = lax.dynamic_slice_in_dim(head_gains, at_c * slab, slab, 1)
    cosine, sine = angles(span)

    packed = pack_call(onward_experts, w_gate, w_up, w_down)
    mine = jnp.stack([w_query, w_key, w_value]).reshape(3, rows, n_c, slab)
    mine = mine.transpose(2, 1, 0, 3).reshape(n_c, rows, 3 * slab)
    mine = exchange(mine, CTX)
    blocks = ctx_ring.gather(tokens[0], {2: [packed[0]], 3: [mine]})
    head_weight = lax.all_gather(mine, "exp", axis=1, tiled=True).reshape(D, 3 * slab)
    out_weight = lax.all_gather(w_out, "exp", axis=0, tiled=True)
    ring_order = jnp.roll(ctx_spots[::-1], 1)

    def along_a(block, shift):
        return lax.ppermute(block, "a", [(j, (j + shift) % n_a) for j in range(n_a)])

    def along_b(block, shift):
        return lax.ppermute(block, "b", [((j + shift) % n_b, j) for j in range(n_b)])

    near = [packed[0]] + [None] * (n_a - 1)
    middle = n_a // 2
    shifts = [j for j in range(1, n_a) if j != middle] + [middle]

    def fetch(j, *after):
        near[j] = along_a(tie(packed[j], *after), j)

    far = {}

    def share(j, *after):
        for k in range(1, n_b):
            far[k, j] = along_b(tie(near[j], *after), k)

    expert_iota = jnp.arange(EXPERTS, dtype=jnp.int32)
    named = jnp.sum(
        (expert_ids[0][:, :, None] == expert_iota[None, None, :]).astype(F32), axis=1
    )
    order = drop_order[0, 0]
    earlier = (order[None, :] < order[:, None]).astype(F32)
    slots = jnp.dot(earlier, named, precision=HIGH, preferred_element_type=F32)
    kept = named * (slots < CAP).astype(F32)
    slot_code = jnp.where(kept > 0, slots, -1.0).astype(BF16)
    lanes = jnp.zeros((length, HD - 2 * EXPERTS), BF16)
    grad_rows_in = cotangent[0]
    grad_output = grad_rows_in.astype(F32)

    hidden_first, raw, sums = heads_call(ctx_spots, blocks, attn_gain[None], head_weight)

    def over_heads(values):
        values = exchange(jnp.broadcast_to(values[None], (n_c,) + values.shape), CTX)
        return jnp.sum(values, axis=0)

    kinds = lax.broadcasted_iota(jnp.int32, (8, span), 0)
    stats = jnp.where(kinds == 2, documents.astype(F32), over_heads(sums))
    attended = attend_call(raw, stats, head_gains, cosine, sine)
    partial = project_call(ring_order, attended, out_weight)
    chain = list(range(1, n_a))
    fetch(chain[0], stats)
    share(0, attended)

    def during_project(step, found):
        if step == 1:
            for j in chain[1:-1]:
                fetch(j, near[chain[0]])
            share(chain[0], near[chain[0]])
            return [near[chain[0]]]
        return ()

    attended_out = ctx_ring.scatter(lambda k: partial[k], during_project)
    attended_out = tie(
        attended_out, *[near[j] for j in chain[1:-1]], *[far[k, 0] for k in range(1, n_b)]
    )
    if len(chain) > 1:
        fetch(chain[-1], attended_out)
    for j in chain[1:-1]:
        share(j, attended_out)
    inputs = tokens[0].astype(F32)
    resid = inputs + attended_out
    inv_second = inv_root(resid)
    normed_second = resid * inv_second
    hidden_second = (normed_second * ffn_gain).astype(BF16)
    logits = ein("td,ed->te", hidden_second, router_weight)
    router_probs = jax.nn.softmax(logits, axis=-1)
    combine = (router_probs * kept).astype(BF16)

    block = jnp.concatenate([hidden_second, combine, slot_code, lanes, grad_rows_in], axis=1)
    waits = {
        2: [far[k, chain[0]] for k in range(1, n_b)],
        3: [near[chain[-1]]],
        4: [far[k, j] for k in range(1, n_b) for j in chain[1:-1]],
    }
    ours, theirs = group_ring.gather(
        block, waits, lambda found: lax.ppermute(found, ALL, swap_cores)
    )
    if len(chain) > 1:
        share(chain[-1], near[chain[-1]])
    parts = near + [far[k, j] for k in range(1, n_b) for j in range(n_a)]
    where = jnp.concatenate([expert[None], weight_slabs])
    *given, give = expert_call(where, theirs, parts)
    got = lax.ppermute(give, ALL, swap_cores)
    *kept_here, keep = expert_call(where, ours, parts)

    def back_part(k):
        i = (n_ring - k) % n_ring
        return keep[i].astype(F32) + got[i].astype(F32)

    def along_b_back(block, shift):
        return lax.ppermute(block, "b", [(j, (j + shift) % n_b) for j in range(n_b)])

    saved = [given, kept_here]
    far_sums = sums_call(grad_slabs[n_a:], saved, slab)
    near_sums = sums_call(grad_slabs[:n_a], [[tie(given[0], far_sums[0])] + given[1:], kept_here], slab)
    moved = {}
    last = ()
    for j in [middle] + shifts[:-1] + [0]:
        for k in range(1, n_b):
            moved[k, j] = along_b_back(tie(far_sums[(k - 1) * n_a + j], *last), k)
        last = [moved[k, j] for k in range(1, n_b)]

    def owner_sum(j):
        total = near_sums[j].astype(F32)
        for k in range(1, n_b):
            total += moved[k, j].astype(F32)
        return total.astype(BF16)

    owned = {middle: along_a(owner_sum(middle), middle)}

    def during_back(step, found):
        if step == 1:
            return [near_sums[0]]
        if step == 2:
            return [moved[k, middle] for k in range(1, n_b)]
        return ()

    grad_back = group_ring.scatter(back_part, during_back, far_sums)
    mixed = grad_back[:, :D]
    grad_rows = grad_back[:, D : 2 * D]
    grad_combine = grad_back[:, 2 * D : 2 * D + EXPERTS]
    output = (resid + mixed).astype(BF16)

    grad_router_probs = grad_combine * kept
    grad_logits = (
        router_probs
        * (grad_router_probs - jnp.sum(router_probs * grad_router_probs, axis=-1, keepdims=True))
    ).astype(BF16)
    grad_router_full = ein("td,te->de", hidden_second, grad_logits)
    grad_hidden_second = dot(grad_logits, router_weight) + grad_rows
    grad_ffn_gain = jnp.sum(grad_hidden_second * normed_second, axis=0)
    grad_resid = grad_output + norm_back(grad_hidden_second, normed_second, inv_second, ffn_gain)
    grad_attn_out = grad_resid.astype(BF16)
    blocks = ctx_ring.gather(
        grad_attn_out,
        {3: [moved[k, j] for k in range(1, n_b) for j in shifts[:1]]},
    )
    blocks[0] = tie(
        blocks[0], owned[middle], *[moved[k, j] for k in range(1, n_b) for j in shifts[1:-1]]
    )
    grad_attended, grad_out = project_back_call(ctx_spots, blocks, attended, out_weight)
    for j in shifts[:-1]:
        owned[j] = along_a(tie(owner_sum(j), *owned.values()), j)
    owned[0] = owner_sum(0)

    def over_exp(values):
        core, at_y = at_e % 2, at_e // 2
        axis = values.ndim - 4
        keep = lax.dynamic_index_in_dim(values, core, axis + 1, False).astype(F32)
        give = lax.dynamic_index_in_dim(values, 1 - core, axis + 1, False)
        keep = keep + lax.ppermute(give, ALL, swap_cores).astype(F32)
        total = lax.dynamic_index_in_dim(keep, at_y, axis, False)
        for k in range(1, n_y):
            give = lax.dynamic_index_in_dim(keep, (at_y + k) % n_y, axis, False).astype(BF16)
            onward = [(i, i - i % n_e + (i % n_e + 2 * k) % n_e) for i in range(n_all)]
            total = total + lax.ppermute(give, ALL, onward).astype(F32)
        return total

    grad_out = over_exp(grad_out.reshape(n_y, 2, rows, D))

    weighted, grad_values, grad_head_gains, sums = attend_back_call(
        raw, stats, head_gains, cosine, sine, grad_attended
    )
    sums = over_heads(tie(sums, *[owned[j] for j in shifts[:1]]))
    stats = jnp.where(kinds < 3, stats, jnp.roll(sums, 3, axis=0))
    grad_raw, grad_hidden = grad_heads_call(ring_order, weighted, raw, stats, grad_values, head_weight)
    grad_heads = ein("td,tf->df", hidden_first, grad_raw).astype(BF16)
    grad_heads = over_exp(grad_heads.reshape(n_c, n_y, 2, rows, 3 * slab))
    grad_heads = exchange(grad_heads.astype(BF16), CTX).reshape(n_c, rows, 3, slab)
    grad_heads = grad_heads.transpose(2, 1, 0, 3).reshape(3, rows, D).astype(F32)
    def during_first(step, found):
        return [owned[j] for j in shifts[1:-1]] if step == 2 else ()

    grad_hidden_first = ctx_ring.scatter(lambda k: grad_hidden[k], during_first)
    grad_hidden_first = tie(grad_hidden_first, grad_heads)

    grad_gate_sum, grad_up_sum, grad_down_sum = unpack_call(
        behind_experts, [owned[j] for j in range(n_a)]
    )

    inv_first = inv_root(inputs)
    normed_first = inputs * inv_first
    grad_attn_gain = jnp.sum(grad_hidden_first * normed_first, axis=0)
    grad_inputs = grad_resid + norm_back(grad_hidden_first, normed_first, inv_first, attn_gain)

    head_gains = grad_head_gains[:2].reshape(2, 1, n_e, rows)
    here = jnp.arange(n_c).reshape(1, n_c, 1, 1) == at_c
    head_gains = jnp.where(here, head_gains, 0.0).reshape(2, n_all, rows)
    sums = jnp.concatenate(
        [
            grad_router_full.T.reshape(EXPERTS, n_all, rows),
            grad_attn_gain.reshape(1, n_all, rows),
            head_gains,
            grad_ffn_gain.reshape(1, n_all, rows),
        ]
    )
    sums = exchange(sums.transpose(1, 0, 2).reshape(n_all, -1), ALL)
    sums = jnp.sum(sums, axis=0).reshape(EXPERTS + 4, rows)
    return (
        output[None],
        grad_inputs[None],
        grad_heads[0],
        grad_heads[1],
        grad_heads[2],
        grad_out,
        sums[:EXPERTS].T,
        sums[EXPERTS],
        sums[EXPERTS + 1],
        sums[EXPERTS + 2],
        sums[EXPERTS + 3],
        grad_gate_sum,
        grad_up_sum,
        grad_down_sum,
    )


def solution(mesh):
    n_c, n_e = mesh.shape["ctx"], mesh.shape["exp"]
    n_a = EXPERTS // n_e
    fine = Mesh(mesh.devices.reshape(n_a, n_c // n_a, n_e), ALL)
    rows, blocks = P(ALL, None), P("exp", CTX, None)
    return jax.shard_map(
        shards,
        mesh=fine,
        in_specs=(blocks, P("exp", CTX), blocks, blocks)
        + (rows,) * 5
        + (P(ALL),) * 4
        + (blocks, blocks, P("exp", None, CTX), blocks),
        out_specs=(blocks, blocks)
        + (rows,) * 5
        + (P(ALL),) * 4
        + (blocks, blocks, P("exp", None, CTX)),
        check_vma=False,
    )
```

```python
import functools

import jax
import jax.numpy as jnp
from jax import lax
from jax.experimental import pallas as pl
from jax.experimental.pallas import tpu as pltpu
from jax.sharding import Mesh, PartitionSpec as P

D = 2048
H = 16
HD = 128
EXPERTS = 16
WINDOW = 1024
CAP = 64

EPS = 1e-05
NEG = -1000000000.0
HIGH = lax.Precision.HIGHEST
F32 = jnp.float32
BF16 = jnp.bfloat16

VMEM_LIMIT = 60 * 1024 * 1024

CTX = ("a", "b")
GROUP = ("a", "exp")
ALL = ("a", "b", "exp")


def dot(left, right):
    return jnp.dot(left, right, preferred_element_type=F32)


def ein(spec, left, right):
    return jnp.einsum(spec, left, right, preferred_element_type=F32)


def exchange(block, axes):
    return lax.all_to_all(block, axes, split_axis=0, concat_axis=0, tiled=True)


def inv_root(values):
    return lax.rsqrt(jnp.mean(values * values, axis=-1, keepdims=True) + EPS)


def norm_back(grad_normed, normed, inverse, gain):
    weighted = grad_normed * gain
    return inverse * (weighted - normed * jnp.mean(weighted * normed, axis=-1, keepdims=True))


def angles(span):
    half = HD // 2
    freqs = 10000.0 ** (-2.0 * jnp.arange(half, dtype=F32) / HD)
    angle = jnp.arange(span, dtype=jnp.int32).astype(F32)[:, None] * freqs[None, :]
    cosine, sine = jnp.cos(angle), jnp.sin(angle)
    return jnp.concatenate([cosine, cosine], axis=1), jnp.concatenate([-sine, sine], axis=1)


def pick(values, index, axis):
    spots = lax.broadcasted_iota(jnp.int32, values.shape, axis)
    return jnp.sum(jnp.where(spots == index, values, jnp.zeros_like(values)), axis=axis)


def contract(left, right, dims):
    return lax.dot_general(left, right, ((dims[:1], dims[1:]), ((), ())), preferred_element_type=F32)

def expert_body(n_blocks, n_parts, where_ref, *refs):
    blocks, refs = refs[:n_blocks], refs[n_blocks:]
    parts, refs = refs[:n_parts], refs[n_parts:]
    saved_hbm, sent, refs = refs[:5], refs[5:7], refs[7:]
    saved, refs = refs[:5], refs[5:]
    rows_ref, grad_out_ref, act_ref, grad_gate_ref, grad_up_ref = saved
    hidden, weights, slot_grads, place, weigh, dots, sems = refs
    slab = parts[0].shape[1]
    fetched = [pltpu.make_async_copy(b, hidden.at[k], sems.at[0, k]) for k, b in enumerate(blocks)]
    for copy in fetched:
        copy.start()
    copies = []
    for i, part in enumerate(parts):
        spot = pl.multiple_of(where_ref[1 + i] * slab, slab)
        target = weights.at[:, pl.ds(spot, slab), :]
        copies.append(pltpu.make_async_copy(part, target, sems.at[2, i]))
        copies[-1].start()
    expert = where_ref[0]
    length = hidden.shape[1]
    pair = 2 * length
    lane = lax.broadcasted_iota(jnp.int32, (pair, HD), 1)
    slot = lax.broadcasted_iota(jnp.int32, (pair, 2 * CAP), 1)
    slot -= CAP * (lax.broadcasted_iota(jnp.int32, slot.shape, 0) // length)
    slot = jnp.where((slot >= 0) & (slot < CAP), slot, CAP).astype(F32)
    for k in range(n_blocks // 2):
        fetched[2 * k].wait()
        fetched[2 * k + 1].wait()
        rows = pl.ds(2 * k * CAP, 2 * CAP)
        two = slice(2 * k, 2 * k + 2)
        tags = hidden[two, :, D : D + HD].reshape(pair, HD).astype(F32)
        share = jnp.sum(jnp.where(lane == expert, tags, 0.0), axis=1, keepdims=True)
        codes = jnp.where(lane == expert + EXPERTS, tags, 0.0)
        codes = jnp.sum(codes, axis=1, keepdims=True)
        chosen = (codes == slot).astype(F32)
        placing = chosen.astype(BF16)
        place[k] = placing
        weigh[k] = (chosen * share).astype(BF16)
        picked = contract(placing, hidden[two, :, :D].reshape(pair, D), (0, 0))
        rows_ref[rows, :] = picked.astype(BF16)
        picked = contract(placing, hidden[two, :, D + HD :].reshape(pair, D), (0, 0))
        slot_grads[rows, :] = picked.astype(BF16)
        row_share = contract(weigh[k], jnp.ones((pair, HD), BF16), (0, 0))[:, :1]
        grad_out_ref[rows, :] = (row_share * picked).astype(BF16)
    for copy in copies:
        copy.wait()
    chunk = 512
    width = weights.shape[2]

    @pl.loop(0, width // chunk)
    def _(i):
        cols = pl.ds(pl.multiple_of(i * chunk, chunk), chunk)
        gate = jnp.dot(rows_ref[...], weights[0, :, cols], preferred_element_type=F32)
        upper = jnp.dot(rows_ref[...], weights[1, :, cols], preferred_element_type=F32)
        grad_act = jnp.dot(grad_out_ref[...], weights[2, :, cols], preferred_element_type=F32)
        sigmoid = jax.nn.sigmoid(gate)
        silu = gate * sigmoid
        act_ref[:, cols] = (silu * upper).astype(BF16)
        grad_gate_ref[:, cols] = (
            grad_act * upper * sigmoid * (1.0 + gate * (1.0 - sigmoid))
        ).astype(BF16)
        grad_up_ref[:, cols] = (grad_act * silu).astype(BF16)

    keep = [
        pltpu.make_async_copy(ours, theirs, sems.at[3, i])
        for i, (ours, theirs) in enumerate(zip(saved, saved_hbm))
    ]
    for copy in keep:
        copy.start()
    dots[...] = jnp.zeros_like(dots)

    def target(k):
        half = n_blocks // 4
        return sent[k // half], slice(2 * (k % half), 2 * (k % half) + 2)

    @pl.loop(0, D // chunk)
    def _(i):
        cols = pl.ds(pl.multiple_of(i * chunk, chunk), chunk)
        out = contract(act_ref[...], weights[2, cols, :], (1, 1)).astype(BF16)
        product = out.astype(F32) * slot_grads[:, cols].astype(F32)
        for j in range(chunk // HD):
            dots[...] += product[:, j * HD : (j + 1) * HD]
        back = contract(grad_gate_ref[...], weights[0, cols, :], (1, 1))
        back += contract(grad_up_ref[...], weights[1, cols, :], (1, 1))
        back = back.astype(BF16)
        for k in range(n_blocks // 2):
            rows = slice(2 * k * CAP, 2 * (k + 1) * CAP)
            back_ref, two = target(k)
            mixed = jnp.dot(weigh[k], out[rows], preferred_element_type=F32).astype(BF16)
            back_ref[two, :, cols] = mixed.reshape(2, length, chunk)
            moved = jnp.dot(place[k], back[rows], preferred_element_type=F32).astype(BF16)
            later = pl.ds(pl.multiple_of(D + i * chunk, chunk), chunk)
            back_ref[two, :, later] = moved.reshape(2, length, chunk)

    total = jnp.sum(dots[...], axis=1, keepdims=True)
    for k in range(n_blocks // 2):
        mine = total[2 * k * CAP : 2 * (k + 1) * CAP]
        mine = jnp.broadcast_to(mine, (2 * CAP, HD)).astype(BF16)
        found = jnp.dot(place[k], mine, preferred_element_type=F32)
        found = jnp.where(lane == expert, found, 0.0).astype(BF16)
        back_ref, two = target(k)
        back_ref[two, :, 2 * D :] = found.reshape(2, length, HD)
    for copy in keep:
        copy.wait()


def expert_call(where, blocks, parts):
    n_blocks, (length, wide) = len(blocks), blocks[0].shape
    rows = n_blocks * CAP
    width = parts[0].shape[2]
    saved = [(rows, D), (rows, D), (rows, width), (rows, width), (rows, width)]
    sent = (n_blocks // 2, length, wide)
    anywhere = pl.BlockSpec(memory_space=pl.ANY)
    return pl.pallas_call(
        functools.partial(expert_body, n_blocks, len(parts)),
        out_shape=[jax.ShapeDtypeStruct(s, BF16) for s in saved + [sent] * 2],
        grid_spec=pltpu.PrefetchScalarGridSpec(
            num_scalar_prefetch=1,
            grid=(1,),
            in_specs=[anywhere] * (n_blocks + len(parts)),
            out_specs=[anywhere] * 5
            + [pl.BlockSpec(sent, lambda *_: (0, 0, 0), pipeline_mode=pl.Buffered(1))] * 2,
            scratch_shapes=[pltpu.VMEM(s, BF16) for s in saved]
            + [
                pltpu.VMEM((n_blocks, length, wide), BF16),
                pltpu.VMEM((3, D, width), BF16),
                pltpu.VMEM((rows, D), BF16),
                pltpu.VMEM((n_blocks // 2, 2 * length, 2 * CAP), BF16),
                pltpu.VMEM((n_blocks // 2, 2 * length, 2 * CAP), BF16),
                pltpu.VMEM((rows, HD), F32),
                pltpu.SemaphoreType.DMA((4, max(n_blocks, len(parts)))),
            ],
        ),
        compiler_params=pltpu.CompilerParams(vmem_limit_bytes=VMEM_LIMIT),
        cost_estimate=pl.CostEstimate(flops=13000000000, bytes_accessed=38000000, transcendentals=0),
        name="expert",
    )(where, *blocks, *parts)


def sums_body(n, where_ref, *refs):
    ins, outs = refs[: 5 * n], refs[5 * n :]
    rows, grad_out, act, grad_gate, grad_up = (ins[i * n : (i + 1) * n] for i in range(5))
    for i, out in enumerate(outs):

        @pl.when(pl.program_id(0) == i)
        def _():
            for j, (left, right) in enumerate(((rows, grad_gate), (rows, grad_up), (grad_out, act))):
                total = contract(left[0][...], right[0][...], (0, 0))
                for h in range(1, n):
                    total += contract(left[h][...], right[h][...], (0, 0))
                out[j] = total.astype(BF16)


def sums_call(where, saved, slab):
    n = len(saved)
    count = where.shape[0]
    length, width = saved[0][2].shape
    by_slab = pl.BlockSpec((length, slab), lambda i, ref: (0, ref[i]))
    fixed = pl.BlockSpec((length, width), lambda i, ref: (0, 0), pipeline_mode=pl.Buffered(1))
    args = [saved[h][j] for j in range(5) for h in range(n)]
    return pl.pallas_call(
        functools.partial(sums_body, n),
        out_shape=[jax.ShapeDtypeStruct((3, slab, width), BF16)] * count,
        grid_spec=pltpu.PrefetchScalarGridSpec(
            num_scalar_prefetch=1,
            grid=(count,),
            in_specs=[by_slab] * (2 * n) + [fixed] * (3 * n),
            out_specs=[
                pl.BlockSpec((3, slab, width), lambda i, ref: (0, 0, 0), pipeline_mode=pl.Buffered(1))
            ]
            * count,
        ),
        compiler_params=pltpu.CompilerParams(vmem_limit_bytes=VMEM_LIMIT),
        cost_estimate=pl.CostEstimate(flops=6500000000, bytes_accessed=30000000, transcendentals=0),
        name="expert_sums",
    )(where, *args)


def pack_body(where_ref, gate_ref, up_ref, down_ref, *outs):
    for i, out in enumerate(outs):

        @pl.when(pl.program_id(0) == i)
        def _():
            out[0] = gate_ref[0]
            out[1] = up_ref[0]
            out[2] = down_ref[0].T


def pack_call(where, gate, up, down):
    count, slab, width = gate.shape
    upright = pl.BlockSpec((1, slab, width), lambda i, ref: (ref[i], 0, 0))
    return pl.pallas_call(
        pack_body,
        out_shape=[jax.ShapeDtypeStruct((3, slab, width), BF16)] * count,
        grid_spec=pltpu.PrefetchScalarGridSpec(
            num_scalar_prefetch=1,
            grid=(count,),
            in_specs=[upright, upright, pl.BlockSpec((1, width, slab), lambda i, ref: (ref[i], 0, 0))],
            out_specs=[pl.BlockSpec((3, slab, width), lambda i, ref: (0, 0, 0))] * count,
        ),
        compiler_params=pltpu.CompilerParams(vmem_limit_bytes=VMEM_LIMIT),
        cost_estimate=pl.CostEstimate(flops=0, bytes_accessed=25000000, transcendentals=0),
        name="pack",
    )(where, gate, up, down)


def unpack_body(counts, where_ref, *refs):
    parts, (gate_ref, up_ref, down_ref) = refs[:-3], refs[-3:]
    at = 0
    for i, count in enumerate(counts):

        @pl.when(pl.program_id(0) == i)
        def _(some=parts[at : at + count]):
            first = 0
            for part in some:
                rows = slice(first, first + part.shape[1])
                gate_ref[0, rows] = part[0].astype(F32)
                up_ref[0, rows] = part[1].astype(F32)
                down_ref[0, :, rows] = part[2].astype(F32).T
                first += part.shape[1]

        at += count


def unpack_call(where, parts):
    count = len(parts)
    width = parts[0][0].shape[2]
    slab = sum(part.shape[1] for part in parts[0])
    flat = [part for some in parts for part in some]
    upright = pl.BlockSpec((1, slab, width), lambda i, ref: (ref[i], 0, 0))
    return pl.pallas_call(
        functools.partial(unpack_body, [len(some) for some in parts]),
        out_shape=[jax.ShapeDtypeStruct((count, slab, width), F32)] * 2
        + [jax.ShapeDtypeStruct((count, width, slab), F32)],
        grid_spec=pltpu.PrefetchScalarGridSpec(
            num_scalar_prefetch=1,
            grid=(count,),
            in_specs=[
                pl.BlockSpec(part.shape, lambda i, ref: (0, 0, 0), pipeline_mode=pl.Buffered(1))
                for part in flat
            ],
            out_specs=[upright, upright, pl.BlockSpec((1, width, slab), lambda i, ref: (ref[i], 0, 0))],
        ),
        compiler_params=pltpu.CompilerParams(vmem_limit_bytes=VMEM_LIMIT),
        cost_estimate=pl.CostEstimate(flops=0, bytes_accessed=32000000, transcendentals=0),
        name="unpack",
    )(where, *flat)


def heads_body(n_blocks, where_ref, *refs):
    blocks, (gain_ref, weight_ref, hidden_ref, raw_ref, sums_ref, tokens, sems) = (
        refs[:n_blocks],
        refs[n_blocks:],
    )
    step = pl.program_id(0)
    copies = [pltpu.make_async_copy(b, tokens.at[k], sems.at[k]) for k, b in enumerate(blocks)]

    @pl.when(step == 0)
    def _():
        for copy in copies:
            copy.start()
        for copy in copies:
            copy.wait()

    values = tokens[step].astype(F32)
    hidden = (values * inv_root(values) * gain_ref[...]).astype(BF16)
    hidden_ref[...] = hidden
    raw = jnp.dot(hidden, weight_ref[...], preferred_element_type=F32)
    raw_ref[...] = raw
    slab = raw.shape[1] // 3
    query, key = raw[:, :slab], raw[:, slab : 2 * slab]
    sums_ref[...] = by_token(
        jnp.sum(query * query, axis=1, keepdims=True), jnp.sum(key * key, axis=1, keepdims=True)
    )


def by_token(first, second):
    lane = lax.broadcasted_iota(jnp.int32, (first.shape[0], HD), 1)
    both = jnp.where(lane == 0, first, jnp.where(lane == 1, second, 0.0))
    return both.T[:8]


def heads_call(where, blocks, gain, weight):
    count, (length, _), wide = len(blocks), blocks[0].shape, weight.shape[1]
    span = count * length
    return pl.pallas_call(
        functools.partial(heads_body, count),
        grid_spec=pltpu.PrefetchScalarGridSpec(
            num_scalar_prefetch=1,
            grid=(count,),
            in_specs=[pl.BlockSpec(memory_space=pl.ANY)] * count
            + [
                pl.BlockSpec((1, D), lambda i, ref: (0, 0)),
                pl.BlockSpec((D, wide), lambda i, ref: (0, 0), pipeline_mode=pl.Buffered(1)),
            ],
            out_specs=[
                pl.BlockSpec((length, D), lambda i, ref: (ref[i], 0)),
                pl.BlockSpec((length, wide), lambda i, ref: (ref[i], 0)),
                pl.BlockSpec((8, length), lambda i, ref: (0, ref[i])),
            ],
            scratch_shapes=[
                pltpu.VMEM((count, length, D), BF16),
                pltpu.SemaphoreType.DMA((count,)),
            ],
        ),
        out_shape=[
            jax.ShapeDtypeStruct((span, D), BF16),
            jax.ShapeDtypeStruct((span, wide), F32),
            jax.ShapeDtypeStruct((8, span), F32),
        ],
        compiler_params=pltpu.CompilerParams(vmem_limit_bytes=VMEM_LIMIT),
        cost_estimate=pl.CostEstimate(flops=3300000000, bytes_accessed=12000000, transcendentals=0),
        name="heads",
    )(where, *blocks, gain, weight)


def project_body(order_ref, attended_ref, weight_ref, out_ref):
    out_ref[0] = jnp.dot(
        attended_ref[...], weight_ref[...], preferred_element_type=F32
    ).astype(BF16)


def project_call(order, attended, weight):
    span, slab = attended.shape
    count = order.shape[0]
    length = span // count
    return pl.pallas_call(
        project_body,
        out_shape=jax.ShapeDtypeStruct((count, length, D), BF16),
        grid_spec=pltpu.PrefetchScalarGridSpec(
            num_scalar_prefetch=1,
            grid=(count,),
            in_specs=[
                pl.BlockSpec((length, slab), lambda i, ref: (ref[i], 0)),
                pl.BlockSpec((slab, D), lambda i, ref: (0, 0), pipeline_mode=pl.Buffered(1)),
            ],
            out_specs=pl.BlockSpec((1, length, D), lambda i, ref: (i, 0, 0)),
        ),
        compiler_params=pltpu.CompilerParams(vmem_limit_bytes=VMEM_LIMIT),
        cost_estimate=pl.CostEstimate(flops=1100000000, bytes_accessed=6000000, transcendentals=0),
        name="project",
    )(order, attended, weight)


def project_back_body(n_blocks, where_ref, *refs):
    blocks, (attended_ref, weight_ref, grad_ref, sum_ref, grads, total, sems) = (
        refs[:n_blocks],
        refs[n_blocks:],
    )
    step = pl.program_id(0)
    copies = [pltpu.make_async_copy(b, grads.at[k], sems.at[k]) for k, b in enumerate(blocks)]

    @pl.when(step == 0)
    def _():
        for copy in copies:
            copy.start()
        total[...] = jnp.zeros_like(total)
        for copy in copies:
            copy.wait()

    mine = grads[step]
    grad_ref[...] = contract(mine, weight_ref[...], (1, 1)).astype(BF16)
    total[...] += contract(attended_ref[...], mine, (0, 0))

    @pl.when(step == n_blocks - 1)
    def _():
        sum_ref[...] = total[...].astype(BF16)


def project_back_call(where, blocks, attended, weight):
    span, slab = attended.shape
    count, (length, _) = len(blocks), blocks[0].shape
    return pl.pallas_call(
        functools.partial(project_back_body, count),
        out_shape=[jax.ShapeDtypeStruct((span, slab), BF16), jax.ShapeDtypeStruct((slab, D), BF16)],
        grid_spec=pltpu.PrefetchScalarGridSpec(
            num_scalar_prefetch=1,
            grid=(count,),
            in_specs=[pl.BlockSpec(memory_space=pl.ANY)] * count
            + [
                pl.BlockSpec((length, slab), lambda i, ref: (ref[i], 0)),
                pl.BlockSpec((slab, D), lambda i, ref: (0, 0), pipeline_mode=pl.Buffered(1)),
            ],
            out_specs=[
                pl.BlockSpec((length, slab), lambda i, ref: (ref[i], 0)),
                pl.BlockSpec((slab, D), lambda i, ref: (0, 0)),
            ],
            scratch_shapes=[
                pltpu.VMEM((count, length, D), BF16),
                pltpu.VMEM((slab, D), F32),
                pltpu.SemaphoreType.DMA((count,)),
            ],
        ),
        compiler_params=pltpu.CompilerParams(vmem_limit_bytes=VMEM_LIMIT),
        cost_estimate=pl.CostEstimate(flops=2200000000, bytes_accessed=10000000, transcendentals=0),
        name="project_back",
    )(where, *blocks, attended, weight)


def turn(values, cosine, sine, sign):
    return values * cosine + sign * pltpu.roll(values, HD // 2, 1) * sine


def ready(head, raw_ref, stats, gains_ref, cosine, sine):
    slab = raw_ref.shape[1] // 3
    cols = slice(head * HD, (head + 1) * HD)
    found = []
    for j in range(2):
        inverse = lax.rsqrt(stats[:, j : j + 1] / D + EPS)
        hat = raw_ref[:, j * slab + head * HD : j * slab + (head + 1) * HD] * inverse
        gain = gains_ref[j : j + 1, cols]
        found.append((turn(hat * gain, cosine, sine, 1.0).astype(BF16), hat, gain))
    value = raw_ref[:, 2 * slab + head * HD : 2 * slab + (head + 1) * HD].astype(BF16)
    return found[0], found[1], value


def soften(first, last, query, key_ref, stats, docs, low):
    scores = contract(query, key_ref[low:last, :], (1, 1)) * HD ** (-0.5)
    row = first + lax.broadcasted_iota(jnp.int32, scores.shape, 0)
    col = low + lax.broadcasted_iota(jnp.int32, scores.shape, 1)
    offset = row - col
    allowed = (offset >= 0) & (offset < WINDOW) & (stats[first:last, 2:3] == docs[:, low:last])
    scores = jnp.where(allowed, scores, NEG)
    expo = jnp.exp(scores - jnp.max(scores, axis=1, keepdims=True))
    return expo * (1.0 / jnp.sum(expo, axis=1, keepdims=True))


def ranges(span):
    rows, reach = 256, min(WINDOW, span // 2)
    return [(i, i + rows, max(0, (i - reach) // rows * rows)) for i in range(0, span, rows)]


def attend_body(raw_ref, rows_ref, gains_ref, cosine_ref, sine_ref, out_ref, key_ref):
    span = raw_ref.shape[0]
    stats = rows_ref[...].T
    docs = rows_ref[2:3, :]
    for head in range(out_ref.shape[1] // HD):
        (query, _, _), (key, _, _), value = ready(
            head, raw_ref, stats, gains_ref, cosine_ref[...], sine_ref[...]
        )
        key_ref[...] = key
        for first, last, low in ranges(span):
            probs = soften(first, last, query[first:last], key_ref, stats, docs, low)
            out_ref[first:last, head * HD : (head + 1) * HD] = jnp.dot(
                probs.astype(BF16), value[low:last], preferred_element_type=F32
            ).astype(BF16)


def attend_call(raw, rows, gains, cosine, sine):
    span, wide = raw.shape
    return pl.pallas_call(
        attend_body,
        out_shape=jax.ShapeDtypeStruct((span, wide // 3), BF16),
        scratch_shapes=[pltpu.VMEM((span, HD), BF16)],
        compiler_params=pltpu.CompilerParams(vmem_limit_bytes=VMEM_LIMIT),
        cost_estimate=pl.CostEstimate(flops=1000000000, bytes_accessed=6000000, transcendentals=0),
        name="attend",
    )(raw, rows, gains, cosine, sine)


def attend_back_body(
    raw_ref,
    rows_ref,
    gains_ref,
    cosine_ref,
    sine_ref,
    grad_ref,
    weighted_ref,
    grad_values_ref,
    grad_gains_ref,
    sums_ref,
    key_ref,
    grad_query,
    grad_key,
    grad_value,
):
    span = raw_ref.shape[0]
    slab = grad_ref.shape[1]
    stats = rows_ref[...].T
    docs = rows_ref[2:3, :]
    cosine, sine = cosine_ref[...], sine_ref[...]
    grad_gains_ref[...] = jnp.zeros_like(grad_gains_ref)
    totals = [jnp.zeros((span, 1), F32), jnp.zeros((span, 1), F32)]
    for head in range(slab // HD):
        cols = slice(head * HD, (head + 1) * HD)
        (query, query_hat, query_gain), (key, key_hat, key_gain), value = ready(
            head, raw_ref, stats, gains_ref, cosine, sine
        )
        key_ref[...] = key
        grad_key[...] = jnp.zeros_like(grad_key)
        grad_value[...] = jnp.zeros_like(grad_value)
        for first, last, low in ranges(span):
            probs = soften(first, last, query[first:last], key_ref, stats, docs, low)
            grad_out = grad_ref[first:last, cols]
            grad_probs = contract(grad_out, value[low:last], (1, 1))
            inner = jnp.sum(probs * grad_probs, axis=1, keepdims=True)
            grad_scores = (probs * (grad_probs - inner)).astype(BF16)
            grad_query[first:last, :] = jnp.dot(
                grad_scores, key_ref[low:last, :], preferred_element_type=F32
            )
            grad_key[low:last, :] += contract(grad_scores, query[first:last], (0, 0))
            grad_value[low:last, :] += contract(probs.astype(BF16), grad_out, (0, 0))
        grad_values_ref[:, cols] = grad_value[...].astype(BF16)
        for j, (grad, hat, gain) in enumerate(
            ((grad_query, query_hat, query_gain), (grad_key, key_hat, key_gain))
        ):
            grad_norm = turn(grad[...] * HD ** (-0.5), cosine, sine, -1.0)
            grad_gains_ref[j : j + 1, cols] = jnp.sum(grad_norm * hat, axis=0, keepdims=True)
            weighted = grad_norm * gain
            weighted_ref[:, j * slab + head * HD : j * slab + (head + 1) * HD] = weighted
            totals[j] += jnp.sum(weighted * hat, axis=1, keepdims=True)
    sums_ref[...] = by_token(*totals)


def attend_back_call(raw, rows, gains, cosine, sine, grad):
    span, slab = grad.shape
    return pl.pallas_call(
        attend_back_body,
        out_shape=[
            jax.ShapeDtypeStruct((span, 2 * slab), F32),
            jax.ShapeDtypeStruct((span, slab), BF16),
            jax.ShapeDtypeStruct((8, slab), F32),
            jax.ShapeDtypeStruct((8, span), F32),
        ],
        scratch_shapes=[pltpu.VMEM((span, HD), BF16)] + [pltpu.VMEM((span, HD), F32)] * 3,
        compiler_params=pltpu.CompilerParams(vmem_limit_bytes=VMEM_LIMIT),
        cost_estimate=pl.CostEstimate(flops=2000000000, bytes_accessed=8000000, transcendentals=0),
        name="attend_back",
    )(raw, rows, gains, cosine, sine, grad)


def grad_heads_body(order_ref, weighted_ref, raw_ref, rows_ref, grad_values_ref, weight_ref, raw_out_ref, hidden_out_ref):
    slab = grad_values_ref.shape[1]
    stats = rows_ref[...].T
    for j in range(2):
        cols = slice(j * slab, (j + 1) * slab)
        inverse = lax.rsqrt(stats[:, j : j + 1] / D + EPS)
        hat = raw_ref[:, cols] * inverse
        mean = stats[:, 3 + j : 4 + j] / D
        raw_out_ref[:, cols] = (inverse * (weighted_ref[:, cols] - hat * mean)).astype(BF16)
    raw_out_ref[:, 2 * slab :] = grad_values_ref[...]
    hidden_out_ref[0] = contract(raw_out_ref[...], weight_ref[...], (1, 1)).astype(BF16)


def grad_heads_call(order, weighted, raw, rows, grad_values, weight):
    span, slab = grad_values.shape
    count = order.shape[0]
    length = span // count

    def spec(width):
        return pl.BlockSpec((length, width), lambda i, ref: (ref[i], 0))

    return pl.pallas_call(
        grad_heads_body,
        out_shape=[
            jax.ShapeDtypeStruct((span, 3 * slab), BF16),
            jax.ShapeDtypeStruct((count, length, D), BF16),
        ],
        grid_spec=pltpu.PrefetchScalarGridSpec(
            num_scalar_prefetch=1,
            grid=(count,),
            in_specs=[
                spec(2 * slab),
                spec(3 * slab),
                pl.BlockSpec((8, length), lambda i, ref: (0, ref[i])),
                spec(slab),
                pl.BlockSpec((D, 3 * slab), lambda i, ref: (0, 0), pipeline_mode=pl.Buffered(1)),
            ],
            out_specs=[spec(3 * slab), pl.BlockSpec((1, length, D), lambda i, ref: (i, 0, 0))],
        ),
        compiler_params=pltpu.CompilerParams(vmem_limit_bytes=VMEM_LIMIT),
        cost_estimate=pl.CostEstimate(flops=3300000000, bytes_accessed=16000000, transcendentals=0),
        name="grad_heads",
    )(order, weighted, raw, rows, grad_values, weight)


def tie(value, *others):
    return lax.optimization_barrier((value, others))[0]


def cycle(high, low):
    cells = [(0, j) for j in range(low)]
    for i in range(1, high):
        columns = range(low - 1, 0, -1) if i % 2 else range(1, low)
        cells += [(i, j) for j in columns]
    cells += [(i, 0) for i in range(high - 1, 0, -1)]
    return [i * low + j for i, j in cells]


class Ring:
    def __init__(self, count, groups):
        self.count = count
        self.onward, self.backward = [], []
        self.device = {}
        for members in groups:
            for i, member in enumerate(members):
                after = members[(i + 1) % count]
                self.onward.append((member, after))
                self.backward.append((after, member))
                self.device[member] = i

    def gather(self, block, waits=None, other=None, visit=None):
        found, passed = {0: block}, {}
        ahead = behind = block
        fresh = [0]
        for step in range(1, self.count // 2 + 1):
            if waits and step in waits:
                behind = tie(behind, *waits[step])
            if other is not None:
                passed.update({k: other(found[k]) for k in fresh})
            held = [passed[k] for k in fresh if k in passed]
            behind = lax.ppermute(behind, ALL, self.onward)
            if step < (self.count + 1) // 2:
                ahead = lax.ppermute(ahead, ALL, self.backward)
            behind, ahead, *held = lax.optimization_barrier((behind, ahead, *held))
            for k, value in zip(fresh, held):
                passed[k] = value
            fresh = [step]
            found[step] = behind
            if step < (self.count + 1) // 2:
                found[self.count - step] = ahead
                fresh.append(self.count - step)
            if visit is not None and step < self.count // 2:
                waits = {**(waits or {}), step + 1: visit(step, found, passed)}
        found = [found[k] for k in range(self.count)]
        if other is None:
            return found
        last = visit(self.count // 2, found, passed) if visit is not None else ()
        passed.update({k: other(tie(found[k], *last)) for k in fresh})
        return found, [passed[k] for k in range(self.count)]

    def scatter(self, part, visit=None, waits=()):
        half = self.count // 2
        far = self.count - half - 1
        onward = backward = None
        for k in range(half, -1, -1):
            term = part(k).astype(F32) if onward is None else onward.astype(F32) + part(k).astype(F32)
            if k == 0:
                return term if backward is None else term + backward.astype(F32)
            term = term.astype(BF16)
            if waits:
                term = tie(term, *waits)
            onward = lax.ppermute(term, ALL, self.onward)
            if k <= far:
                term = part(self.count - k).astype(F32)
                if backward is not None:
                    term = term + backward.astype(F32)
                backward = lax.ppermute(term.astype(BF16), ALL, self.backward)
                onward, backward = lax.optimization_barrier((onward, backward))
            waits = visit(half - k + 1, onward) if visit is not None else ()


def shards(
    tokens,
    doc_ids,
    expert_ids,
    drop_order,
    w_query,
    w_key,
    w_value,
    w_out,
    w_router,
    gain_attn,
    gain_query,
    gain_key,
    gain_ffn,
    w_gate,
    w_up,
    w_down,
    cotangent,
):
    n_a, n_b, n_e = (lax.axis_size(name) for name in ALL)
    n_c = n_a * n_b
    n_all = n_c * n_e
    group = n_a * n_e
    length = tokens.shape[1]
    span = n_c * length
    slab = D // n_c
    rows = D // n_all
    at_a, at_b, at_e = (lax.axis_index(name) for name in ALL)
    at_c = at_a * n_b + at_b
    expert = at_e * n_a + at_a
    at_all = at_c * n_e + at_e

    walk = cycle(n_a, n_b) if n_b % 2 == 0 and n_a % 2 == 0 else list(range(n_c))
    ctx_ring = Ring(n_c, [[c * n_e + e for c in walk] for e in range(n_e)])
    n_y = n_e // 2
    n_ring = n_a * n_y
    y_walk = cycle(n_a, n_y)
    group_ring = Ring(
        n_ring,
        [
            [((w // n_y) * n_b + b) * n_e + (w % n_y) * 2 + core for w in y_walk]
            for b in range(n_b)
            for core in range(2)
        ],
    )
    swap_cores = [(i, i + 1 - 2 * (i % 2)) for i in range(n_all)]
    table = []
    for i in range(n_all):
        c, e = divmod(i, n_e)
        a, b = divmod(c, n_b)
        p, q = ctx_ring.device[i], group_ring.device[i]
        line = [walk[(p - k) % n_c] for k in range(n_c)]
        for core in (1 - e % 2, e % 2):
            for k in range(n_ring):
                w = y_walk[(q - k) % n_ring]
                line.append((w // n_y) * n_e + (w % n_y) * 2 + core)
        line += [(a + k) % n_a for k in range(n_a)] + [(a - k) % n_a for k in range(n_a)]
        line += [((a - j) % n_a) * n_b + (b + k) % n_b for k in range(n_b) for j in range(n_a)]
        line += [((a + j) % n_a) * n_b + (b + k) % n_b for k in range(n_b) for j in range(n_a)]
        table.append(line)
    line = lax.dynamic_slice_in_dim(jnp.array(table, jnp.int32), at_all, 1, 0)[0]
    cuts = [n_c, 2 * n_ring, n_a, n_a, n_c, n_c]
    ends = [sum(cuts[: i + 1]) for i in range(len(cuts))]
    ctx_spots, group_spots, onward_experts, behind_experts, weight_slabs, grad_slabs = (
        line[end - cut : end] for cut, end in zip(cuts, ends)
    )

    vectors = jnp.stack([gain_attn, gain_query, gain_key, gain_ffn])
    small = jnp.concatenate([w_router.T, vectors]).reshape(-1)
    small = jnp.concatenate([small, doc_ids[0].astype(BF16)])
    small = exchange(jnp.broadcast_to(small[None], (n_all, small.shape[0])), ALL)
    params = small[:, : (EXPERTS + 4) * rows].reshape(n_all, EXPERTS + 4, rows)
    params = params.transpose(1, 0, 2).reshape(EXPERTS + 4, D)
    router_weight = params[:EXPERTS]
    attn_gain, query_gain, key_gain, ffn_gain = params[EXPERTS:].astype(F32)
    documents = pick(small[:, (EXPERTS + 4) * rows :].reshape(n_c, n_e, length), at_e, 1)
    documents = documents.reshape(1, span)
    head_gains = jnp.stack([query_gain, key_gain])
    head_gains = lax.dynamic_slice_in_dim(head_gains, at_c * slab, slab, 1)
    cosine, sine = angles(span)

    def along_a(block, shift):
        return lax.ppermute(block, "a", [(j, (j + shift) % n_a) for j in range(n_a)])

    def along_b(block, shift):
        return lax.ppermute(block, "b", [((j + shift) % n_b, j) for j in range(n_b)])

    packed = pack_call(onward_experts, w_gate, w_up, w_down)
    near = [packed[0]] + [None] * (n_a - 1)
    middle = n_a // 2
    shifts = [j for j in range(1, n_a) if j != middle] + [middle]

    def fetch(j, *after):
        near[j] = along_a(tie(packed[j], *after), j)

    far = {}

    def share(j, *after):
        for k in range(1, n_b):
            far[k, j] = along_b(tie(near[j], *after), k)

    mine = jnp.stack([w_query, w_key, w_value]).reshape(3, rows, n_c, slab)
    mine = mine.transpose(2, 1, 0, 3).reshape(n_c, rows, 3 * slab)
    mine = exchange(mine, CTX)
    chain = list(range(1, n_a))
    fetch(chain[0])
    share(0)
    early = [near[chain[0]]] + [far[k, 0] for k in range(1, n_b)]
    blocks = ctx_ring.gather(tokens[0], {2: [packed[0]], 3: [mine], 4: early})
    head_weight = lax.all_gather(mine, "exp", axis=1, tiled=True).reshape(D, 3 * slab)
    out_weight = lax.all_gather(w_out, "exp", axis=0, tiled=True)
    ring_order = jnp.roll(ctx_spots[::-1], 1)

    expert_iota = jnp.arange(EXPERTS, dtype=jnp.int32)
    named = jnp.sum(
        (expert_ids[0][:, :, None] == expert_iota[None, None, :]).astype(F32), axis=1
    )
    order = drop_order[0, 0]
    earlier = (order[None, :] < order[:, None]).astype(F32)
    slots = jnp.dot(earlier, named, precision=HIGH, preferred_element_type=F32)
    kept = named * (slots < CAP).astype(F32)
    slot_code = jnp.where(kept > 0, slots, -1.0).astype(BF16)
    lanes = jnp.zeros((length, HD - 2 * EXPERTS), BF16)
    grad_rows_in = cotangent[0]
    grad_output = grad_rows_in.astype(F32)

    hidden_first, raw, sums = heads_call(ctx_spots, blocks, attn_gain[None], head_weight)

    def over_heads(values):
        values = exchange(jnp.broadcast_to(values[None], (n_c,) + values.shape), CTX)
        return jnp.sum(values, axis=0)

    kinds = lax.broadcasted_iota(jnp.int32, (8, span), 0)
    stats = jnp.where(kinds == 2, documents.astype(F32), over_heads(sums))
    attended = attend_call(raw, stats, head_gains, cosine, sine)
    partial = project_call(ring_order, attended, out_weight)
    middle_ones = chain[1:-1]
    for j in middle_ones:
        fetch(j, blocks[n_c // 2])
    share(chain[0], near[chain[0]])

    def during_project(step, found):
        if step == 1:
            return [near[j] for j in middle_ones] + [far[k, chain[0]] for k in range(1, n_b)]
        if step == 2 and len(chain) > 1:
            fetch(chain[-1], *[near[j] for j in middle_ones])
            for j in middle_ones:
                share(j, near[j])
        return ()

    attended_out = ctx_ring.scatter(lambda k: partial[k], during_project)
    if len(chain) > 1:
        attended_out = tie(attended_out, near[chain[-1]])
    inputs = tokens[0].astype(F32)
    resid = inputs + attended_out
    inv_second = inv_root(resid)
    normed_second = resid * inv_second
    hidden_second = (normed_second * ffn_gain).astype(BF16)
    logits = ein("td,ed->te", hidden_second, router_weight)
    router_probs = jax.nn.softmax(logits, axis=-1)
    combine = (router_probs * kept).astype(BF16)

    block = jnp.concatenate([hidden_second, combine, slot_code, lanes, grad_rows_in], axis=1)
    if len(chain) > 1:
        share(chain[-1], near[chain[-1]])
    parts = near + [far[k, j] for k in range(1, n_b) for j in range(n_a)]
    where = jnp.concatenate([expert[None], weight_slabs])
    quarter = n_ring // 4
    soon = [k % n_ring for k in range(1 - quarter, quarter + 1)]
    late = [k for k in range(n_ring) if k not in soon]
    results = {}

    def during_rows(step, found, passed):
        if step == 1:
            return [far[k, j] for k in range(1, n_b) for j in middle_ones]
        if step == 2:
            return [far[k, chain[-1]] for k in range(1, n_b)]
        if step == quarter + 1:
            results["soon"] = expert_call(
                where, [passed[k] for k in soon] + [found[k] for k in soon], parts
            )
        if step == n_ring // 2:
            return [results["soon"][-1]]
        return ()

    ours, theirs = group_ring.gather(
        block, None, lambda found: lax.ppermute(found, ALL, swap_cores), during_rows
    )
    *given, give, keep = results["soon"]
    keeps = dict(zip(soon, keep))
    gots = dict(zip(soon, lax.ppermute(give, ALL, swap_cores)))
    *kept_here, give, keep = expert_call(
        where, [theirs[k] for k in late] + [ours[k] for k in late], parts
    )
    keeps.update(zip(late, keep))
    gots.update(zip(late, lax.ppermute(give, ALL, swap_cores)))

    def back_part(k):
        i = (n_ring - k) % n_ring
        return keeps[i].astype(F32) + gots[i].astype(F32)

    def along_b_back(block, shift):
        return lax.ppermute(block, "b", [(j, (j + shift) % n_b) for j in range(n_b)])

    saved = [given, kept_here]
    far_sums = sums_call(grad_slabs[n_a:], saved, slab)
    near_sums = sums_call(grad_slabs[:n_a], [[tie(given[0], far_sums[0])] + given[1:], kept_here], slab)
    moved = {}
    last = ()
    for j in [middle] + shifts[:-1] + [0]:
        for k in range(1, n_b):
            moved[k, j] = along_b_back(tie(far_sums[(k - 1) * n_a + j], *last), k)
        last = [moved[k, j] for k in range(1, n_b)]

    def owner_sum(j, rows=slice(None)):
        total = near_sums[j][:, rows].astype(F32)
        for k in range(1, n_b):
            total += moved[k, j][:, rows].astype(F32)
        return total.astype(BF16)

    cut = slab // 2
    halves = [slice(0, cut), slice(cut, slab)]
    owned = {}

    def give_back(j, *after):
        done = owned.setdefault(j, [])
        done.append(along_a(tie(owner_sum(j, halves[len(done)]), *after), j))

    def during_back(step, found):
        if step == 1:
            return [far_sums[0]]
        if step == 2:
            return [near_sums[0]] + [moved[k, middle] for k in range(1, n_b)]
        if step == 3:
            give_back(middle)
            return owned[middle] + [moved[k, j] for k in range(1, n_b) for j in shifts[:1]]
        return ()

    grad_back = group_ring.scatter(back_part, during_back)
    if not owned:
        give_back(middle)
    give_back(middle, *owned[middle])
    grad_back = tie(grad_back, *owned[middle])
    mixed = grad_back[:, :D]
    grad_rows = grad_back[:, D : 2 * D]
    grad_combine = grad_back[:, 2 * D : 2 * D + EXPERTS]
    output = (resid + mixed).astype(BF16)

    grad_router_probs = grad_combine * kept
    grad_logits = (
        router_probs
        * (grad_router_probs - jnp.sum(router_probs * grad_router_probs, axis=-1, keepdims=True))
    ).astype(BF16)
    grad_router_full = ein("td,te->de", hidden_second, grad_logits)
    grad_hidden_second = dot(grad_logits, router_weight) + grad_rows
    grad_ffn_gain = jnp.sum(grad_hidden_second * normed_second, axis=0)
    grad_resid = grad_output + norm_back(grad_hidden_second, normed_second, inv_second, ffn_gain)
    grad_attn_out = grad_resid.astype(BF16)
    for j in shifts[:1] if n_a > 2 else []:
        give_back(j, grad_attn_out)
        give_back(j, *owned[j])
    first = shifts[:1] if n_a > 2 else []
    blocks = ctx_ring.gather(
        grad_attn_out,
        {
            3: [moved[k, j] for k in range(1, n_b) for j in shifts[1:-1]],
            4: [owned[j][0] for j in first],
        },
    )
    for j in shifts[1:-1]:
        give_back(j, blocks[n_c // 2])
    blocks[0] = tie(blocks[0], *[owned[j][1] for j in first])
    grad_attended, grad_out = project_back_call(ctx_spots, blocks, attended, out_weight)
    owned[0] = [owner_sum(0)]

    def over_exp(values):
        core, at_y = at_e % 2, at_e // 2
        axis = values.ndim - 4
        keep = lax.dynamic_index_in_dim(values, core, axis + 1, False).astype(F32)
        give = lax.dynamic_index_in_dim(values, 1 - core, axis + 1, False)
        keep = keep + lax.ppermute(give, ALL, swap_cores).astype(F32)
        total = lax.dynamic_index_in_dim(keep, at_y, axis, False)
        for k in range(1, n_y):
            give = lax.dynamic_index_in_dim(keep, (at_y + k) % n_y, axis, False).astype(BF16)
            onward = [(i, i - i % n_e + (i % n_e + 2 * k) % n_e) for i in range(n_all)]
            total = total + lax.ppermute(give, ALL, onward).astype(F32)
        return total

    grad_out = over_exp(grad_out.reshape(n_y, 2, rows, D))

    grad_attended = tie(grad_attended, *[owned[j][0] for j in shifts[1:-1]])
    for j in shifts[1:-1]:
        give_back(j, *owned[j])
    weighted, grad_values, grad_head_gains, sums = attend_back_call(
        raw, stats, head_gains, cosine, sine, grad_attended
    )
    sums = over_heads(tie(sums, *[moved[k, 0] for k in range(1, n_b)]))
    stats = jnp.where(kinds < 3, stats, jnp.roll(sums, 3, axis=0))
    grad_raw, grad_hidden = grad_heads_call(ring_order, weighted, raw, stats, grad_values, head_weight)
    grad_heads = ein("td,tf->df", hidden_first, grad_raw).astype(BF16)
    grad_heads = over_exp(grad_heads.reshape(n_c, n_y, 2, rows, 3 * slab))
    grad_heads = grad_heads.astype(BF16)

    def during_first(step, found):
        return [grad_heads] if step == n_c // 2 - 1 else ()

    waits = [owned[j][1] for j in shifts[1:-1]]
    grad_hidden_first = ctx_ring.scatter(lambda k: grad_hidden[k], during_first, waits)
    grad_heads = exchange(grad_heads, CTX).reshape(n_c, rows, 3, slab)
    grad_heads = grad_heads.transpose(2, 1, 0, 3).reshape(3, rows, D).astype(F32)
    grad_hidden_first = tie(grad_hidden_first, grad_heads)

    grad_gate_sum, grad_up_sum, grad_down_sum = unpack_call(
        behind_experts, [owned[j] for j in range(n_a)]
    )

    inv_first = inv_root(inputs)
    normed_first = inputs * inv_first
    grad_attn_gain = jnp.sum(grad_hidden_first * normed_first, axis=0)
    grad_inputs = grad_resid + norm_back(grad_hidden_first, normed_first, inv_first, attn_gain)

    head_gains = grad_head_gains[:2].reshape(2, 1, n_e, rows)
    here = jnp.arange(n_c).reshape(1, n_c, 1, 1) == at_c
    head_gains = jnp.where(here, head_gains, 0.0).reshape(2, n_all, rows)
    sums = jnp.concatenate(
        [
            grad_router_full.T.reshape(EXPERTS, n_all, rows),
            grad_attn_gain.reshape(1, n_all, rows),
            head_gains,
            grad_ffn_gain.reshape(1, n_all, rows),
        ]
    )
    sums = exchange(sums.transpose(1, 0, 2).reshape(n_all, -1), ALL)
    sums = jnp.sum(sums, axis=0).reshape(EXPERTS + 4, rows)
    return (
        output[None],
        grad_inputs[None],
        grad_heads[0],
        grad_heads[1],
        grad_heads[2],
        grad_out,
        sums[:EXPERTS].T,
        sums[EXPERTS],
        sums[EXPERTS + 1],
        sums[EXPERTS + 2],
        sums[EXPERTS + 3],
        grad_gate_sum,
        grad_up_sum,
        grad_down_sum,
    )


def solution(mesh):
    n_c, n_e = mesh.shape["ctx"], mesh.shape["exp"]
    n_a = EXPERTS // n_e
    fine = Mesh(mesh.devices.reshape(n_a, n_c // n_a, n_e), ALL)
    rows, blocks = P(ALL, None), P("exp", CTX, None)
    return jax.shard_map(
        shards,
        mesh=fine,
        in_specs=(blocks, P("exp", CTX), blocks, blocks)
        + (rows,) * 5
        + (P(ALL),) * 4
        + (blocks, blocks, P("exp", None, CTX), blocks),
        out_specs=(blocks, blocks)
        + (rows,) * 5
        + (P(ALL),) * 4
        + (blocks, blocks, P("exp", None, CTX)),
        check_vma=False,
    )
```

```python
import functools

import jax
import jax.numpy as jnp
from jax import lax
from jax.experimental import pallas as pl
from jax.experimental.pallas import tpu as pltpu
from jax.sharding import Mesh, PartitionSpec as P

D = 2048
H = 16
HD = 128
EXPERTS = 16
WINDOW = 1024
CAP = 64

EPS = 1e-05
NEG = -1000000000.0
HIGH = lax.Precision.HIGHEST
F32 = jnp.float32
BF16 = jnp.bfloat16

VMEM_LIMIT = 60 * 1024 * 1024

CTX = ("a", "b")
GROUP = ("a", "exp")
ALL = ("a", "b", "exp")


def dot(left, right):
    return jnp.dot(left, right, preferred_element_type=F32)


def ein(spec, left, right):
    return jnp.einsum(spec, left, right, preferred_element_type=F32)


def exchange(block, axes):
    return lax.all_to_all(block, axes, split_axis=0, concat_axis=0, tiled=True)


def inv_root(values):
    return lax.rsqrt(jnp.mean(values * values, axis=-1, keepdims=True) + EPS)


def norm_back(grad_normed, normed, inverse, gain):
    weighted = grad_normed * gain
    return inverse * (weighted - normed * jnp.mean(weighted * normed, axis=-1, keepdims=True))


def angles(span):
    half = HD // 2
    freqs = 10000.0 ** (-2.0 * jnp.arange(half, dtype=F32) / HD)
    angle = jnp.arange(span, dtype=jnp.int32).astype(F32)[:, None] * freqs[None, :]
    cosine, sine = jnp.cos(angle), jnp.sin(angle)
    return jnp.concatenate([cosine, cosine], axis=1), jnp.concatenate([-sine, sine], axis=1)


def pick(values, index, axis):
    spots = lax.broadcasted_iota(jnp.int32, values.shape, axis)
    return jnp.sum(jnp.where(spots == index, values, jnp.zeros_like(values)), axis=axis)


def contract(left, right, dims):
    return lax.dot_general(left, right, ((dims[:1], dims[1:]), ((), ())), preferred_element_type=F32)

def expert_body(n_blocks, n_parts, where_ref, *refs):
    blocks, refs = refs[:n_blocks], refs[n_blocks:]
    parts, refs = refs[:n_parts], refs[n_parts:]
    saved_hbm, sent, refs = refs[:5], refs[5:7], refs[7:]
    saved, refs = refs[:5], refs[5:]
    rows_ref, grad_out_ref, act_ref, grad_gate_ref, grad_up_ref = saved
    hidden, weights, slot_grads, place, weigh, dots, sems = refs
    slab = parts[0].shape[1]
    fetched = [pltpu.make_async_copy(b, hidden.at[k], sems.at[0, k]) for k, b in enumerate(blocks)]
    for copy in fetched:
        copy.start()
    copies = []
    for i, part in enumerate(parts):
        spot = pl.multiple_of(where_ref[1 + i] * slab, slab)
        target = weights.at[:, pl.ds(spot, slab), :]
        copies.append(pltpu.make_async_copy(part, target, sems.at[2, i]))
        copies[-1].start()
    expert = where_ref[0]
    length = hidden.shape[1]
    pair = 2 * length
    lane = lax.broadcasted_iota(jnp.int32, (pair, HD), 1)
    slot = lax.broadcasted_iota(jnp.int32, (pair, 2 * CAP), 1)
    slot -= CAP * (lax.broadcasted_iota(jnp.int32, slot.shape, 0) // length)
    slot = jnp.where((slot >= 0) & (slot < CAP), slot, CAP).astype(F32)
    for k in range(n_blocks // 2):
        fetched[2 * k].wait()
        fetched[2 * k + 1].wait()
        rows = pl.ds(2 * k * CAP, 2 * CAP)
        two = slice(2 * k, 2 * k + 2)
        tags = hidden[two, :, D : D + HD].reshape(pair, HD).astype(F32)
        share = jnp.sum(jnp.where(lane == expert, tags, 0.0), axis=1, keepdims=True)
        codes = jnp.where(lane == expert + EXPERTS, tags, 0.0)
        codes = jnp.sum(codes, axis=1, keepdims=True)
        chosen = (codes == slot).astype(F32)
        placing = chosen.astype(BF16)
        place[k] = placing
        weigh[k] = (chosen * share).astype(BF16)
        picked = contract(placing, hidden[two, :, :D].reshape(pair, D), (0, 0))
        rows_ref[rows, :] = picked.astype(BF16)
        picked = contract(placing, hidden[two, :, D + HD :].reshape(pair, D), (0, 0))
        slot_grads[rows, :] = picked.astype(BF16)
        row_share = contract(weigh[k], jnp.ones((pair, HD), BF16), (0, 0))[:, :1]
        grad_out_ref[rows, :] = (row_share * picked).astype(BF16)
    for copy in copies:
        copy.wait()
    chunk = 512
    width = weights.shape[2]

    @pl.loop(0, width // chunk)
    def _(i):
        cols = pl.ds(pl.multiple_of(i * chunk, chunk), chunk)
        gate = jnp.dot(rows_ref[...], weights[0, :, cols], preferred_element_type=F32)
        upper = jnp.dot(rows_ref[...], weights[1, :, cols], preferred_element_type=F32)
        grad_act = jnp.dot(grad_out_ref[...], weights[2, :, cols], preferred_element_type=F32)
        sigmoid = jax.nn.sigmoid(gate)
        silu = gate * sigmoid
        act_ref[:, cols] = (silu * upper).astype(BF16)
        grad_gate_ref[:, cols] = (
            grad_act * upper * sigmoid * (1.0 + gate * (1.0 - sigmoid))
        ).astype(BF16)
        grad_up_ref[:, cols] = (grad_act * silu).astype(BF16)

    keep = [
        pltpu.make_async_copy(ours, theirs, sems.at[3, i])
        for i, (ours, theirs) in enumerate(zip(saved, saved_hbm))
    ]
    for copy in keep:
        copy.start()
    dots[...] = jnp.zeros_like(dots)

    def target(k):
        half = n_blocks // 4
        return sent[k // half], slice(2 * (k % half), 2 * (k % half) + 2)

    @pl.loop(0, D // chunk)
    def _(i):
        cols = pl.ds(pl.multiple_of(i * chunk, chunk), chunk)
        out = contract(act_ref[...], weights[2, cols, :], (1, 1)).astype(BF16)
        product = out.astype(F32) * slot_grads[:, cols].astype(F32)
        for j in range(chunk // HD):
            dots[...] += product[:, j * HD : (j + 1) * HD]
        back = contract(grad_gate_ref[...], weights[0, cols, :], (1, 1))
        back += contract(grad_up_ref[...], weights[1, cols, :], (1, 1))
        back = back.astype(BF16)
        for k in range(n_blocks // 2):
            rows = slice(2 * k * CAP, 2 * (k + 1) * CAP)
            back_ref, two = target(k)
            mixed = jnp.dot(weigh[k], out[rows], preferred_element_type=F32).astype(BF16)
            back_ref[two, :, cols] = mixed.reshape(2, length, chunk)
            moved = jnp.dot(place[k], back[rows], preferred_element_type=F32).astype(BF16)
            later = pl.ds(pl.multiple_of(D + i * chunk, chunk), chunk)
            back_ref[two, :, later] = moved.reshape(2, length, chunk)

    total = jnp.sum(dots[...], axis=1, keepdims=True)
    for k in range(n_blocks // 2):
        mine = total[2 * k * CAP : 2 * (k + 1) * CAP]
        mine = jnp.broadcast_to(mine, (2 * CAP, HD)).astype(BF16)
        found = jnp.dot(place[k], mine, preferred_element_type=F32)
        found = jnp.where(lane == expert, found, 0.0).astype(BF16)
        back_ref, two = target(k)
        back_ref[two, :, 2 * D :] = found.reshape(2, length, HD)
    for copy in keep:
        copy.wait()


def expert_call(where, blocks, parts):
    n_blocks, (length, wide) = len(blocks), blocks[0].shape
    rows = n_blocks * CAP
    width = parts[0].shape[2]
    saved = [(rows, D), (rows, D), (rows, width), (rows, width), (rows, width)]
    sent = (n_blocks // 2, length, wide)
    anywhere = pl.BlockSpec(memory_space=pl.ANY)
    return pl.pallas_call(
        functools.partial(expert_body, n_blocks, len(parts)),
        out_shape=[jax.ShapeDtypeStruct(s, BF16) for s in saved + [sent] * 2],
        grid_spec=pltpu.PrefetchScalarGridSpec(
            num_scalar_prefetch=1,
            grid=(1,),
            in_specs=[anywhere] * (n_blocks + len(parts)),
            out_specs=[anywhere] * 5
            + [pl.BlockSpec(sent, lambda *_: (0, 0, 0), pipeline_mode=pl.Buffered(1))] * 2,
            scratch_shapes=[pltpu.VMEM(s, BF16) for s in saved]
            + [
                pltpu.VMEM((n_blocks, length, wide), BF16),
                pltpu.VMEM((3, D, width), BF16),
                pltpu.VMEM((rows, D), BF16),
                pltpu.VMEM((n_blocks // 2, 2 * length, 2 * CAP), BF16),
                pltpu.VMEM((n_blocks // 2, 2 * length, 2 * CAP), BF16),
                pltpu.VMEM((rows, HD), F32),
                pltpu.SemaphoreType.DMA((4, max(n_blocks, len(parts)))),
            ],
        ),
        compiler_params=pltpu.CompilerParams(vmem_limit_bytes=VMEM_LIMIT),
        cost_estimate=pl.CostEstimate(flops=13000000000, bytes_accessed=38000000, transcendentals=0),
        name="expert",
    )(where, *blocks, *parts)


def sums_body(n, where_ref, *refs):
    ins, outs = refs[: 5 * n], refs[5 * n :]
    rows, grad_out, act, grad_gate, grad_up = (ins[i * n : (i + 1) * n] for i in range(5))
    for i, out in enumerate(outs):

        @pl.when(pl.program_id(0) == i)
        def _():
            for j, (left, right) in enumerate(((rows, grad_gate), (rows, grad_up), (grad_out, act))):
                total = contract(left[0][...], right[0][...], (0, 0))
                for h in range(1, n):
                    total += contract(left[h][...], right[h][...], (0, 0))
                out[j] = total.astype(BF16)


def sums_call(where, saved, slab):
    n = len(saved)
    count = where.shape[0]
    length, width = saved[0][2].shape
    by_slab = pl.BlockSpec((length, slab), lambda i, ref: (0, ref[i]))
    fixed = pl.BlockSpec((length, width), lambda i, ref: (0, 0), pipeline_mode=pl.Buffered(1))
    args = [saved[h][j] for j in range(5) for h in range(n)]
    return pl.pallas_call(
        functools.partial(sums_body, n),
        out_shape=[jax.ShapeDtypeStruct((3, slab, width), BF16)] * count,
        grid_spec=pltpu.PrefetchScalarGridSpec(
            num_scalar_prefetch=1,
            grid=(count,),
            in_specs=[by_slab] * (2 * n) + [fixed] * (3 * n),
            out_specs=[
                pl.BlockSpec((3, slab, width), lambda i, ref: (0, 0, 0), pipeline_mode=pl.Buffered(1))
            ]
            * count,
        ),
        compiler_params=pltpu.CompilerParams(vmem_limit_bytes=VMEM_LIMIT),
        cost_estimate=pl.CostEstimate(flops=6500000000, bytes_accessed=30000000, transcendentals=0),
        name="expert_sums",
    )(where, *args)


def pack_body(where_ref, gate_ref, up_ref, down_ref, *outs):
    for i, out in enumerate(outs):

        @pl.when(pl.program_id(0) == i)
        def _():
            out[0] = gate_ref[0]
            out[1] = up_ref[0]
            out[2] = down_ref[0].T


def pack_call(where, gate, up, down):
    count, slab, width = gate.shape
    upright = pl.BlockSpec((1, slab, width), lambda i, ref: (ref[i], 0, 0))
    return pl.pallas_call(
        pack_body,
        out_shape=[jax.ShapeDtypeStruct((3, slab, width), BF16)] * count,
        grid_spec=pltpu.PrefetchScalarGridSpec(
            num_scalar_prefetch=1,
            grid=(count,),
            in_specs=[upright, upright, pl.BlockSpec((1, width, slab), lambda i, ref: (ref[i], 0, 0))],
            out_specs=[pl.BlockSpec((3, slab, width), lambda i, ref: (0, 0, 0))] * count,
        ),
        compiler_params=pltpu.CompilerParams(vmem_limit_bytes=VMEM_LIMIT),
        cost_estimate=pl.CostEstimate(flops=0, bytes_accessed=25000000, transcendentals=0),
        name="pack",
    )(where, gate, up, down)


def unpack_body(counts, where_ref, *refs):
    parts, (gate_ref, up_ref, down_ref) = refs[:-3], refs[-3:]
    at = 0
    for i, count in enumerate(counts):

        @pl.when(pl.program_id(0) == i)
        def _(some=parts[at : at + count]):
            first = 0
            for part in some:
                rows = slice(first, first + part.shape[1])
                gate_ref[0, rows] = part[0].astype(F32)
                up_ref[0, rows] = part[1].astype(F32)
                down_ref[0, :, rows] = part[2].astype(F32).T
                first += part.shape[1]

        at += count


def unpack_call(where, parts):
    count = len(parts)
    width = parts[0][0].shape[2]
    slab = sum(part.shape[1] for part in parts[0])
    flat = [part for some in parts for part in some]
    upright = pl.BlockSpec((1, slab, width), lambda i, ref: (ref[i], 0, 0))
    return pl.pallas_call(
        functools.partial(unpack_body, [len(some) for some in parts]),
        out_shape=[jax.ShapeDtypeStruct((count, slab, width), F32)] * 2
        + [jax.ShapeDtypeStruct((count, width, slab), F32)],
        grid_spec=pltpu.PrefetchScalarGridSpec(
            num_scalar_prefetch=1,
            grid=(count,),
            in_specs=[
                pl.BlockSpec(part.shape, lambda i, ref: (0, 0, 0), pipeline_mode=pl.Buffered(1))
                for part in flat
            ],
            out_specs=[upright, upright, pl.BlockSpec((1, width, slab), lambda i, ref: (ref[i], 0, 0))],
        ),
        compiler_params=pltpu.CompilerParams(vmem_limit_bytes=VMEM_LIMIT),
        cost_estimate=pl.CostEstimate(flops=0, bytes_accessed=32000000, transcendentals=0),
        name="unpack",
    )(where, *flat)


def heads_body(n_blocks, where_ref, *refs):
    blocks, refs = refs[:n_blocks], refs[n_blocks:]
    gain_ref, weight_ref, hidden_ref, raw_hbm, sums_ref, tokens, raw_all, sems = refs
    step = pl.program_id(0)
    length = tokens.shape[1]
    copies = [pltpu.make_async_copy(b, tokens.at[k], sems.at[0, k]) for k, b in enumerate(blocks)]

    def raw_copy(k):
        rows = pl.ds(pl.multiple_of(where_ref[k] * length, length), length)
        return pltpu.make_async_copy(raw_all.at[k], raw_hbm.at[rows], sems.at[1, k])

    @pl.when(step == 0)
    def _():
        for copy in copies:
            copy.start()

    for k in range(0, n_blocks, 2):

        @pl.when(step == k // 2)
        def _():
            copies[k].wait()
            copies[k + 1].wait()

    values = tokens[pl.ds(2 * step, 2)].reshape(2 * length, D).astype(F32)
    hidden = (values * inv_root(values) * gain_ref[...]).astype(BF16)
    for i in range(2):
        k = 2 * step + i
        hidden_ref[lax.rem(n_blocks - k, n_blocks)] = hidden[i * length : (i + 1) * length]
    raw = jnp.dot(hidden, weight_ref[...], preferred_element_type=F32)
    slab = raw.shape[1] // 3
    query, key = raw[:, :slab], raw[:, slab : 2 * slab]
    sums = by_token(
        jnp.sum(query * query, axis=1, keepdims=True), jnp.sum(key * key, axis=1, keepdims=True)
    )
    for i in range(2):
        k = 2 * step + i
        rows = slice(i * length, (i + 1) * length)
        raw_all[k] = raw[rows]
        raw_copy(k).start()
        sums_ref[:, pl.ds(pl.multiple_of(where_ref[k] * length, length), length)] = sums[:, rows]

    @pl.when(step == n_blocks // 2 - 1)
    def _():
        for k in range(n_blocks):
            raw_copy(k).wait()


def by_token(first, second):
    lane = lax.broadcasted_iota(jnp.int32, (first.shape[0], HD), 1)
    both = jnp.where(lane == 0, first, jnp.where(lane == 1, second, 0.0))
    return both.T[:8]


def heads_call(where, blocks, gain, weight):
    count, (length, _), wide = len(blocks), blocks[0].shape, weight.shape[1]
    span = count * length
    return pl.pallas_call(
        functools.partial(heads_body, count),
        grid_spec=pltpu.PrefetchScalarGridSpec(
            num_scalar_prefetch=1,
            grid=(count // 2,),
            in_specs=[pl.BlockSpec(memory_space=pl.ANY)] * count
            + [
                pl.BlockSpec((1, D), lambda i, ref: (0, 0)),
                pl.BlockSpec((D, wide), lambda i, ref: (0, 0), pipeline_mode=pl.Buffered(1)),
            ],
            out_specs=[
                pl.BlockSpec(
                    (count, length, D), lambda i, ref: (0, 0, 0), pipeline_mode=pl.Buffered(1)
                ),
                pl.BlockSpec(memory_space=pl.ANY),
                pl.BlockSpec((8, span), lambda i, ref: (0, 0)),
            ],
            scratch_shapes=[
                pltpu.VMEM((count, length, D), BF16),
                pltpu.VMEM((count, length, wide), F32),
                pltpu.SemaphoreType.DMA((2, count)),
            ],
        ),
        out_shape=[
            jax.ShapeDtypeStruct((count, length, D), BF16),
            jax.ShapeDtypeStruct((span, wide), F32),
            jax.ShapeDtypeStruct((8, span), F32),
        ],
        compiler_params=pltpu.CompilerParams(vmem_limit_bytes=VMEM_LIMIT),
        cost_estimate=pl.CostEstimate(flops=3300000000, bytes_accessed=12000000, transcendentals=0),
        name="heads",
    )(where, *blocks, gain, weight)


def by_two(shape, axis):
    def spec(i):
        def place(step, ref):
            at = ref[2 * step + i]
            return (at, 0) if axis == 0 else (0, at)

        return pl.BlockSpec(shape, place)

    return [spec(0), spec(1)]


def project_body(order_ref, first_ref, second_ref, weight_ref, out_ref):
    attended = jnp.concatenate([first_ref[...], second_ref[...]], axis=0)
    found = jnp.dot(attended, weight_ref[...], preferred_element_type=F32)
    out_ref[...] = found.astype(BF16).reshape(out_ref.shape)


def project_call(order, attended, weight):
    span, slab = attended.shape
    count = order.shape[0]
    length = span // count
    return pl.pallas_call(
        project_body,
        out_shape=jax.ShapeDtypeStruct((count, length, D), BF16),
        grid_spec=pltpu.PrefetchScalarGridSpec(
            num_scalar_prefetch=1,
            grid=(count // 2,),
            in_specs=by_two((length, slab), 0)
            + [pl.BlockSpec((slab, D), lambda i, ref: (0, 0), pipeline_mode=pl.Buffered(1))],
            out_specs=pl.BlockSpec((2, length, D), lambda i, ref: (i, 0, 0)),
        ),
        compiler_params=pltpu.CompilerParams(vmem_limit_bytes=VMEM_LIMIT),
        cost_estimate=pl.CostEstimate(flops=1100000000, bytes_accessed=6000000, transcendentals=0),
        name="project",
    )(order, attended, attended, weight)


def project_back_body(n_blocks, where_ref, *refs):
    blocks, refs = refs[:n_blocks], refs[n_blocks:]
    first_ref, second_ref, weight_ref, grad_ref, sum_ref, grads, total, sems = refs
    step = pl.program_id(0)
    length = grads.shape[1]
    copies = [pltpu.make_async_copy(b, grads.at[k], sems.at[k]) for k, b in enumerate(blocks)]

    @pl.when(step == 0)
    def _():
        for copy in copies:
            copy.start()
        total[...] = jnp.zeros_like(total)

    for k in range(0, n_blocks, 2):

        @pl.when(step == k // 2)
        def _():
            copies[k].wait()
            copies[k + 1].wait()

    mine = grads[pl.ds(2 * step, 2)].reshape(2 * length, D)
    found = contract(mine, weight_ref[...], (1, 1)).astype(BF16)
    for i in range(2):
        rows = pl.ds(pl.multiple_of(where_ref[2 * step + i] * length, length), length)
        grad_ref[rows, :] = found[i * length : (i + 1) * length]
    attended = jnp.concatenate([first_ref[...], second_ref[...]], axis=0)
    total[...] += contract(attended, mine, (0, 0))

    @pl.when(step == n_blocks // 2 - 1)
    def _():
        sum_ref[...] = total[...].astype(BF16)


def project_back_call(where, blocks, attended, weight):
    span, slab = attended.shape
    count, (length, _) = len(blocks), blocks[0].shape
    return pl.pallas_call(
        functools.partial(project_back_body, count),
        out_shape=[jax.ShapeDtypeStruct((span, slab), BF16), jax.ShapeDtypeStruct((slab, D), BF16)],
        grid_spec=pltpu.PrefetchScalarGridSpec(
            num_scalar_prefetch=1,
            grid=(count // 2,),
            in_specs=[pl.BlockSpec(memory_space=pl.ANY)] * count
            + by_two((length, slab), 0)
            + [pl.BlockSpec((slab, D), lambda i, ref: (0, 0), pipeline_mode=pl.Buffered(1))],
            out_specs=[
                pl.BlockSpec((span, slab), lambda i, ref: (0, 0)),
                pl.BlockSpec((slab, D), lambda i, ref: (0, 0)),
            ],
            scratch_shapes=[
                pltpu.VMEM((count, length, D), BF16),
                pltpu.VMEM((slab, D), F32),
                pltpu.SemaphoreType.DMA((count,)),
            ],
        ),
        compiler_params=pltpu.CompilerParams(vmem_limit_bytes=VMEM_LIMIT),
        cost_estimate=pl.CostEstimate(flops=2200000000, bytes_accessed=10000000, transcendentals=0),
        name="project_back",
    )(where, *blocks, attended, attended, weight)


def turn(values, cosine, sine, sign):
    return values * cosine + sign * pltpu.roll(values, HD // 2, 1) * sine


def ready(head, raw_ref, stats, gains_ref, cosine, sine):
    slab = raw_ref.shape[1] // 3
    cols = slice(head * HD, (head + 1) * HD)
    found = []
    for j in range(2):
        inverse = lax.rsqrt(stats[:, j : j + 1] / D + EPS)
        hat = raw_ref[:, j * slab + head * HD : j * slab + (head + 1) * HD] * inverse
        gain = gains_ref[j : j + 1, cols]
        found.append((turn(hat * gain, cosine, sine, 1.0).astype(BF16), hat, gain))
    value = raw_ref[:, 2 * slab + head * HD : 2 * slab + (head + 1) * HD].astype(BF16)
    return found[0], found[1], value


def soften(first, last, query, key_ref, stats, docs, low):
    scores = contract(query, key_ref[low:last, :], (1, 1)) * HD ** (-0.5)
    row = first + lax.broadcasted_iota(jnp.int32, scores.shape, 0)
    col = low + lax.broadcasted_iota(jnp.int32, scores.shape, 1)
    offset = row - col
    allowed = (offset >= 0) & (offset < WINDOW) & (stats[first:last, 2:3] == docs[:, low:last])
    scores = jnp.where(allowed, scores, NEG)
    expo = jnp.exp(scores - jnp.max(scores, axis=1, keepdims=True))
    return expo * (1.0 / jnp.sum(expo, axis=1, keepdims=True))


def ranges(span):
    rows, reach = 256, min(WINDOW, span // 2)
    return [(i, i + rows, max(0, (i - reach) // rows * rows)) for i in range(0, span, rows)]


def attend_body(raw_ref, rows_ref, gains_ref, cosine_ref, sine_ref, out_ref, key_ref):
    span = raw_ref.shape[0]
    stats = rows_ref[...].T
    docs = rows_ref[2:3, :]
    for head in range(out_ref.shape[1] // HD):
        (query, _, _), (key, _, _), value = ready(
            head, raw_ref, stats, gains_ref, cosine_ref[...], sine_ref[...]
        )
        key_ref[...] = key
        for first, last, low in ranges(span):
            probs = soften(first, last, query[first:last], key_ref, stats, docs, low)
            out_ref[first:last, head * HD : (head + 1) * HD] = jnp.dot(
                probs.astype(BF16), value[low:last], preferred_element_type=F32
            ).astype(BF16)


def attend_call(raw, rows, gains, cosine, sine):
    span, wide = raw.shape
    return pl.pallas_call(
        attend_body,
        out_shape=jax.ShapeDtypeStruct((span, wide // 3), BF16),
        scratch_shapes=[pltpu.VMEM((span, HD), BF16)],
        compiler_params=pltpu.CompilerParams(vmem_limit_bytes=VMEM_LIMIT),
        cost_estimate=pl.CostEstimate(flops=1000000000, bytes_accessed=6000000, transcendentals=0),
        name="attend",
    )(raw, rows, gains, cosine, sine)


def attend_back_body(
    raw_ref,
    rows_ref,
    gains_ref,
    cosine_ref,
    sine_ref,
    grad_ref,
    weighted_ref,
    grad_values_ref,
    grad_gains_ref,
    sums_ref,
    key_ref,
    grad_query,
    grad_key,
    grad_value,
):
    span = raw_ref.shape[0]
    slab = grad_ref.shape[1]
    stats = rows_ref[...].T
    docs = rows_ref[2:3, :]
    cosine, sine = cosine_ref[...], sine_ref[...]
    grad_gains_ref[...] = jnp.zeros_like(grad_gains_ref)
    totals = [jnp.zeros((span, 1), F32), jnp.zeros((span, 1), F32)]
    for head in range(slab // HD):
        cols = slice(head * HD, (head + 1) * HD)
        (query, query_hat, query_gain), (key, key_hat, key_gain), value = ready(
            head, raw_ref, stats, gains_ref, cosine, sine
        )
        key_ref[...] = key
        grad_key[...] = jnp.zeros_like(grad_key)
        grad_value[...] = jnp.zeros_like(grad_value)
        for first, last, low in ranges(span):
            probs = soften(first, last, query[first:last], key_ref, stats, docs, low)
            grad_out = grad_ref[first:last, cols]
            grad_probs = contract(grad_out, value[low:last], (1, 1))
            inner = jnp.sum(probs * grad_probs, axis=1, keepdims=True)
            grad_scores = (probs * (grad_probs - inner)).astype(BF16)
            grad_query[first:last, :] = jnp.dot(
                grad_scores, key_ref[low:last, :], preferred_element_type=F32
            )
            grad_key[low:last, :] += contract(grad_scores, query[first:last], (0, 0))
            grad_value[low:last, :] += contract(probs.astype(BF16), grad_out, (0, 0))
        grad_values_ref[:, cols] = grad_value[...].astype(BF16)
        for j, (grad, hat, gain) in enumerate(
            ((grad_query, query_hat, query_gain), (grad_key, key_hat, key_gain))
        ):
            grad_norm = turn(grad[...] * HD ** (-0.5), cosine, sine, -1.0)
            grad_gains_ref[j : j + 1, cols] = jnp.sum(grad_norm * hat, axis=0, keepdims=True)
            weighted = grad_norm * gain
            weighted_ref[:, j * slab + head * HD : j * slab + (head + 1) * HD] = weighted
            totals[j] += jnp.sum(weighted * hat, axis=1, keepdims=True)
    sums_ref[...] = by_token(*totals)


def attend_back_call(raw, rows, gains, cosine, sine, grad):
    span, slab = grad.shape
    return pl.pallas_call(
        attend_back_body,
        out_shape=[
            jax.ShapeDtypeStruct((span, 2 * slab), F32),
            jax.ShapeDtypeStruct((span, slab), BF16),
            jax.ShapeDtypeStruct((8, slab), F32),
            jax.ShapeDtypeStruct((8, span), F32),
        ],
        scratch_shapes=[pltpu.VMEM((span, HD), BF16)] + [pltpu.VMEM((span, HD), F32)] * 3,
        compiler_params=pltpu.CompilerParams(vmem_limit_bytes=VMEM_LIMIT),
        cost_estimate=pl.CostEstimate(flops=2000000000, bytes_accessed=8000000, transcendentals=0),
        name="attend_back",
    )(raw, rows, gains, cosine, sine, grad)


def grad_heads_body(order_ref, *refs):
    pairs, (weight_ref, raw_out_ref, hidden_out_ref) = refs[:8], refs[8:]
    slab = pairs[6].shape[1]
    for i in range(2):
        weighted_ref, raw_ref, rows_ref, grad_values_ref = pairs[i::2]
        length = raw_ref.shape[0]
        rows = slice(i * length, (i + 1) * length)
        stats = rows_ref[...].T
        for j in range(2):
            cols = slice(j * slab, (j + 1) * slab)
            inverse = lax.rsqrt(stats[:, j : j + 1] / D + EPS)
            hat = raw_ref[:, cols] * inverse
            mean = stats[:, 3 + j : 4 + j] / D
            raw_out_ref[rows, cols] = (inverse * (weighted_ref[:, cols] - hat * mean)).astype(BF16)
        raw_out_ref[rows, 2 * slab :] = grad_values_ref[...]
    found = contract(raw_out_ref[...], weight_ref[...], (1, 1)).astype(BF16)
    hidden_out_ref[...] = found.reshape(hidden_out_ref.shape)


def grad_heads_call(order, weighted, raw, rows, grad_values, weight):
    span, slab = grad_values.shape
    count = order.shape[0]
    length = span // count
    return pl.pallas_call(
        grad_heads_body,
        out_shape=[
            jax.ShapeDtypeStruct((span, 3 * slab), BF16),
            jax.ShapeDtypeStruct((count, length, D), BF16),
        ],
        grid_spec=pltpu.PrefetchScalarGridSpec(
            num_scalar_prefetch=1,
            grid=(count // 2,),
            in_specs=by_two((length, 2 * slab), 0)
            + by_two((length, 3 * slab), 0)
            + by_two((8, length), 1)
            + by_two((length, slab), 0)
            + [pl.BlockSpec((D, 3 * slab), lambda i, ref: (0, 0), pipeline_mode=pl.Buffered(1))],
            out_specs=[
                pl.BlockSpec((2 * length, 3 * slab), lambda i, ref: (i, 0)),
                pl.BlockSpec((2, length, D), lambda i, ref: (i, 0, 0)),
            ],
        ),
        compiler_params=pltpu.CompilerParams(vmem_limit_bytes=VMEM_LIMIT),
        cost_estimate=pl.CostEstimate(flops=3300000000, bytes_accessed=16000000, transcendentals=0),
        name="grad_heads",
    )(order, weighted, weighted, raw, raw, rows, rows, grad_values, grad_values, weight)


def tie(value, *others):
    return lax.optimization_barrier((value, others))[0]


def cycle(high, low):
    cells = [(0, j) for j in range(low)]
    for i in range(1, high):
        columns = range(low - 1, 0, -1) if i % 2 else range(1, low)
        cells += [(i, j) for j in columns]
    cells += [(i, 0) for i in range(high - 1, 0, -1)]
    return [i * low + j for i, j in cells]


class Ring:
    def __init__(self, count, groups):
        self.count = count
        self.onward, self.backward = [], []
        self.device = {}
        for members in groups:
            for i, member in enumerate(members):
                after = members[(i + 1) % count]
                self.onward.append((member, after))
                self.backward.append((after, member))
                self.device[member] = i

    def gather(self, block, waits=None, other=None, visit=None):
        found, passed = {0: block}, {}
        ahead = behind = block
        fresh = [0]
        for step in range(1, self.count // 2 + 1):
            if waits and step in waits:
                behind = tie(behind, *waits[step])
            if other is not None:
                passed.update({k: other(found[k]) for k in fresh})
            held = [passed[k] for k in fresh if k in passed]
            behind = lax.ppermute(behind, ALL, self.onward)
            if step < (self.count + 1) // 2:
                ahead = lax.ppermute(ahead, ALL, self.backward)
            behind, ahead, *held = lax.optimization_barrier((behind, ahead, *held))
            for k, value in zip(fresh, held):
                passed[k] = value
            fresh = [step]
            found[step] = behind
            if step < (self.count + 1) // 2:
                found[self.count - step] = ahead
                fresh.append(self.count - step)
            if visit is not None and step < self.count // 2:
                waits = {**(waits or {}), step + 1: visit(step, found, passed)}
        found = [found[k] for k in range(self.count)]
        if other is None:
            return found
        last = visit(self.count // 2, found, passed) if visit is not None else ()
        passed.update({k: other(tie(found[k], *last)) for k in fresh})
        return found, [passed[k] for k in range(self.count)]

    def scatter(self, part, visit=None, waits=()):
        half = self.count // 2
        far = self.count - half - 1
        onward = backward = None
        for k in range(half, -1, -1):
            term = part(k).astype(F32) if onward is None else onward.astype(F32) + part(k).astype(F32)
            if k == 0:
                return term if backward is None else term + backward.astype(F32)
            term = term.astype(BF16)
            if waits:
                term = tie(term, *waits)
            onward = lax.ppermute(term, ALL, self.onward)
            if k <= far:
                term = part(self.count - k).astype(F32)
                if backward is not None:
                    term = term + backward.astype(F32)
                backward = lax.ppermute(term.astype(BF16), ALL, self.backward)
                onward, backward = lax.optimization_barrier((onward, backward))
            waits = visit(half - k + 1, onward) if visit is not None else ()


def shards(
    tokens,
    doc_ids,
    expert_ids,
    drop_order,
    w_query,
    w_key,
    w_value,
    w_out,
    w_router,
    gain_attn,
    gain_query,
    gain_key,
    gain_ffn,
    w_gate,
    w_up,
    w_down,
    cotangent,
):
    n_a, n_b, n_e = (lax.axis_size(name) for name in ALL)
    n_c = n_a * n_b
    n_all = n_c * n_e
    group = n_a * n_e
    length = tokens.shape[1]
    span = n_c * length
    slab = D // n_c
    rows = D // n_all
    at_a, at_b, at_e = (lax.axis_index(name) for name in ALL)
    at_c = at_a * n_b + at_b
    expert = at_e * n_a + at_a
    at_all = at_c * n_e + at_e

    walk = cycle(n_a, n_b) if n_b % 2 == 0 and n_a % 2 == 0 else list(range(n_c))
    ctx_ring = Ring(n_c, [[c * n_e + e for c in walk] for e in range(n_e)])
    n_y = n_e // 2
    n_ring = n_a * n_y
    y_walk = cycle(n_a, n_y)
    group_ring = Ring(
        n_ring,
        [
            [((w // n_y) * n_b + b) * n_e + (w % n_y) * 2 + core for w in y_walk]
            for b in range(n_b)
            for core in range(2)
        ],
    )
    swap_cores = [(i, i + 1 - 2 * (i % 2)) for i in range(n_all)]
    table = []
    for i in range(n_all):
        c, e = divmod(i, n_e)
        a, b = divmod(c, n_b)
        p, q = ctx_ring.device[i], group_ring.device[i]
        line = [walk[(p - k) % n_c] for k in range(n_c)]
        for core in (1 - e % 2, e % 2):
            for k in range(n_ring):
                w = y_walk[(q - k) % n_ring]
                line.append((w // n_y) * n_e + (w % n_y) * 2 + core)
        line += [(a + k) % n_a for k in range(n_a)] + [(a - k) % n_a for k in range(n_a)]
        line += [((a - j) % n_a) * n_b + (b + k) % n_b for k in range(n_b) for j in range(n_a)]
        line += [((a + j) % n_a) * n_b + (b + k) % n_b for k in range(n_b) for j in range(n_a)]
        table.append(line)
    line = lax.dynamic_slice_in_dim(jnp.array(table, jnp.int32), at_all, 1, 0)[0]
    cuts = [n_c, 2 * n_ring, n_a, n_a, n_c, n_c]
    ends = [sum(cuts[: i + 1]) for i in range(len(cuts))]
    ctx_spots, group_spots, onward_experts, behind_experts, weight_slabs, grad_slabs = (
        line[end - cut : end] for cut, end in zip(cuts, ends)
    )

    vectors = jnp.stack([gain_attn, gain_query, gain_key, gain_ffn])
    small = jnp.concatenate([w_router.T, vectors]).reshape(-1)
    small = jnp.concatenate([small, doc_ids[0].astype(BF16)])
    small = exchange(jnp.broadcast_to(small[None], (n_all, small.shape[0])), ALL)
    params = small[:, : (EXPERTS + 4) * rows].reshape(n_all, EXPERTS + 4, rows)
    params = params.transpose(1, 0, 2).reshape(EXPERTS + 4, D)
    router_weight = params[:EXPERTS]
    attn_gain, query_gain, key_gain, ffn_gain = params[EXPERTS:].astype(F32)
    documents = pick(small[:, (EXPERTS + 4) * rows :].reshape(n_c, n_e, length), at_e, 1)
    documents = documents.reshape(1, span)
    head_gains = jnp.stack([query_gain, key_gain])
    head_gains = lax.dynamic_slice_in_dim(head_gains, at_c * slab, slab, 1)
    cosine, sine = angles(span)

    def along_a(block, shift):
        return lax.ppermute(block, "a", [(j, (j + shift) % n_a) for j in range(n_a)])

    def along_b(block, shift):
        return lax.ppermute(block, "b", [((j + shift) % n_b, j) for j in range(n_b)])

    packed = pack_call(onward_experts, w_gate, w_up, w_down)
    near = [packed[0]] + [None] * (n_a - 1)
    middle = n_a // 2
    shifts = [j for j in range(1, n_a) if j != middle] + [middle]

    def fetch(j, *after):
        near[j] = along_a(tie(packed[j], *after), j)

    far = {}

    def share(j, *after):
        for k in range(1, n_b):
            far[k, j] = along_b(tie(near[j], *after), k)

    mine = jnp.stack([w_query, w_key, w_value]).reshape(3, rows, n_c, slab)
    mine = mine.transpose(2, 1, 0, 3).reshape(n_c, rows, 3 * slab)
    mine = exchange(mine, CTX)
    chain = list(range(1, n_a))
    blocks = ctx_ring.gather(tokens[0], {2: [packed[0]], 3: [mine]})
    head_weight = lax.all_gather(mine, "exp", axis=1, tiled=True).reshape(D, 3 * slab)
    out_weight = lax.all_gather(w_out, "exp", axis=0, tiled=True)
    ring_order = jnp.roll(ctx_spots[::-1], 1)

    expert_iota = jnp.arange(EXPERTS, dtype=jnp.int32)
    named = jnp.sum(
        (expert_ids[0][:, :, None] == expert_iota[None, None, :]).astype(F32), axis=1
    )
    order = drop_order[0, 0]
    earlier = (order[None, :] < order[:, None]).astype(F32)
    slots = jnp.dot(earlier, named, precision=HIGH, preferred_element_type=F32)
    kept = named * (slots < CAP).astype(F32)
    slot_code = jnp.where(kept > 0, slots, -1.0).astype(BF16)
    lanes = jnp.zeros((length, HD - 2 * EXPERTS), BF16)
    grad_rows_in = cotangent[0]
    grad_output = grad_rows_in.astype(F32)

    hidden_first, raw, sums = heads_call(ctx_spots, blocks, attn_gain[None], head_weight)

    def over_heads(values):
        values = exchange(jnp.broadcast_to(values[None], (n_c,) + values.shape), CTX)
        return jnp.sum(values, axis=0)

    kinds = lax.broadcasted_iota(jnp.int32, (8, span), 0)
    fetch(chain[0], blocks[n_c // 2])
    share(0, blocks[n_c // 2])
    stats = jnp.where(kinds == 2, documents.astype(F32), over_heads(sums))
    stats = tie(stats, near[chain[0]])
    attended = attend_call(raw, stats, head_gains, cosine, sine)
    partial = project_call(ring_order, attended, out_weight)
    middle_ones = chain[1:-1]
    for j in middle_ones:
        fetch(j, near[chain[0]])
    share(chain[0], near[chain[0]])

    def during_project(step, found):
        if step == 1:
            return [near[j] for j in middle_ones] + [far[k, chain[0]] for k in range(1, n_b)]
        if step == 2 and len(chain) > 1:
            fetch(chain[-1], *[near[j] for j in middle_ones])
            for j in middle_ones:
                share(j, near[j])
        return ()

    attended_out = ctx_ring.scatter(lambda k: partial[k], during_project)
    if len(chain) > 1:
        attended_out = tie(attended_out, near[chain[-1]])
    inputs = tokens[0].astype(F32)
    resid = inputs + attended_out
    inv_second = inv_root(resid)
    normed_second = resid * inv_second
    hidden_second = (normed_second * ffn_gain).astype(BF16)
    logits = ein("td,ed->te", hidden_second, router_weight)
    router_probs = jax.nn.softmax(logits, axis=-1)
    combine = (router_probs * kept).astype(BF16)

    block = jnp.concatenate([hidden_second, combine, slot_code, lanes, grad_rows_in], axis=1)
    if len(chain) > 1:
        share(chain[-1], near[chain[-1]])
    parts = near + [far[k, j] for k in range(1, n_b) for j in range(n_a)]
    where = jnp.concatenate([expert[None], weight_slabs])
    quarter = n_ring // 4
    soon = [k % n_ring for k in range(1 - quarter, quarter + 1)]
    late = [k for k in range(n_ring) if k not in soon]
    results = {}

    def during_rows(step, found, passed):
        if step == 1:
            return [far[k, j] for k in range(1, n_b) for j in middle_ones]
        if step == 2:
            return [far[k, chain[-1]] for k in range(1, n_b)]
        if step == quarter + 1:
            results["soon"] = expert_call(
                where, [passed[k] for k in soon] + [found[k] for k in soon], parts
            )
        if step == n_ring // 2:
            return [results["soon"][-1]]
        return ()

    ours, theirs = group_ring.gather(
        block, None, lambda found: lax.ppermute(found, ALL, swap_cores), during_rows
    )
    *given, give, keep = results["soon"]
    keeps = dict(zip(soon, keep))
    gots = dict(zip(soon, lax.ppermute(give, ALL, swap_cores)))
    *kept_here, give, keep = expert_call(
        where, [theirs[k] for k in late] + [ours[k] for k in late], parts
    )
    keeps.update(zip(late, keep))
    gots.update(zip(late, lax.ppermute(give, ALL, swap_cores)))

    def back_part(k):
        i = (n_ring - k) % n_ring
        return keeps[i].astype(F32) + gots[i].astype(F32)

    def along_b_back(block, shift):
        return lax.ppermute(block, "b", [(j, (j + shift) % n_b) for j in range(n_b)])

    saved = [given, kept_here]
    far_sums = sums_call(grad_slabs[n_a:], saved, slab)
    near_sums = sums_call(grad_slabs[:n_a], [[tie(given[0], far_sums[0])] + given[1:], kept_here], slab)
    moved = {}
    last = ()
    for j in [middle] + shifts[:-1] + [0]:
        for k in range(1, n_b):
            moved[k, j] = along_b_back(tie(far_sums[(k - 1) * n_a + j], *last), k)
        last = [moved[k, j] for k in range(1, n_b)]

    def owner_sum(j, rows=slice(None)):
        total = near_sums[j][:, rows].astype(F32)
        for k in range(1, n_b):
            total += moved[k, j][:, rows].astype(F32)
        return total.astype(BF16)

    cut = slab // 2
    halves = [slice(0, cut), slice(cut, slab)]
    owned = {}

    def give_back(j, *after):
        done = owned.setdefault(j, [])
        done.append(along_a(tie(owner_sum(j, halves[len(done)]), *after), j))

    def during_back(step, found):
        if step == 1:
            return [far_sums[0]]
        if step == 2:
            return [near_sums[0]] + [moved[k, middle] for k in range(1, n_b)]
        if step == 3:
            give_back(middle)
            return owned[middle] + [moved[k, j] for k in range(1, n_b) for j in shifts[:1]]
        return ()

    grad_back = group_ring.scatter(back_part, during_back)
    if not owned:
        give_back(middle)
    give_back(middle, *owned[middle])
    grad_back = tie(grad_back, *owned[middle])
    mixed = grad_back[:, :D]
    grad_rows = grad_back[:, D : 2 * D]
    grad_combine = grad_back[:, 2 * D : 2 * D + EXPERTS]
    output = (resid + mixed).astype(BF16)

    grad_router_probs = grad_combine * kept
    grad_logits = (
        router_probs
        * (grad_router_probs - jnp.sum(router_probs * grad_router_probs, axis=-1, keepdims=True))
    ).astype(BF16)
    grad_router_full = ein("td,te->de", hidden_second, grad_logits)
    grad_hidden_second = dot(grad_logits, router_weight) + grad_rows
    grad_ffn_gain = jnp.sum(grad_hidden_second * normed_second, axis=0)
    grad_resid = grad_output + norm_back(grad_hidden_second, normed_second, inv_second, ffn_gain)
    grad_attn_out = grad_resid.astype(BF16)
    for j in shifts[:1] if n_a > 2 else []:
        give_back(j, grad_attn_out)
        give_back(j, *owned[j])
    first = shifts[:1] if n_a > 2 else []
    blocks = ctx_ring.gather(
        grad_attn_out,
        {
            3: [moved[k, j] for k in range(1, n_b) for j in shifts[1:-1]],
            4: [owned[j][0] for j in first],
        },
    )
    for j in shifts[1:-1]:
        give_back(j, blocks[n_c // 2])
    blocks[0] = tie(blocks[0], *[owned[j][1] for j in first])
    grad_attended, grad_out = project_back_call(ctx_spots, blocks, attended, out_weight)
    owned[0] = [owner_sum(0)]

    stages = []

    def over_exp(values):
        core, at_y = at_e % 2, at_e // 2
        axis = values.ndim - 4
        keep = lax.dynamic_index_in_dim(values, core, axis + 1, False).astype(F32)
        give = lax.dynamic_index_in_dim(values, 1 - core, axis + 1, False)
        keep = keep + lax.ppermute(give, ALL, swap_cores).astype(F32)
        stages.append(keep)
        total = lax.dynamic_index_in_dim(keep, at_y, axis, False)
        for k in range(1, n_y):
            give = lax.dynamic_index_in_dim(keep, (at_y + k) % n_y, axis, False).astype(BF16)
            onward = [(i, i - i % n_e + (i % n_e + 2 * k) % n_e) for i in range(n_all)]
            total = total + lax.ppermute(give, ALL, onward).astype(F32)
        return total

    grad_out = over_exp(grad_out.reshape(n_y, 2, rows, D))

    grad_attended = tie(grad_attended, *[owned[j][0] for j in shifts[1:-1]])
    for j in shifts[1:-1]:
        give_back(j, *owned[j])
    weighted, grad_values, grad_head_gains, sums = attend_back_call(
        raw, stats, head_gains, cosine, sine, grad_attended
    )
    sums = over_heads(tie(sums, *[moved[k, 0] for k in range(1, n_b)]))
    stats = jnp.where(kinds < 3, stats, jnp.roll(sums, 3, axis=0))
    grad_raw, grad_hidden = grad_heads_call(ring_order, weighted, raw, stats, grad_values, head_weight)
    grad_heads = ein("td,tf->df", hidden_first.reshape(span, D), grad_raw).astype(BF16)
    grad_heads = over_exp(grad_heads.reshape(n_c, n_y, 2, rows, 3 * slab))
    grad_heads = grad_heads.astype(BF16)

    def during_first(step, found):
        if step == 1:
            return stages[-1:]
        return [grad_heads] if step == 2 else ()

    waits = [owned[j][1] for j in shifts[1:-1]]
    grad_hidden_first = ctx_ring.scatter(lambda k: grad_hidden[k], during_first, waits)
    grad_heads = exchange(grad_heads, CTX).reshape(n_c, rows, 3, slab)
    grad_hidden_first = tie(grad_hidden_first, grad_heads)
    grad_heads = grad_heads.transpose(2, 1, 0, 3).reshape(3, rows, D).astype(F32)

    grad_gate_sum, grad_up_sum, grad_down_sum = unpack_call(
        behind_experts, [owned[j] for j in range(n_a)]
    )

    inv_first = inv_root(inputs)
    normed_first = inputs * inv_first
    grad_attn_gain = jnp.sum(grad_hidden_first * normed_first, axis=0)
    grad_inputs = grad_resid + norm_back(grad_hidden_first, normed_first, inv_first, attn_gain)

    head_gains = grad_head_gains[:2].reshape(2, 1, n_e, rows)
    here = jnp.arange(n_c).reshape(1, n_c, 1, 1) == at_c
    head_gains = jnp.where(here, head_gains, 0.0).reshape(2, n_all, rows)
    sums = jnp.concatenate(
        [
            grad_router_full.T.reshape(EXPERTS, n_all, rows),
            grad_attn_gain.reshape(1, n_all, rows),
            head_gains,
            grad_ffn_gain.reshape(1, n_all, rows),
        ]
    )
    sums = exchange(sums.transpose(1, 0, 2).reshape(n_all, -1), ALL)
    sums = jnp.sum(sums, axis=0).reshape(EXPERTS + 4, rows)
    return (
        output[None],
        grad_inputs[None],
        grad_heads[0],
        grad_heads[1],
        grad_heads[2],
        grad_out,
        sums[:EXPERTS].T,
        sums[EXPERTS],
        sums[EXPERTS + 1],
        sums[EXPERTS + 2],
        sums[EXPERTS + 3],
        grad_gate_sum,
        grad_up_sum,
        grad_down_sum,
    )


def solution(mesh):
    n_c, n_e = mesh.shape["ctx"], mesh.shape["exp"]
    n_a = EXPERTS // n_e
    fine = Mesh(mesh.devices.reshape(n_a, n_c // n_a, n_e), ALL)
    rows, blocks = P(ALL, None), P("exp", CTX, None)
    return jax.shard_map(
        shards,
        mesh=fine,
        in_specs=(blocks, P("exp", CTX), blocks, blocks)
        + (rows,) * 5
        + (P(ALL),) * 4
        + (blocks, blocks, P("exp", None, CTX), blocks),
        out_specs=(blocks, blocks)
        + (rows,) * 5
        + (P(ALL),) * 4
        + (blocks, blocks, P("exp", None, CTX)),
        check_vma=False,
    )
```

```python
import functools

import jax
import jax.numpy as jnp
from jax import lax
from jax.experimental import pallas as pl
from jax.experimental.pallas import tpu as pltpu
from jax.sharding import Mesh, PartitionSpec as P

D = 2048
H = 16
HD = 128
EXPERTS = 16
WINDOW = 1024
CAP = 64

EPS = 1e-05
NEG = -1000000000.0
HIGH = lax.Precision.HIGHEST
F32 = jnp.float32
BF16 = jnp.bfloat16

VMEM_LIMIT = 60 * 1024 * 1024

CTX = ("a", "b")
GROUP = ("a", "exp")
ALL = ("a", "b", "exp")


def dot(left, right):
    return jnp.dot(left, right, preferred_element_type=F32)


def ein(spec, left, right):
    return jnp.einsum(spec, left, right, preferred_element_type=F32)


def exchange(block, axes):
    return lax.all_to_all(block, axes, split_axis=0, concat_axis=0, tiled=True)


def inv_root(values):
    return lax.rsqrt(jnp.mean(values * values, axis=-1, keepdims=True) + EPS)


def norm_back(grad_normed, normed, inverse, gain):
    weighted = grad_normed * gain
    return inverse * (weighted - normed * jnp.mean(weighted * normed, axis=-1, keepdims=True))


def angles(span):
    half = HD // 2
    freqs = 10000.0 ** (-2.0 * jnp.arange(half, dtype=F32) / HD)
    angle = jnp.arange(span, dtype=jnp.int32).astype(F32)[:, None] * freqs[None, :]
    cosine, sine = jnp.cos(angle), jnp.sin(angle)
    return jnp.concatenate([cosine, cosine], axis=1), jnp.concatenate([-sine, sine], axis=1)


def pick(values, index, axis):
    spots = lax.broadcasted_iota(jnp.int32, values.shape, axis)
    return jnp.sum(jnp.where(spots == index, values, jnp.zeros_like(values)), axis=axis)


def contract(left, right, dims):
    return lax.dot_general(left, right, ((dims[:1], dims[1:]), ((), ())), preferred_element_type=F32)

def expert_body(n_blocks, n_parts, where_ref, *refs):
    blocks, refs = refs[:n_blocks], refs[n_blocks:]
    parts, refs = refs[:n_parts], refs[n_parts:]
    saved_hbm, sent, refs = refs[:5], refs[5:7], refs[7:]
    saved, refs = refs[:5], refs[5:]
    rows_ref, grad_out_ref, act_ref, grad_gate_ref, grad_up_ref = saved
    hidden, weights, slot_grads, place, weigh, dots, sems = refs
    slab = parts[0].shape[1]
    fetched = [pltpu.make_async_copy(b, hidden.at[k], sems.at[0, k]) for k, b in enumerate(blocks)]
    for copy in fetched:
        copy.start()
    copies = []
    for i, part in enumerate(parts):
        spot = pl.multiple_of(where_ref[1 + i] * slab, slab)
        target = weights.at[:, pl.ds(spot, slab), :]
        copies.append(pltpu.make_async_copy(part, target, sems.at[2, i]))
        copies[-1].start()
    expert = where_ref[0]
    length = hidden.shape[1]
    pair = 2 * length
    lane = lax.broadcasted_iota(jnp.int32, (pair, HD), 1)
    slot = lax.broadcasted_iota(jnp.int32, (pair, 2 * CAP), 1)
    slot -= CAP * (lax.broadcasted_iota(jnp.int32, slot.shape, 0) // length)
    slot = jnp.where((slot >= 0) & (slot < CAP), slot, CAP).astype(F32)
    for k in range(n_blocks // 2):
        fetched[2 * k].wait()
        fetched[2 * k + 1].wait()
        rows = pl.ds(2 * k * CAP, 2 * CAP)
        two = slice(2 * k, 2 * k + 2)
        tags = hidden[two, :, D : D + HD].reshape(pair, HD).astype(F32)
        share = jnp.sum(jnp.where(lane == expert, tags, 0.0), axis=1, keepdims=True)
        codes = jnp.where(lane == expert + EXPERTS, tags, 0.0)
        codes = jnp.sum(codes, axis=1, keepdims=True)
        chosen = (codes == slot).astype(F32)
        placing = chosen.astype(BF16)
        place[k] = placing
        weigh[k] = (chosen * share).astype(BF16)
        picked = contract(placing, hidden[two, :, :D].reshape(pair, D), (0, 0))
        rows_ref[rows, :] = picked.astype(BF16)
        picked = contract(placing, hidden[two, :, D + HD :].reshape(pair, D), (0, 0))
        slot_grads[rows, :] = picked.astype(BF16)
        row_share = contract(weigh[k], jnp.ones((pair, HD), BF16), (0, 0))[:, :1]
        grad_out_ref[rows, :] = (row_share * picked).astype(BF16)
    for copy in copies:
        copy.wait()
    chunk = 512
    width = weights.shape[2]

    @pl.loop(0, width // chunk)
    def _(i):
        cols = pl.ds(pl.multiple_of(i * chunk, chunk), chunk)
        gate = jnp.dot(rows_ref[...], weights[0, :, cols], preferred_element_type=F32)
        upper = jnp.dot(rows_ref[...], weights[1, :, cols], preferred_element_type=F32)
        grad_act = jnp.dot(grad_out_ref[...], weights[2, :, cols], preferred_element_type=F32)
        sigmoid = jax.nn.sigmoid(gate)
        silu = gate * sigmoid
        act_ref[:, cols] = (silu * upper).astype(BF16)
        grad_gate_ref[:, cols] = (
            grad_act * upper * sigmoid * (1.0 + gate * (1.0 - sigmoid))
        ).astype(BF16)
        grad_up_ref[:, cols] = (grad_act * silu).astype(BF16)

    keep = [
        pltpu.make_async_copy(ours, theirs, sems.at[3, i])
        for i, (ours, theirs) in enumerate(zip(saved, saved_hbm))
    ]
    for copy in keep:
        copy.start()
    dots[...] = jnp.zeros_like(dots)

    def target(k):
        half = n_blocks // 4
        return sent[k // half], slice(2 * (k % half), 2 * (k % half) + 2)

    @pl.loop(0, D // chunk)
    def _(i):
        cols = pl.ds(pl.multiple_of(i * chunk, chunk), chunk)
        out = contract(act_ref[...], weights[2, cols, :], (1, 1)).astype(BF16)
        product = out.astype(F32) * slot_grads[:, cols].astype(F32)
        for j in range(chunk // HD):
            dots[...] += product[:, j * HD : (j + 1) * HD]
        back = contract(grad_gate_ref[...], weights[0, cols, :], (1, 1))
        back += contract(grad_up_ref[...], weights[1, cols, :], (1, 1))
        back = back.astype(BF16)
        for k in range(n_blocks // 2):
            rows = slice(2 * k * CAP, 2 * (k + 1) * CAP)
            back_ref, two = target(k)
            mixed = jnp.dot(weigh[k], out[rows], preferred_element_type=F32).astype(BF16)
            back_ref[two, :, cols] = mixed.reshape(2, length, chunk)
            moved = jnp.dot(place[k], back[rows], preferred_element_type=F32).astype(BF16)
            later = pl.ds(pl.multiple_of(D + i * chunk, chunk), chunk)
            back_ref[two, :, later] = moved.reshape(2, length, chunk)

    total = jnp.sum(dots[...], axis=1, keepdims=True)
    for k in range(n_blocks // 2):
        mine = total[2 * k * CAP : 2 * (k + 1) * CAP]
        mine = jnp.broadcast_to(mine, (2 * CAP, HD)).astype(BF16)
        found = jnp.dot(place[k], mine, preferred_element_type=F32)
        found = jnp.where(lane == expert, found, 0.0).astype(BF16)
        back_ref, two = target(k)
        back_ref[two, :, 2 * D :] = found.reshape(2, length, HD)
    for copy in keep:
        copy.wait()


def expert_call(where, blocks, parts):
    n_blocks, (length, wide) = len(blocks), blocks[0].shape
    rows = n_blocks * CAP
    width = parts[0].shape[2]
    saved = [(rows, D), (rows, D), (rows, width), (rows, width), (rows, width)]
    sent = (n_blocks // 2, length, wide)
    anywhere = pl.BlockSpec(memory_space=pl.ANY)
    return pl.pallas_call(
        functools.partial(expert_body, n_blocks, len(parts)),
        out_shape=[jax.ShapeDtypeStruct(s, BF16) for s in saved + [sent] * 2],
        grid_spec=pltpu.PrefetchScalarGridSpec(
            num_scalar_prefetch=1,
            grid=(1,),
            in_specs=[anywhere] * (n_blocks + len(parts)),
            out_specs=[anywhere] * 5
            + [pl.BlockSpec(sent, lambda *_: (0, 0, 0), pipeline_mode=pl.Buffered(1))] * 2,
            scratch_shapes=[pltpu.VMEM(s, BF16) for s in saved]
            + [
                pltpu.VMEM((n_blocks, length, wide), BF16),
                pltpu.VMEM((3, D, width), BF16),
                pltpu.VMEM((rows, D), BF16),
                pltpu.VMEM((n_blocks // 2, 2 * length, 2 * CAP), BF16),
                pltpu.VMEM((n_blocks // 2, 2 * length, 2 * CAP), BF16),
                pltpu.VMEM((rows, HD), F32),
                pltpu.SemaphoreType.DMA((4, max(n_blocks, len(parts)))),
            ],
        ),
        compiler_params=pltpu.CompilerParams(vmem_limit_bytes=VMEM_LIMIT),
        cost_estimate=pl.CostEstimate(flops=13000000000, bytes_accessed=38000000, transcendentals=0),
        name="expert",
    )(where, *blocks, *parts)


def sums_body(n, where_ref, *refs):
    ins, outs = refs[: 5 * n], refs[5 * n :]
    rows, grad_out, act, grad_gate, grad_up = (ins[i * n : (i + 1) * n] for i in range(5))
    for i, out in enumerate(outs):

        @pl.when(pl.program_id(0) == i)
        def _():
            for j, (left, right) in enumerate(((rows, grad_gate), (rows, grad_up), (grad_out, act))):
                total = contract(left[0][...], right[0][...], (0, 0))
                for h in range(1, n):
                    total += contract(left[h][...], right[h][...], (0, 0))
                out[j] = total.astype(BF16)


def sums_call(where, saved, slab):
    n = len(saved)
    count = where.shape[0]
    length, width = saved[0][2].shape
    by_slab = pl.BlockSpec((length, slab), lambda i, ref: (0, ref[i]))
    fixed = pl.BlockSpec((length, width), lambda i, ref: (0, 0), pipeline_mode=pl.Buffered(1))
    args = [saved[h][j] for j in range(5) for h in range(n)]
    return pl.pallas_call(
        functools.partial(sums_body, n),
        out_shape=[jax.ShapeDtypeStruct((3, slab, width), BF16)] * count,
        grid_spec=pltpu.PrefetchScalarGridSpec(
            num_scalar_prefetch=1,
            grid=(count,),
            in_specs=[by_slab] * (2 * n) + [fixed] * (3 * n),
            out_specs=[
                pl.BlockSpec((3, slab, width), lambda i, ref: (0, 0, 0), pipeline_mode=pl.Buffered(1))
            ]
            * count,
        ),
        compiler_params=pltpu.CompilerParams(vmem_limit_bytes=VMEM_LIMIT),
        cost_estimate=pl.CostEstimate(flops=6500000000, bytes_accessed=30000000, transcendentals=0),
        name="expert_sums",
    )(where, *args)


def pack_body(where_ref, gate_ref, up_ref, down_ref, *outs):
    for i, out in enumerate(outs):

        @pl.when(pl.program_id(0) == i)
        def _():
            out[0] = gate_ref[0]
            out[1] = up_ref[0]
            out[2] = down_ref[0].T


def pack_call(where, gate, up, down):
    count, slab, width = gate.shape
    upright = pl.BlockSpec((1, slab, width), lambda i, ref: (ref[i], 0, 0))
    return pl.pallas_call(
        pack_body,
        out_shape=[jax.ShapeDtypeStruct((3, slab, width), BF16)] * count,
        grid_spec=pltpu.PrefetchScalarGridSpec(
            num_scalar_prefetch=1,
            grid=(count,),
            in_specs=[upright, upright, pl.BlockSpec((1, width, slab), lambda i, ref: (ref[i], 0, 0))],
            out_specs=[pl.BlockSpec((3, slab, width), lambda i, ref: (0, 0, 0))] * count,
        ),
        compiler_params=pltpu.CompilerParams(vmem_limit_bytes=VMEM_LIMIT),
        cost_estimate=pl.CostEstimate(flops=0, bytes_accessed=25000000, transcendentals=0),
        name="pack",
    )(where, gate, up, down)


def unpack_body(counts, where_ref, *refs):
    parts, (gate_ref, up_ref, down_ref) = refs[:-3], refs[-3:]
    at = 0
    for i, count in enumerate(counts):

        @pl.when(pl.program_id(0) == i)
        def _(some=parts[at : at + count]):
            first = 0
            for part in some:
                rows = slice(first, first + part.shape[1])
                gate_ref[0, rows] = part[0].astype(F32)
                up_ref[0, rows] = part[1].astype(F32)
                down_ref[0, :, rows] = part[2].astype(F32).T
                first += part.shape[1]

        at += count


def unpack_call(where, parts):
    count = len(parts)
    width = parts[0][0].shape[2]
    slab = sum(part.shape[1] for part in parts[0])
    flat = [part for some in parts for part in some]
    upright = pl.BlockSpec((1, slab, width), lambda i, ref: (ref[i], 0, 0))
    return pl.pallas_call(
        functools.partial(unpack_body, [len(some) for some in parts]),
        out_shape=[jax.ShapeDtypeStruct((count, slab, width), F32)] * 2
        + [jax.ShapeDtypeStruct((count, width, slab), F32)],
        grid_spec=pltpu.PrefetchScalarGridSpec(
            num_scalar_prefetch=1,
            grid=(count,),
            in_specs=[
                pl.BlockSpec(part.shape, lambda i, ref: (0, 0, 0), pipeline_mode=pl.Buffered(1))
                for part in flat
            ],
            out_specs=[upright, upright, pl.BlockSpec((1, width, slab), lambda i, ref: (ref[i], 0, 0))],
        ),
        compiler_params=pltpu.CompilerParams(vmem_limit_bytes=VMEM_LIMIT),
        cost_estimate=pl.CostEstimate(flops=0, bytes_accessed=32000000, transcendentals=0),
        name="unpack",
    )(where, *flat)


def heads_body(n_blocks, where_ref, *refs):
    blocks, refs = refs[:n_blocks], refs[n_blocks:]
    gain_ref, weight_ref, hidden_ref, raw_hbm, sums_ref, tokens, raw_all, sems = refs
    step = pl.program_id(0)
    length = tokens.shape[1]
    copies = [pltpu.make_async_copy(b, tokens.at[k], sems.at[0, k]) for k, b in enumerate(blocks)]

    def raw_copy(k):
        rows = pl.ds(pl.multiple_of(where_ref[k] * length, length), length)
        return pltpu.make_async_copy(raw_all.at[k], raw_hbm.at[rows], sems.at[1, k])

    @pl.when(step == 0)
    def _():
        for copy in copies:
            copy.start()

    for k in range(0, n_blocks, 2):

        @pl.when(step == k // 2)
        def _():
            copies[k].wait()
            copies[k + 1].wait()

    values = tokens[pl.ds(2 * step, 2)].reshape(2 * length, D).astype(F32)
    hidden = (values * inv_root(values) * gain_ref[...]).astype(BF16)
    for i in range(2):
        k = 2 * step + i
        hidden_ref[lax.rem(n_blocks - k, n_blocks)] = hidden[i * length : (i + 1) * length]
    raw = jnp.dot(hidden, weight_ref[...], preferred_element_type=F32)
    slab = raw.shape[1] // 3
    query, key = raw[:, :slab], raw[:, slab : 2 * slab]
    sums = by_token(
        jnp.sum(query * query, axis=1, keepdims=True), jnp.sum(key * key, axis=1, keepdims=True)
    )
    for i in range(2):
        k = 2 * step + i
        rows = slice(i * length, (i + 1) * length)
        raw_all[k] = raw[rows]
        raw_copy(k).start()
        sums_ref[:, pl.ds(pl.multiple_of(where_ref[k] * length, length), length)] = sums[:, rows]

    @pl.when(step == n_blocks // 2 - 1)
    def _():
        for k in range(n_blocks):
            raw_copy(k).wait()


def by_token(first, second):
    lane = lax.broadcasted_iota(jnp.int32, (first.shape[0], HD), 1)
    both = jnp.where(lane == 0, first, jnp.where(lane == 1, second, 0.0))
    return both.T[:8]


def heads_call(where, blocks, gain, weight):
    count, (length, _), wide = len(blocks), blocks[0].shape, weight.shape[1]
    span = count * length
    return pl.pallas_call(
        functools.partial(heads_body, count),
        grid_spec=pltpu.PrefetchScalarGridSpec(
            num_scalar_prefetch=1,
            grid=(count // 2,),
            in_specs=[pl.BlockSpec(memory_space=pl.ANY)] * count
            + [
                pl.BlockSpec((1, D), lambda i, ref: (0, 0)),
                pl.BlockSpec((D, wide), lambda i, ref: (0, 0), pipeline_mode=pl.Buffered(1)),
            ],
            out_specs=[
                pl.BlockSpec(
                    (count, length, D), lambda i, ref: (0, 0, 0), pipeline_mode=pl.Buffered(1)
                ),
                pl.BlockSpec(memory_space=pl.ANY),
                pl.BlockSpec((8, span), lambda i, ref: (0, 0)),
            ],
            scratch_shapes=[
                pltpu.VMEM((count, length, D), BF16),
                pltpu.VMEM((count, length, wide), F32),
                pltpu.SemaphoreType.DMA((2, count)),
            ],
        ),
        out_shape=[
            jax.ShapeDtypeStruct((count, length, D), BF16),
            jax.ShapeDtypeStruct((span, wide), F32),
            jax.ShapeDtypeStruct((8, span), F32),
        ],
        compiler_params=pltpu.CompilerParams(vmem_limit_bytes=VMEM_LIMIT),
        cost_estimate=pl.CostEstimate(flops=3300000000, bytes_accessed=12000000, transcendentals=0),
        name="heads",
    )(where, *blocks, gain, weight)


def by_two(shape, axis):
    def spec(i):
        def place(step, ref):
            at = ref[2 * step + i]
            return (at, 0) if axis == 0 else (0, at)

        return pl.BlockSpec(shape, place)

    return [spec(0), spec(1)]


def project_body(order_ref, first_ref, second_ref, weight_ref, out_ref):
    attended = jnp.concatenate([first_ref[...], second_ref[...]], axis=0)
    found = jnp.dot(attended, weight_ref[...], preferred_element_type=F32)
    out_ref[...] = found.astype(BF16).reshape(out_ref.shape)


def project_call(order, attended, weight):
    span, slab = attended.shape
    count = order.shape[0]
    length = span // count
    return pl.pallas_call(
        project_body,
        out_shape=jax.ShapeDtypeStruct((count, length, D), BF16),
        grid_spec=pltpu.PrefetchScalarGridSpec(
            num_scalar_prefetch=1,
            grid=(count // 2,),
            in_specs=by_two((length, slab), 0)
            + [pl.BlockSpec((slab, D), lambda i, ref: (0, 0), pipeline_mode=pl.Buffered(1))],
            out_specs=pl.BlockSpec((2, length, D), lambda i, ref: (i, 0, 0)),
        ),
        compiler_params=pltpu.CompilerParams(vmem_limit_bytes=VMEM_LIMIT),
        cost_estimate=pl.CostEstimate(flops=1100000000, bytes_accessed=6000000, transcendentals=0),
        name="project",
    )(order, attended, attended, weight)


def project_back_body(n_blocks, where_ref, *refs):
    blocks, refs = refs[:n_blocks], refs[n_blocks:]
    first_ref, second_ref, weight_ref, grad_ref, sum_ref, grads, total, sems = refs
    step = pl.program_id(0)
    length = grads.shape[1]
    copies = [pltpu.make_async_copy(b, grads.at[k], sems.at[k]) for k, b in enumerate(blocks)]

    @pl.when(step == 0)
    def _():
        for copy in copies:
            copy.start()
        total[...] = jnp.zeros_like(total)

    for k in range(0, n_blocks, 2):

        @pl.when(step == k // 2)
        def _():
            copies[k].wait()
            copies[k + 1].wait()

    mine = grads[pl.ds(2 * step, 2)].reshape(2 * length, D)
    found = contract(mine, weight_ref[...], (1, 1)).astype(BF16)
    for i in range(2):
        rows = pl.ds(pl.multiple_of(where_ref[2 * step + i] * length, length), length)
        grad_ref[rows, :] = found[i * length : (i + 1) * length]
    attended = jnp.concatenate([first_ref[...], second_ref[...]], axis=0)
    total[...] += contract(attended, mine, (0, 0))

    @pl.when(step == n_blocks // 2 - 1)
    def _():
        sum_ref[...] = total[...].astype(BF16)


def project_back_call(where, blocks, attended, weight):
    span, slab = attended.shape
    count, (length, _) = len(blocks), blocks[0].shape
    return pl.pallas_call(
        functools.partial(project_back_body, count),
        out_shape=[jax.ShapeDtypeStruct((span, slab), BF16), jax.ShapeDtypeStruct((slab, D), BF16)],
        grid_spec=pltpu.PrefetchScalarGridSpec(
            num_scalar_prefetch=1,
            grid=(count // 2,),
            in_specs=[pl.BlockSpec(memory_space=pl.ANY)] * count
            + by_two((length, slab), 0)
            + [pl.BlockSpec((slab, D), lambda i, ref: (0, 0), pipeline_mode=pl.Buffered(1))],
            out_specs=[
                pl.BlockSpec((span, slab), lambda i, ref: (0, 0)),
                pl.BlockSpec((slab, D), lambda i, ref: (0, 0)),
            ],
            scratch_shapes=[
                pltpu.VMEM((count, length, D), BF16),
                pltpu.VMEM((slab, D), F32),
                pltpu.SemaphoreType.DMA((count,)),
            ],
        ),
        compiler_params=pltpu.CompilerParams(vmem_limit_bytes=VMEM_LIMIT),
        cost_estimate=pl.CostEstimate(flops=2200000000, bytes_accessed=10000000, transcendentals=0),
        name="project_back",
    )(where, *blocks, attended, attended, weight)


def turn(values, cosine, sine, sign):
    return values * cosine + sign * pltpu.roll(values, HD // 2, 1) * sine


def ready(head, raw_ref, stats, gains_ref, cosine, sine):
    slab = raw_ref.shape[1] // 3
    cols = slice(head * HD, (head + 1) * HD)
    found = []
    for j in range(2):
        inverse = lax.rsqrt(stats[:, j : j + 1] / D + EPS)
        hat = raw_ref[:, j * slab + head * HD : j * slab + (head + 1) * HD] * inverse
        gain = gains_ref[j : j + 1, cols]
        found.append((turn(hat * gain, cosine, sine, 1.0).astype(BF16), hat, gain))
    value = raw_ref[:, 2 * slab + head * HD : 2 * slab + (head + 1) * HD].astype(BF16)
    return found[0], found[1], value


def soften(first, last, query, key_ref, stats, docs, low):
    scores = contract(query, key_ref[low:last, :], (1, 1)) * HD ** (-0.5)
    row = first + lax.broadcasted_iota(jnp.int32, scores.shape, 0)
    col = low + lax.broadcasted_iota(jnp.int32, scores.shape, 1)
    offset = row - col
    allowed = (offset >= 0) & (offset < WINDOW) & (stats[first:last, 2:3] == docs[:, low:last])
    scores = jnp.where(allowed, scores, NEG)
    expo = jnp.exp(scores - jnp.max(scores, axis=1, keepdims=True))
    return expo * (1.0 / jnp.sum(expo, axis=1, keepdims=True))


def ranges(span):
    rows, reach = 256, min(WINDOW, span // 2)
    return [(i, i + rows, max(0, (i - reach) // rows * rows)) for i in range(0, span, rows)]


def attend_body(raw_ref, rows_ref, gains_ref, cosine_ref, sine_ref, out_ref, key_ref):
    span = raw_ref.shape[0]
    stats = rows_ref[...].T
    docs = rows_ref[2:3, :]
    for head in range(out_ref.shape[1] // HD):
        (query, _, _), (key, _, _), value = ready(
            head, raw_ref, stats, gains_ref, cosine_ref[...], sine_ref[...]
        )
        key_ref[...] = key
        for first, last, low in ranges(span):
            probs = soften(first, last, query[first:last], key_ref, stats, docs, low)
            out_ref[first:last, head * HD : (head + 1) * HD] = jnp.dot(
                probs.astype(BF16), value[low:last], preferred_element_type=F32
            ).astype(BF16)


def attend_call(raw, rows, gains, cosine, sine):
    span, wide = raw.shape
    return pl.pallas_call(
        attend_body,
        out_shape=jax.ShapeDtypeStruct((span, wide // 3), BF16),
        scratch_shapes=[pltpu.VMEM((span, HD), BF16)],
        compiler_params=pltpu.CompilerParams(vmem_limit_bytes=VMEM_LIMIT),
        cost_estimate=pl.CostEstimate(flops=1000000000, bytes_accessed=6000000, transcendentals=0),
        name="attend",
    )(raw, rows, gains, cosine, sine)


def attend_back_body(
    raw_ref,
    rows_ref,
    gains_ref,
    cosine_ref,
    sine_ref,
    grad_ref,
    weighted_ref,
    grad_values_ref,
    grad_gains_ref,
    sums_ref,
    key_ref,
    grad_query,
    grad_key,
    grad_value,
):
    span = raw_ref.shape[0]
    slab = grad_ref.shape[1]
    stats = rows_ref[...].T
    docs = rows_ref[2:3, :]
    cosine, sine = cosine_ref[...], sine_ref[...]
    grad_gains_ref[...] = jnp.zeros_like(grad_gains_ref)
    totals = [jnp.zeros((span, 1), F32), jnp.zeros((span, 1), F32)]
    for head in range(slab // HD):
        cols = slice(head * HD, (head + 1) * HD)
        (query, query_hat, query_gain), (key, key_hat, key_gain), value = ready(
            head, raw_ref, stats, gains_ref, cosine, sine
        )
        key_ref[...] = key
        grad_key[...] = jnp.zeros_like(grad_key)
        grad_value[...] = jnp.zeros_like(grad_value)
        for first, last, low in ranges(span):
            probs = soften(first, last, query[first:last], key_ref, stats, docs, low)
            grad_out = grad_ref[first:last, cols]
            grad_probs = contract(grad_out, value[low:last], (1, 1))
            inner = jnp.sum(probs * grad_probs, axis=1, keepdims=True)
            grad_scores = (probs * (grad_probs - inner)).astype(BF16)
            grad_query[first:last, :] = jnp.dot(
                grad_scores, key_ref[low:last, :], preferred_element_type=F32
            )
            grad_key[low:last, :] += contract(grad_scores, query[first:last], (0, 0))
            grad_value[low:last, :] += contract(probs.astype(BF16), grad_out, (0, 0))
        grad_values_ref[:, cols] = grad_value[...].astype(BF16)
        for j, (grad, hat, gain) in enumerate(
            ((grad_query, query_hat, query_gain), (grad_key, key_hat, key_gain))
        ):
            grad_norm = turn(grad[...] * HD ** (-0.5), cosine, sine, -1.0)
            grad_gains_ref[j : j + 1, cols] = jnp.sum(grad_norm * hat, axis=0, keepdims=True)
            weighted = grad_norm * gain
            weighted_ref[:, j * slab + head * HD : j * slab + (head + 1) * HD] = weighted
            totals[j] += jnp.sum(weighted * hat, axis=1, keepdims=True)
    sums_ref[...] = by_token(*totals)


def attend_back_call(raw, rows, gains, cosine, sine, grad):
    span, slab = grad.shape
    return pl.pallas_call(
        attend_back_body,
        out_shape=[
            jax.ShapeDtypeStruct((span, 2 * slab), F32),
            jax.ShapeDtypeStruct((span, slab), BF16),
            jax.ShapeDtypeStruct((8, slab), F32),
            jax.ShapeDtypeStruct((8, span), F32),
        ],
        scratch_shapes=[pltpu.VMEM((span, HD), BF16)] + [pltpu.VMEM((span, HD), F32)] * 3,
        compiler_params=pltpu.CompilerParams(vmem_limit_bytes=VMEM_LIMIT),
        cost_estimate=pl.CostEstimate(flops=2000000000, bytes_accessed=8000000, transcendentals=0),
        name="attend_back",
    )(raw, rows, gains, cosine, sine, grad)


def grad_heads_body(order_ref, *refs):
    pairs, (weight_ref, raw_out_ref, hidden_out_ref) = refs[:8], refs[8:]
    slab = pairs[6].shape[1]
    for i in range(2):
        weighted_ref, raw_ref, rows_ref, grad_values_ref = pairs[i::2]
        length = raw_ref.shape[0]
        rows = slice(i * length, (i + 1) * length)
        stats = rows_ref[...].T
        for j in range(2):
            cols = slice(j * slab, (j + 1) * slab)
            inverse = lax.rsqrt(stats[:, j : j + 1] / D + EPS)
            hat = raw_ref[:, cols] * inverse
            mean = stats[:, 3 + j : 4 + j] / D
            raw_out_ref[rows, cols] = (inverse * (weighted_ref[:, cols] - hat * mean)).astype(BF16)
        raw_out_ref[rows, 2 * slab :] = grad_values_ref[...]
    found = contract(raw_out_ref[...], weight_ref[...], (1, 1)).astype(BF16)
    hidden_out_ref[...] = found.reshape(hidden_out_ref.shape)


def grad_heads_call(order, weighted, raw, rows, grad_values, weight):
    span, slab = grad_values.shape
    count = order.shape[0]
    length = span // count
    return pl.pallas_call(
        grad_heads_body,
        out_shape=[
            jax.ShapeDtypeStruct((span, 3 * slab), BF16),
            jax.ShapeDtypeStruct((count, length, D), BF16),
        ],
        grid_spec=pltpu.PrefetchScalarGridSpec(
            num_scalar_prefetch=1,
            grid=(count // 2,),
            in_specs=by_two((length, 2 * slab), 0)
            + by_two((length, 3 * slab), 0)
            + by_two((8, length), 1)
            + by_two((length, slab), 0)
            + [pl.BlockSpec((D, 3 * slab), lambda i, ref: (0, 0), pipeline_mode=pl.Buffered(1))],
            out_specs=[
                pl.BlockSpec((2 * length, 3 * slab), lambda i, ref: (i, 0)),
                pl.BlockSpec((2, length, D), lambda i, ref: (i, 0, 0)),
            ],
        ),
        compiler_params=pltpu.CompilerParams(vmem_limit_bytes=VMEM_LIMIT),
        cost_estimate=pl.CostEstimate(flops=3300000000, bytes_accessed=16000000, transcendentals=0),
        name="grad_heads",
    )(order, weighted, weighted, raw, raw, rows, rows, grad_values, grad_values, weight)


def tie(value, *others):
    return lax.optimization_barrier((value, others))[0]


def cycle(high, low):
    cells = [(0, j) for j in range(low)]
    for i in range(1, high):
        columns = range(low - 1, 0, -1) if i % 2 else range(1, low)
        cells += [(i, j) for j in columns]
    cells += [(i, 0) for i in range(high - 1, 0, -1)]
    return [i * low + j for i, j in cells]


class Ring:
    def __init__(self, count, groups):
        self.count = count
        self.onward, self.backward = [], []
        self.device = {}
        for members in groups:
            for i, member in enumerate(members):
                after = members[(i + 1) % count]
                self.onward.append((member, after))
                self.backward.append((after, member))
                self.device[member] = i

    def gather(self, block, waits=None, other=None, visit=None):
        found, passed = {0: block}, {}
        ahead = behind = block
        fresh = [0]
        for step in range(1, self.count // 2 + 1):
            if waits and step in waits:
                behind = tie(behind, *waits[step])
            if other is not None:
                passed.update({k: other(found[k]) for k in fresh})
            held = [passed[k] for k in fresh if k in passed]
            behind = lax.ppermute(behind, ALL, self.onward)
            if step < (self.count + 1) // 2:
                ahead = lax.ppermute(ahead, ALL, self.backward)
            behind, ahead, *held = lax.optimization_barrier((behind, ahead, *held))
            for k, value in zip(fresh, held):
                passed[k] = value
            fresh = [step]
            found[step] = behind
            if step < (self.count + 1) // 2:
                found[self.count - step] = ahead
                fresh.append(self.count - step)
            if visit is not None and step < self.count // 2:
                waits = {**(waits or {}), step + 1: visit(step, found, passed)}
        found = [found[k] for k in range(self.count)]
        if other is None:
            return found
        last = visit(self.count // 2, found, passed) if visit is not None else ()
        passed.update({k: other(tie(found[k], *last)) for k in fresh})
        return found, [passed[k] for k in range(self.count)]

    def scatter(self, part, visit=None, waits=()):
        half = self.count // 2
        far = self.count - half - 1
        onward = backward = None
        for k in range(half, -1, -1):
            term = part(k).astype(F32) if onward is None else onward.astype(F32) + part(k).astype(F32)
            if k == 0:
                return term if backward is None else term + backward.astype(F32)
            term = term.astype(BF16)
            if waits:
                term = tie(term, *waits)
            onward = lax.ppermute(term, ALL, self.onward)
            if k <= far:
                term = part(self.count - k).astype(F32)
                if backward is not None:
                    term = term + backward.astype(F32)
                backward = lax.ppermute(term.astype(BF16), ALL, self.backward)
                onward, backward = lax.optimization_barrier((onward, backward))
            waits = visit(half - k + 1, onward) if visit is not None else ()


def shards(
    tokens,
    doc_ids,
    expert_ids,
    drop_order,
    w_query,
    w_key,
    w_value,
    w_out,
    w_router,
    gain_attn,
    gain_query,
    gain_key,
    gain_ffn,
    w_gate,
    w_up,
    w_down,
    cotangent,
):
    n_a, n_b, n_e = (lax.axis_size(name) for name in ALL)
    n_c = n_a * n_b
    n_all = n_c * n_e
    group = n_a * n_e
    length = tokens.shape[1]
    span = n_c * length
    slab = D // n_c
    rows = D // n_all
    at_a, at_b, at_e = (lax.axis_index(name) for name in ALL)
    at_c = at_a * n_b + at_b
    expert = at_e * n_a + at_a
    at_all = at_c * n_e + at_e

    walk = cycle(n_a, n_b) if n_b % 2 == 0 and n_a % 2 == 0 else list(range(n_c))
    ctx_ring = Ring(n_c, [[c * n_e + e for c in walk] for e in range(n_e)])
    n_y = n_e // 2
    n_ring = n_a * n_y
    y_walk = cycle(n_a, n_y)
    group_ring = Ring(
        n_ring,
        [
            [((w // n_y) * n_b + b) * n_e + (w % n_y) * 2 + core for w in y_walk]
            for b in range(n_b)
            for core in range(2)
        ],
    )
    swap_cores = [(i, i + 1 - 2 * (i % 2)) for i in range(n_all)]
    table = []
    for i in range(n_all):
        c, e = divmod(i, n_e)
        a, b = divmod(c, n_b)
        p, q = ctx_ring.device[i], group_ring.device[i]
        line = [walk[(p - k) % n_c] for k in range(n_c)]
        for core in (1 - e % 2, e % 2):
            for k in range(n_ring):
                w = y_walk[(q - k) % n_ring]
                line.append((w // n_y) * n_e + (w % n_y) * 2 + core)
        line += [(a + k) % n_a for k in range(n_a)] + [(a - k) % n_a for k in range(n_a)]
        line += [((a - j) % n_a) * n_b + (b + k) % n_b for k in range(n_b) for j in range(n_a)]
        line += [((a + j) % n_a) * n_b + (b + k) % n_b for k in range(n_b) for j in range(n_a)]
        table.append(line)
    line = lax.dynamic_slice_in_dim(jnp.array(table, jnp.int32), at_all, 1, 0)[0]
    cuts = [n_c, 2 * n_ring, n_a, n_a, n_c, n_c]
    ends = [sum(cuts[: i + 1]) for i in range(len(cuts))]
    ctx_spots, group_spots, onward_experts, behind_experts, weight_slabs, grad_slabs = (
        line[end - cut : end] for cut, end in zip(cuts, ends)
    )

    vectors = jnp.stack([gain_attn, gain_query, gain_key, gain_ffn])
    small = jnp.concatenate([w_router.T, vectors]).reshape(-1)
    small = jnp.concatenate([small, doc_ids[0].astype(BF16)])
    small = exchange(jnp.broadcast_to(small[None], (n_all, small.shape[0])), ALL)
    params = small[:, : (EXPERTS + 4) * rows].reshape(n_all, EXPERTS + 4, rows)
    params = params.transpose(1, 0, 2).reshape(EXPERTS + 4, D)
    router_weight = params[:EXPERTS]
    attn_gain, query_gain, key_gain, ffn_gain = params[EXPERTS:].astype(F32)
    documents = pick(small[:, (EXPERTS + 4) * rows :].reshape(n_c, n_e, length), at_e, 1)
    documents = documents.reshape(1, span)
    head_gains = jnp.stack([query_gain, key_gain])
    head_gains = lax.dynamic_slice_in_dim(head_gains, at_c * slab, slab, 1)
    cosine, sine = angles(span)

    def along_a(block, shift):
        return lax.ppermute(block, "a", [(j, (j + shift) % n_a) for j in range(n_a)])

    def along_b(block, shift):
        return lax.ppermute(block, "b", [((j + shift) % n_b, j) for j in range(n_b)])

    packed = pack_call(onward_experts, w_gate, w_up, w_down)
    near = [packed[0]] + [None] * (n_a - 1)
    middle = n_a // 2
    shifts = [j for j in range(1, n_a) if j != middle] + [middle]

    def fetch(j, *after):
        near[j] = along_a(tie(packed[j], *after), j)

    far = {}

    def share(j, *after):
        for k in range(1, n_b):
            far[k, j] = along_b(tie(near[j], *after), k)

    mine = jnp.stack([w_query, w_key, w_value]).reshape(3, rows, n_c, slab)
    mine = mine.transpose(2, 1, 0, 3).reshape(n_c, rows, 3 * slab)
    mine = exchange(mine, CTX)
    chain = list(range(1, n_a))
    blocks = ctx_ring.gather(tokens[0], {2: [packed[0]], 3: [mine]})
    head_weight = lax.all_gather(mine, "exp", axis=1, tiled=True).reshape(D, 3 * slab)
    out_weight = lax.all_gather(w_out, "exp", axis=0, tiled=True)
    ring_order = jnp.roll(ctx_spots[::-1], 1)

    expert_iota = jnp.arange(EXPERTS, dtype=jnp.int32)
    named = jnp.sum(
        (expert_ids[0][:, :, None] == expert_iota[None, None, :]).astype(F32), axis=1
    )
    order = drop_order[0, 0]
    earlier = (order[None, :] < order[:, None]).astype(F32)
    slots = jnp.dot(earlier, named, precision=HIGH, preferred_element_type=F32)
    kept = named * (slots < CAP).astype(F32)
    slot_code = jnp.where(kept > 0, slots, -1.0).astype(BF16)
    lanes = jnp.zeros((length, HD - 2 * EXPERTS), BF16)
    grad_rows_in = cotangent[0]
    grad_output = grad_rows_in.astype(F32)

    hidden_first, raw, sums = heads_call(ctx_spots, blocks, attn_gain[None], head_weight)

    def over_heads(values):
        values = exchange(jnp.broadcast_to(values[None], (n_c,) + values.shape), CTX)
        return jnp.sum(values, axis=0)

    kinds = lax.broadcasted_iota(jnp.int32, (8, span), 0)
    fetch(chain[0], blocks[n_c // 2])
    share(0, blocks[n_c // 2])
    stats = jnp.where(kinds == 2, documents.astype(F32), over_heads(sums))
    stats = tie(stats, near[chain[0]])
    attended = attend_call(raw, stats, head_gains, cosine, sine)
    partial = project_call(ring_order, attended, out_weight)
    middle_ones = chain[1:-1]
    for j in middle_ones:
        fetch(j, near[chain[0]])
    share(chain[0], near[chain[0]])

    def during_project(step, found):
        if step == 1:
            return [near[j] for j in middle_ones] + [far[k, chain[0]] for k in range(1, n_b)]
        if step == 2 and len(chain) > 1:
            fetch(chain[-1], *[near[j] for j in middle_ones])
            for j in middle_ones:
                share(j, near[j])
        return ()

    attended_out = ctx_ring.scatter(lambda k: partial[k], during_project)
    if len(chain) > 1:
        attended_out = tie(attended_out, near[chain[-1]])
    inputs = tokens[0].astype(F32)
    resid = inputs + attended_out
    inv_second = inv_root(resid)
    normed_second = resid * inv_second
    hidden_second = (normed_second * ffn_gain).astype(BF16)
    logits = ein("td,ed->te", hidden_second, router_weight)
    router_probs = jax.nn.softmax(logits, axis=-1)
    combine = (router_probs * kept).astype(BF16)

    block = jnp.concatenate([hidden_second, combine, slot_code, lanes, grad_rows_in], axis=1)
    if len(chain) > 1:
        share(chain[-1], near[chain[-1]])
    parts = near + [far[k, j] for k in range(1, n_b) for j in range(n_a)]
    where = jnp.concatenate([expert[None], weight_slabs])
    quarter = n_ring // 4
    soon = [k % n_ring for k in range(1 - quarter, quarter + 1)]
    late = [k for k in range(n_ring) if k not in soon]
    results = {}

    def during_rows(step, found, passed):
        if step == 1:
            return [far[k, j] for k in range(1, n_b) for j in middle_ones]
        if step == 2:
            return [far[k, chain[-1]] for k in range(1, n_b)]
        if step == quarter + 1:
            results["soon"] = expert_call(
                where, [passed[k] for k in soon] + [found[k] for k in soon], parts
            )
        if step == n_ring // 2:
            return [results["soon"][-1]]
        return ()

    ours, theirs = group_ring.gather(
        block, None, lambda found: lax.ppermute(found, ALL, swap_cores), during_rows
    )
    *given, give, keep = results["soon"]
    keeps = dict(zip(soon, keep))
    gots = dict(zip(soon, lax.ppermute(give, ALL, swap_cores)))
    *kept_here, give, keep = expert_call(
        where, [theirs[k] for k in late] + [ours[k] for k in late], parts
    )
    keeps.update(zip(late, keep))
    gots.update(zip(late, lax.ppermute(give, ALL, swap_cores)))

    def back_part(k):
        i = (n_ring - k) % n_ring
        return keeps[i].astype(F32) + gots[i].astype(F32)

    def along_b_back(block, shift):
        return lax.ppermute(block, "b", [(j, (j + shift) % n_b) for j in range(n_b)])

    saved = [given, kept_here]
    far_sums = sums_call(grad_slabs[n_a:], saved, slab)
    near_sums = sums_call(grad_slabs[:n_a], [[tie(given[0], far_sums[0])] + given[1:], kept_here], slab)
    moved = {}
    last = ()
    for j in [middle] + shifts[:-1]:
        for k in range(1, n_b):
            moved[k, j] = along_b_back(tie(far_sums[(k - 1) * n_a + j], *last), k)
        last = [moved[k, j] for k in range(1, n_b)]

    def owner_sum(j, rows=slice(None)):
        total = near_sums[j][:, rows].astype(F32)
        for k in range(1, n_b):
            total += moved[k, j][:, rows].astype(F32)
        return total.astype(BF16)

    cut = slab // 2
    halves = [slice(0, cut), slice(cut, slab)]
    owned = {}

    def give_back(j, *after):
        done = owned.setdefault(j, [])
        done.append(along_a(tie(owner_sum(j, halves[len(done)]), *after), j))

    def during_back(step, found):
        if step == 1:
            return [far_sums[0]]
        if step == 2:
            return [near_sums[0]] + [moved[k, middle] for k in range(1, n_b)]
        if step == 3:
            give_back(middle)
            return owned[middle] + [moved[k, j] for k in range(1, n_b) for j in shifts[:1]]
        return ()

    grad_back = group_ring.scatter(back_part, during_back)
    if not owned:
        give_back(middle)
    give_back(middle, *owned[middle])
    grad_back = tie(grad_back, *owned[middle])
    mixed = grad_back[:, :D]
    grad_rows = grad_back[:, D : 2 * D]
    grad_combine = grad_back[:, 2 * D : 2 * D + EXPERTS]
    output = (resid + mixed).astype(BF16)

    grad_router_probs = grad_combine * kept
    grad_logits = (
        router_probs
        * (grad_router_probs - jnp.sum(router_probs * grad_router_probs, axis=-1, keepdims=True))
    ).astype(BF16)
    grad_router_full = ein("td,te->de", hidden_second, grad_logits)
    grad_hidden_second = dot(grad_logits, router_weight) + grad_rows
    grad_ffn_gain = jnp.sum(grad_hidden_second * normed_second, axis=0)
    grad_resid = grad_output + norm_back(grad_hidden_second, normed_second, inv_second, ffn_gain)
    grad_attn_out = grad_resid.astype(BF16)
    first = shifts[:1] if n_a > 2 else []
    blocks = ctx_ring.gather(
        grad_attn_out, {3: [moved[k, j] for k in range(1, n_b) for j in shifts[1:-1]]}
    )
    for j in first:
        give_back(j, blocks[n_c // 2])
    for k in range(1, n_b):
        moved[k, 0] = along_b_back(tie(far_sums[(k - 1) * n_a], blocks[n_c // 2]), k)
    grad_attended, grad_out = project_back_call(ctx_spots, blocks, attended, out_weight)
    owned[0] = [owner_sum(0)]

    stages = []

    def over_exp(values):
        core, at_y = at_e % 2, at_e // 2
        axis = values.ndim - 4
        keep = lax.dynamic_index_in_dim(values, core, axis + 1, False).astype(F32)
        give = lax.dynamic_index_in_dim(values, 1 - core, axis + 1, False)
        keep = keep + lax.ppermute(give, ALL, swap_cores).astype(F32)
        stages.append(keep)
        total = lax.dynamic_index_in_dim(keep, at_y, axis, False)
        for k in range(1, n_y):
            give = lax.dynamic_index_in_dim(keep, (at_y + k) % n_y, axis, False).astype(BF16)
            onward = [(i, i - i % n_e + (i % n_e + 2 * k) % n_e) for i in range(n_all)]
            total = total + lax.ppermute(give, ALL, onward).astype(F32)
        return total

    grad_out = over_exp(grad_out.reshape(n_y, 2, rows, D))

    weighted, grad_values, grad_head_gains, sums = attend_back_call(
        raw, stats, head_gains, cosine, sine, grad_attended
    )
    sums = over_heads(
        tie(sums, *[owned[j][0] for j in first])
    )
    for j in first:
        give_back(j, *owned[j])
    stats = jnp.where(kinds < 3, stats, jnp.roll(sums, 3, axis=0))
    stats = tie(stats, *[owned[j][1] for j in first], *[moved[k, 0] for k in range(1, n_b)])
    for j in shifts[1:-1]:
        give_back(j, *[owned[i][1] for i in first])
        give_back(j, *owned[j])
    grad_raw, grad_hidden = grad_heads_call(ring_order, weighted, raw, stats, grad_values, head_weight)
    grad_heads = ein("td,tf->df", hidden_first.reshape(span, D), grad_raw).astype(BF16)
    grad_heads = over_exp(grad_heads.reshape(n_c, n_y, 2, rows, 3 * slab))
    grad_heads = grad_heads.astype(BF16)

    def during_first(step, found):
        if step == 1:
            return stages[-1:]
        return [grad_heads] + [owned[j][1] for j in shifts[1:-1]] if step == 2 else ()

    waits = [owned[j][0] for j in shifts[1:-1]]
    grad_hidden_first = ctx_ring.scatter(lambda k: grad_hidden[k], during_first, waits)
    grad_heads = exchange(grad_heads, CTX).reshape(n_c, rows, 3, slab)
    grad_hidden_first = tie(grad_hidden_first, grad_heads)
    grad_heads = grad_heads.transpose(2, 1, 0, 3).reshape(3, rows, D).astype(F32)

    grad_gate_sum, grad_up_sum, grad_down_sum = unpack_call(
        behind_experts, [owned[j] for j in range(n_a)]
    )

    inv_first = inv_root(inputs)
    normed_first = inputs * inv_first
    grad_attn_gain = jnp.sum(grad_hidden_first * normed_first, axis=0)
    grad_inputs = grad_resid + norm_back(grad_hidden_first, normed_first, inv_first, attn_gain)

    head_gains = grad_head_gains[:2].reshape(2, 1, n_e, rows)
    here = jnp.arange(n_c).reshape(1, n_c, 1, 1) == at_c
    head_gains = jnp.where(here, head_gains, 0.0).reshape(2, n_all, rows)
    sums = jnp.concatenate(
        [
            grad_router_full.T.reshape(EXPERTS, n_all, rows),
            grad_attn_gain.reshape(1, n_all, rows),
            head_gains,
            grad_ffn_gain.reshape(1, n_all, rows),
        ]
    )
    sums = exchange(sums.transpose(1, 0, 2).reshape(n_all, -1), ALL)
    sums = jnp.sum(sums, axis=0).reshape(EXPERTS + 4, rows)
    return (
        output[None],
        grad_inputs[None],
        grad_heads[0],
        grad_heads[1],
        grad_heads[2],
        grad_out,
        sums[:EXPERTS].T,
        sums[EXPERTS],
        sums[EXPERTS + 1],
        sums[EXPERTS + 2],
        sums[EXPERTS + 3],
        grad_gate_sum,
        grad_up_sum,
        grad_down_sum,
    )


def solution(mesh):
    n_c, n_e = mesh.shape["ctx"], mesh.shape["exp"]
    n_a = EXPERTS // n_e
    fine = Mesh(mesh.devices.reshape(n_a, n_c // n_a, n_e), ALL)
    rows, blocks = P(ALL, None), P("exp", CTX, None)
    return jax.shard_map(
        shards,
        mesh=fine,
        in_specs=(blocks, P("exp", CTX), blocks, blocks)
        + (rows,) * 5
        + (P(ALL),) * 4
        + (blocks, blocks, P("exp", None, CTX), blocks),
        out_specs=(blocks, blocks)
        + (rows,) * 5
        + (P(ALL),) * 4
        + (blocks, blocks, P("exp", None, CTX)),
        check_vma=False,
    )
```

```python
import functools

import jax
import jax.numpy as jnp
from jax import lax
from jax.experimental import pallas as pl
from jax.experimental.pallas import tpu as pltpu
from jax.sharding import Mesh, PartitionSpec as P

D = 2048
H = 16
HD = 128
EXPERTS = 16
WINDOW = 1024
CAP = 64

EPS = 1e-05
NEG = -1000000000.0
HIGH = lax.Precision.HIGHEST
F32 = jnp.float32
BF16 = jnp.bfloat16

VMEM_LIMIT = 60 * 1024 * 1024

CTX = ("a", "b")
GROUP = ("a", "exp")
ALL = ("a", "b", "exp")


def dot(left, right):
    return jnp.dot(left, right, preferred_element_type=F32)


def ein(spec, left, right):
    return jnp.einsum(spec, left, right, preferred_element_type=F32)


def exchange(block, axes):
    return lax.all_to_all(block, axes, split_axis=0, concat_axis=0, tiled=True)


def inv_root(values):
    return lax.rsqrt(jnp.mean(values * values, axis=-1, keepdims=True) + EPS)


def norm_back(grad_normed, normed, inverse, gain):
    weighted = grad_normed * gain
    return inverse * (weighted - normed * jnp.mean(weighted * normed, axis=-1, keepdims=True))


def angles(span):
    half = HD // 2
    freqs = 10000.0 ** (-2.0 * jnp.arange(half, dtype=F32) / HD)
    angle = jnp.arange(span, dtype=jnp.int32).astype(F32)[:, None] * freqs[None, :]
    cosine, sine = jnp.cos(angle), jnp.sin(angle)
    return jnp.concatenate([cosine, cosine], axis=1), jnp.concatenate([-sine, sine], axis=1)


def pick(values, index, axis):
    spots = lax.broadcasted_iota(jnp.int32, values.shape, axis)
    return jnp.sum(jnp.where(spots == index, values, jnp.zeros_like(values)), axis=axis)


def contract(left, right, dims):
    return lax.dot_general(left, right, ((dims[:1], dims[1:]), ((), ())), preferred_element_type=F32)

def expert_body(n_blocks, n_parts, where_ref, *refs):
    blocks, refs = refs[:n_blocks], refs[n_blocks:]
    parts, refs = refs[:n_parts], refs[n_parts:]
    saved_hbm, sent, refs = refs[:5], refs[5:7], refs[7:]
    saved, refs = refs[:5], refs[5:]
    rows_ref, grad_out_ref, act_ref, grad_gate_ref, grad_up_ref = saved
    hidden, weights, slot_grads, place, weigh, dots, sems = refs
    slab = parts[0].shape[1]
    fetched = [pltpu.make_async_copy(b, hidden.at[k], sems.at[0, k]) for k, b in enumerate(blocks)]
    for copy in fetched:
        copy.start()
    copies = []
    for i, part in enumerate(parts):
        spot = pl.multiple_of(where_ref[1 + i] * slab, slab)
        target = weights.at[:, pl.ds(spot, slab), :]
        copies.append(pltpu.make_async_copy(part, target, sems.at[2, i]))
        copies[-1].start()
    expert = where_ref[0]
    length = hidden.shape[1]
    pair = 2 * length
    lane = lax.broadcasted_iota(jnp.int32, (pair, HD), 1)
    slot = lax.broadcasted_iota(jnp.int32, (pair, 2 * CAP), 1)
    slot -= CAP * (lax.broadcasted_iota(jnp.int32, slot.shape, 0) // length)
    slot = jnp.where((slot >= 0) & (slot < CAP), slot, CAP).astype(F32)
    for k in range(n_blocks // 2):
        fetched[2 * k].wait()
        fetched[2 * k + 1].wait()
        rows = pl.ds(2 * k * CAP, 2 * CAP)
        two = slice(2 * k, 2 * k + 2)
        tags = hidden[two, :, D : D + HD].reshape(pair, HD).astype(F32)
        share = jnp.sum(jnp.where(lane == expert, tags, 0.0), axis=1, keepdims=True)
        codes = jnp.where(lane == expert + EXPERTS, tags, 0.0)
        codes = jnp.sum(codes, axis=1, keepdims=True)
        chosen = (codes == slot).astype(F32)
        placing = chosen.astype(BF16)
        place[k] = placing
        weigh[k] = (chosen * share).astype(BF16)
        picked = contract(placing, hidden[two, :, :D].reshape(pair, D), (0, 0))
        rows_ref[rows, :] = picked.astype(BF16)
        picked = contract(placing, hidden[two, :, D + HD :].reshape(pair, D), (0, 0))
        slot_grads[rows, :] = picked.astype(BF16)
        row_share = contract(weigh[k], jnp.ones((pair, HD), BF16), (0, 0))[:, :1]
        grad_out_ref[rows, :] = (row_share * picked).astype(BF16)
    for copy in copies:
        copy.wait()
    chunk = 512
    width = weights.shape[2]

    @pl.loop(0, width // chunk)
    def _(i):
        cols = pl.ds(pl.multiple_of(i * chunk, chunk), chunk)
        gate = jnp.dot(rows_ref[...], weights[0, :, cols], preferred_element_type=F32)
        upper = jnp.dot(rows_ref[...], weights[1, :, cols], preferred_element_type=F32)
        grad_act = jnp.dot(grad_out_ref[...], weights[2, :, cols], preferred_element_type=F32)
        sigmoid = jax.nn.sigmoid(gate)
        silu = gate * sigmoid
        act_ref[:, cols] = (silu * upper).astype(BF16)
        grad_gate_ref[:, cols] = (
            grad_act * upper * sigmoid * (1.0 + gate * (1.0 - sigmoid))
        ).astype(BF16)
        grad_up_ref[:, cols] = (grad_act * silu).astype(BF16)

    keep = [
        pltpu.make_async_copy(ours, theirs, sems.at[3, i])
        for i, (ours, theirs) in enumerate(zip(saved, saved_hbm))
    ]
    for copy in keep:
        copy.start()
    dots[...] = jnp.zeros_like(dots)

    def target(k):
        half = n_blocks // 4
        return sent[k // half], slice(2 * (k % half), 2 * (k % half) + 2)

    @pl.loop(0, D // chunk)
    def _(i):
        cols = pl.ds(pl.multiple_of(i * chunk, chunk), chunk)
        out = contract(act_ref[...], weights[2, cols, :], (1, 1)).astype(BF16)
        product = out.astype(F32) * slot_grads[:, cols].astype(F32)
        for j in range(chunk // HD):
            dots[...] += product[:, j * HD : (j + 1) * HD]
        back = contract(grad_gate_ref[...], weights[0, cols, :], (1, 1))
        back += contract(grad_up_ref[...], weights[1, cols, :], (1, 1))
        back = back.astype(BF16)
        for k in range(n_blocks // 2):
            rows = slice(2 * k * CAP, 2 * (k + 1) * CAP)
            back_ref, two = target(k)
            mixed = jnp.dot(weigh[k], out[rows], preferred_element_type=F32).astype(BF16)
            back_ref[two, :, cols] = mixed.reshape(2, length, chunk)
            moved = jnp.dot(place[k], back[rows], preferred_element_type=F32).astype(BF16)
            later = pl.ds(pl.multiple_of(D + i * chunk, chunk), chunk)
            back_ref[two, :, later] = moved.reshape(2, length, chunk)

    total = jnp.sum(dots[...], axis=1, keepdims=True)
    for k in range(n_blocks // 2):
        mine = total[2 * k * CAP : 2 * (k + 1) * CAP]
        mine = jnp.broadcast_to(mine, (2 * CAP, HD)).astype(BF16)
        found = jnp.dot(place[k], mine, preferred_element_type=F32)
        found = jnp.where(lane == expert, found, 0.0).astype(BF16)
        back_ref, two = target(k)
        back_ref[two, :, 2 * D :] = found.reshape(2, length, HD)
    for copy in keep:
        copy.wait()


def expert_call(where, blocks, parts):
    n_blocks, (length, wide) = len(blocks), blocks[0].shape
    rows = n_blocks * CAP
    width = parts[0].shape[2]
    saved = [(rows, D), (rows, D), (rows, width), (rows, width), (rows, width)]
    sent = (n_blocks // 2, length, wide)
    anywhere = pl.BlockSpec(memory_space=pl.ANY)
    return pl.pallas_call(
        functools.partial(expert_body, n_blocks, len(parts)),
        out_shape=[jax.ShapeDtypeStruct(s, BF16) for s in saved + [sent] * 2],
        grid_spec=pltpu.PrefetchScalarGridSpec(
            num_scalar_prefetch=1,
            grid=(1,),
            in_specs=[anywhere] * (n_blocks + len(parts)),
            out_specs=[anywhere] * 5
            + [pl.BlockSpec(sent, lambda *_: (0, 0, 0), pipeline_mode=pl.Buffered(1))] * 2,
            scratch_shapes=[pltpu.VMEM(s, BF16) for s in saved]
            + [
                pltpu.VMEM((n_blocks, length, wide), BF16),
                pltpu.VMEM((3, D, width), BF16),
                pltpu.VMEM((rows, D), BF16),
                pltpu.VMEM((n_blocks // 2, 2 * length, 2 * CAP), BF16),
                pltpu.VMEM((n_blocks // 2, 2 * length, 2 * CAP), BF16),
                pltpu.VMEM((rows, HD), F32),
                pltpu.SemaphoreType.DMA((4, max(n_blocks, len(parts)))),
            ],
        ),
        compiler_params=pltpu.CompilerParams(vmem_limit_bytes=VMEM_LIMIT),
        cost_estimate=pl.CostEstimate(flops=13000000000, bytes_accessed=38000000, transcendentals=0),
        name="expert",
    )(where, *blocks, *parts)


def sums_body(n, where_ref, *refs):
    ins, outs = refs[: 5 * n], refs[5 * n :]
    rows, grad_out, act, grad_gate, grad_up = (ins[i * n : (i + 1) * n] for i in range(5))
    for i, out in enumerate(outs):

        @pl.when(pl.program_id(0) == i)
        def _():
            for j, (left, right) in enumerate(((rows, grad_gate), (rows, grad_up), (grad_out, act))):
                total = contract(left[0][...], right[0][...], (0, 0))
                for h in range(1, n):
                    total += contract(left[h][...], right[h][...], (0, 0))
                out[j] = total.astype(BF16)


def sums_call(where, saved, slab):
    n = len(saved)
    count = where.shape[0]
    length, width = saved[0][2].shape
    by_slab = pl.BlockSpec((length, slab), lambda i, ref: (0, ref[i]))
    fixed = pl.BlockSpec((length, width), lambda i, ref: (0, 0), pipeline_mode=pl.Buffered(1))
    args = [saved[h][j] for j in range(5) for h in range(n)]
    return pl.pallas_call(
        functools.partial(sums_body, n),
        out_shape=[jax.ShapeDtypeStruct((3, slab, width), BF16)] * count,
        grid_spec=pltpu.PrefetchScalarGridSpec(
            num_scalar_prefetch=1,
            grid=(count,),
            in_specs=[by_slab] * (2 * n) + [fixed] * (3 * n),
            out_specs=[
                pl.BlockSpec((3, slab, width), lambda i, ref: (0, 0, 0), pipeline_mode=pl.Buffered(1))
            ]
            * count,
        ),
        compiler_params=pltpu.CompilerParams(vmem_limit_bytes=VMEM_LIMIT),
        cost_estimate=pl.CostEstimate(flops=6500000000, bytes_accessed=30000000, transcendentals=0),
        name="expert_sums",
    )(where, *args)


def pack_body(where_ref, gate_ref, up_ref, down_ref, *outs):
    for i, out in enumerate(outs):

        @pl.when(pl.program_id(0) == i)
        def _():
            out[0] = gate_ref[0]
            out[1] = up_ref[0]
            out[2] = down_ref[0].T


def pack_call(where, gate, up, down):
    count, slab, width = gate.shape
    upright = pl.BlockSpec((1, slab, width), lambda i, ref: (ref[i], 0, 0))
    return pl.pallas_call(
        pack_body,
        out_shape=[jax.ShapeDtypeStruct((3, slab, width), BF16)] * count,
        grid_spec=pltpu.PrefetchScalarGridSpec(
            num_scalar_prefetch=1,
            grid=(count,),
            in_specs=[upright, upright, pl.BlockSpec((1, width, slab), lambda i, ref: (ref[i], 0, 0))],
            out_specs=[pl.BlockSpec((3, slab, width), lambda i, ref: (0, 0, 0))] * count,
        ),
        compiler_params=pltpu.CompilerParams(vmem_limit_bytes=VMEM_LIMIT),
        cost_estimate=pl.CostEstimate(flops=0, bytes_accessed=25000000, transcendentals=0),
        name="pack",
    )(where, gate, up, down)


def unpack_body(counts, where_ref, *refs):
    parts, (gate_ref, up_ref, down_ref) = refs[:-3], refs[-3:]
    at = 0
    for i, count in enumerate(counts):

        @pl.when(pl.program_id(0) == i)
        def _(some=parts[at : at + count]):
            first = 0
            for part in some:
                rows = slice(first, first + part.shape[1])
                gate_ref[0, rows] = part[0].astype(F32)
                up_ref[0, rows] = part[1].astype(F32)
                down_ref[0, :, rows] = part[2].astype(F32).T
                first += part.shape[1]

        at += count


def unpack_call(where, parts):
    count = len(parts)
    width = parts[0][0].shape[2]
    slab = sum(part.shape[1] for part in parts[0])
    flat = [part for some in parts for part in some]
    upright = pl.BlockSpec((1, slab, width), lambda i, ref: (ref[i], 0, 0))
    return pl.pallas_call(
        functools.partial(unpack_body, [len(some) for some in parts]),
        out_shape=[jax.ShapeDtypeStruct((count, slab, width), F32)] * 2
        + [jax.ShapeDtypeStruct((count, width, slab), F32)],
        grid_spec=pltpu.PrefetchScalarGridSpec(
            num_scalar_prefetch=1,
            grid=(count,),
            in_specs=[
                pl.BlockSpec(part.shape, lambda i, ref: (0, 0, 0), pipeline_mode=pl.Buffered(1))
                for part in flat
            ],
            out_specs=[upright, upright, pl.BlockSpec((1, width, slab), lambda i, ref: (ref[i], 0, 0))],
        ),
        compiler_params=pltpu.CompilerParams(vmem_limit_bytes=VMEM_LIMIT),
        cost_estimate=pl.CostEstimate(flops=0, bytes_accessed=32000000, transcendentals=0),
        name="unpack",
    )(where, *flat)


def heads_body(n_blocks, where_ref, *refs):
    blocks, refs = refs[:n_blocks], refs[n_blocks:]
    gain_ref, weight_ref, hidden_ref, raw_hbm, sums_ref, tokens, raw_all, sems = refs
    step = pl.program_id(0)
    length = tokens.shape[1]
    copies = [pltpu.make_async_copy(b, tokens.at[k], sems.at[0, k]) for k, b in enumerate(blocks)]

    def raw_copy(k):
        rows = pl.ds(pl.multiple_of(where_ref[k] * length, length), length)
        return pltpu.make_async_copy(raw_all.at[k], raw_hbm.at[rows], sems.at[1, k])

    @pl.when(step == 0)
    def _():
        for copy in copies:
            copy.start()

    for k in range(0, n_blocks, 2):

        @pl.when(step == k // 2)
        def _():
            copies[k].wait()
            copies[k + 1].wait()

    values = tokens[pl.ds(2 * step, 2)].reshape(2 * length, D).astype(F32)
    hidden = (values * inv_root(values) * gain_ref[...]).astype(BF16)
    for i in range(2):
        k = 2 * step + i
        hidden_ref[lax.rem(n_blocks - k, n_blocks)] = hidden[i * length : (i + 1) * length]
    raw = jnp.dot(hidden, weight_ref[...], preferred_element_type=F32)
    slab = raw.shape[1] // 3
    query, key = raw[:, :slab], raw[:, slab : 2 * slab]
    sums = by_token(
        jnp.sum(query * query, axis=1, keepdims=True), jnp.sum(key * key, axis=1, keepdims=True)
    )
    for i in range(2):
        k = 2 * step + i
        rows = slice(i * length, (i + 1) * length)
        raw_all[k] = raw[rows]
        raw_copy(k).start()
        sums_ref[:, pl.ds(pl.multiple_of(where_ref[k] * length, length), length)] = sums[:, rows]

    @pl.when(step == n_blocks // 2 - 1)
    def _():
        for k in range(n_blocks):
            raw_copy(k).wait()


def by_token(first, second):
    lane = lax.broadcasted_iota(jnp.int32, (first.shape[0], HD), 1)
    both = jnp.where(lane == 0, first, jnp.where(lane == 1, second, 0.0))
    return both.T[:8]


def heads_call(where, blocks, gain, weight):
    count, (length, _), wide = len(blocks), blocks[0].shape, weight.shape[1]
    span = count * length
    return pl.pallas_call(
        functools.partial(heads_body, count),
        grid_spec=pltpu.PrefetchScalarGridSpec(
            num_scalar_prefetch=1,
            grid=(count // 2,),
            in_specs=[pl.BlockSpec(memory_space=pl.ANY)] * count
            + [
                pl.BlockSpec((1, D), lambda i, ref: (0, 0)),
                pl.BlockSpec((D, wide), lambda i, ref: (0, 0), pipeline_mode=pl.Buffered(1)),
            ],
            out_specs=[
                pl.BlockSpec(
                    (count, length, D), lambda i, ref: (0, 0, 0), pipeline_mode=pl.Buffered(1)
                ),
                pl.BlockSpec(memory_space=pl.ANY),
                pl.BlockSpec((8, span), lambda i, ref: (0, 0)),
            ],
            scratch_shapes=[
                pltpu.VMEM((count, length, D), BF16),
                pltpu.VMEM((count, length, wide), F32),
                pltpu.SemaphoreType.DMA((2, count)),
            ],
        ),
        out_shape=[
            jax.ShapeDtypeStruct((count, length, D), BF16),
            jax.ShapeDtypeStruct((span, wide), F32),
            jax.ShapeDtypeStruct((8, span), F32),
        ],
        compiler_params=pltpu.CompilerParams(vmem_limit_bytes=VMEM_LIMIT),
        cost_estimate=pl.CostEstimate(flops=3300000000, bytes_accessed=12000000, transcendentals=0),
        name="heads",
    )(where, *blocks, gain, weight)


def by_two(shape, axis):
    def spec(i):
        def place(step, ref):
            at = ref[2 * step + i]
            return (at, 0) if axis == 0 else (0, at)

        return pl.BlockSpec(shape, place)

    return [spec(0), spec(1)]


def project_body(order_ref, first_ref, second_ref, weight_ref, out_ref):
    attended = jnp.concatenate([first_ref[...], second_ref[...]], axis=0)
    found = jnp.dot(attended, weight_ref[...], preferred_element_type=F32)
    out_ref[...] = found.astype(BF16).reshape(out_ref.shape)


def project_call(order, attended, weight):
    span, slab = attended.shape
    count = order.shape[0]
    length = span // count
    return pl.pallas_call(
        project_body,
        out_shape=jax.ShapeDtypeStruct((count, length, D), BF16),
        grid_spec=pltpu.PrefetchScalarGridSpec(
            num_scalar_prefetch=1,
            grid=(count // 2,),
            in_specs=by_two((length, slab), 0)
            + [pl.BlockSpec((slab, D), lambda i, ref: (0, 0), pipeline_mode=pl.Buffered(1))],
            out_specs=pl.BlockSpec((2, length, D), lambda i, ref: (i, 0, 0)),
        ),
        compiler_params=pltpu.CompilerParams(vmem_limit_bytes=VMEM_LIMIT),
        cost_estimate=pl.CostEstimate(flops=1100000000, bytes_accessed=6000000, transcendentals=0),
        name="project",
    )(order, attended, attended, weight)


def project_back_body(n_blocks, where_ref, *refs):
    blocks, refs = refs[:n_blocks], refs[n_blocks:]
    first_ref, second_ref, weight_ref, grad_ref, sum_ref, grads, total, sems = refs
    step = pl.program_id(0)
    length = grads.shape[1]
    copies = [pltpu.make_async_copy(b, grads.at[k], sems.at[k]) for k, b in enumerate(blocks)]

    @pl.when(step == 0)
    def _():
        for copy in copies:
            copy.start()
        total[...] = jnp.zeros_like(total)

    for k in range(0, n_blocks, 2):

        @pl.when(step == k // 2)
        def _():
            copies[k].wait()
            copies[k + 1].wait()

    mine = grads[pl.ds(2 * step, 2)].reshape(2 * length, D)
    found = contract(mine, weight_ref[...], (1, 1)).astype(BF16)
    for i in range(2):
        rows = pl.ds(pl.multiple_of(where_ref[2 * step + i] * length, length), length)
        grad_ref[rows, :] = found[i * length : (i + 1) * length]
    attended = jnp.concatenate([first_ref[...], second_ref[...]], axis=0)
    total[...] += contract(attended, mine, (0, 0))

    @pl.when(step == n_blocks // 2 - 1)
    def _():
        sum_ref[...] = total[...].astype(BF16)


def project_back_call(where, blocks, attended, weight):
    span, slab = attended.shape
    count, (length, _) = len(blocks), blocks[0].shape
    return pl.pallas_call(
        functools.partial(project_back_body, count),
        out_shape=[jax.ShapeDtypeStruct((span, slab), BF16), jax.ShapeDtypeStruct((slab, D), BF16)],
        grid_spec=pltpu.PrefetchScalarGridSpec(
            num_scalar_prefetch=1,
            grid=(count // 2,),
            in_specs=[pl.BlockSpec(memory_space=pl.ANY)] * count
            + by_two((length, slab), 0)
            + [pl.BlockSpec((slab, D), lambda i, ref: (0, 0), pipeline_mode=pl.Buffered(1))],
            out_specs=[
                pl.BlockSpec((span, slab), lambda i, ref: (0, 0)),
                pl.BlockSpec((slab, D), lambda i, ref: (0, 0)),
            ],
            scratch_shapes=[
                pltpu.VMEM((count, length, D), BF16),
                pltpu.VMEM((slab, D), F32),
                pltpu.SemaphoreType.DMA((count,)),
            ],
        ),
        compiler_params=pltpu.CompilerParams(vmem_limit_bytes=VMEM_LIMIT),
        cost_estimate=pl.CostEstimate(flops=2200000000, bytes_accessed=10000000, transcendentals=0),
        name="project_back",
    )(where, *blocks, attended, attended, weight)


def turn(values, cosine, sine, sign):
    return values * cosine + sign * pltpu.roll(values, HD // 2, 1) * sine


def ready(head, raw_ref, stats, gains_ref, cosine, sine):
    slab = raw_ref.shape[1] // 3
    cols = slice(head * HD, (head + 1) * HD)
    found = []
    for j in range(2):
        inverse = lax.rsqrt(stats[:, j : j + 1] / D + EPS)
        hat = raw_ref[:, j * slab + head * HD : j * slab + (head + 1) * HD] * inverse
        gain = gains_ref[j : j + 1, cols]
        found.append((turn(hat * gain, cosine, sine, 1.0).astype(BF16), hat, gain))
    value = raw_ref[:, 2 * slab + head * HD : 2 * slab + (head + 1) * HD].astype(BF16)
    return found[0], found[1], value


def soften(first, last, query, key_ref, stats, docs, low):
    scores = contract(query, key_ref[low:last, :], (1, 1)) * HD ** (-0.5)
    row = first + lax.broadcasted_iota(jnp.int32, scores.shape, 0)
    col = low + lax.broadcasted_iota(jnp.int32, scores.shape, 1)
    offset = row - col
    allowed = (offset >= 0) & (offset < WINDOW) & (stats[first:last, 2:3] == docs[:, low:last])
    scores = jnp.where(allowed, scores, NEG)
    expo = jnp.exp(scores - jnp.max(scores, axis=1, keepdims=True))
    return expo * (1.0 / jnp.sum(expo, axis=1, keepdims=True))


def ranges(span):
    rows, reach = 256, min(WINDOW, span // 2)
    return [(i, i + rows, max(0, (i - reach) // rows * rows)) for i in range(0, span, rows)]


def attend_body(raw_ref, rows_ref, gains_ref, cosine_ref, sine_ref, out_ref, key_ref):
    span = raw_ref.shape[0]
    stats = rows_ref[...].T
    docs = rows_ref[2:3, :]
    for head in range(out_ref.shape[1] // HD):
        (query, _, _), (key, _, _), value = ready(
            head, raw_ref, stats, gains_ref, cosine_ref[...], sine_ref[...]
        )
        key_ref[...] = key
        for first, last, low in ranges(span):
            probs = soften(first, last, query[first:last], key_ref, stats, docs, low)
            out_ref[first:last, head * HD : (head + 1) * HD] = jnp.dot(
                probs.astype(BF16), value[low:last], preferred_element_type=F32
            ).astype(BF16)


def attend_call(raw, rows, gains, cosine, sine):
    span, wide = raw.shape
    return pl.pallas_call(
        attend_body,
        out_shape=jax.ShapeDtypeStruct((span, wide // 3), BF16),
        scratch_shapes=[pltpu.VMEM((span, HD), BF16)],
        compiler_params=pltpu.CompilerParams(vmem_limit_bytes=VMEM_LIMIT),
        cost_estimate=pl.CostEstimate(flops=1000000000, bytes_accessed=6000000, transcendentals=0),
        name="attend",
    )(raw, rows, gains, cosine, sine)


def attend_back_body(
    raw_ref,
    rows_ref,
    gains_ref,
    cosine_ref,
    sine_ref,
    grad_ref,
    weighted_ref,
    grad_values_ref,
    grad_gains_ref,
    sums_ref,
    key_ref,
    grad_query,
    grad_key,
    grad_value,
):
    span = raw_ref.shape[0]
    slab = grad_ref.shape[1]
    stats = rows_ref[...].T
    docs = rows_ref[2:3, :]
    cosine, sine = cosine_ref[...], sine_ref[...]
    grad_gains_ref[...] = jnp.zeros_like(grad_gains_ref)
    totals = [jnp.zeros((span, 1), F32), jnp.zeros((span, 1), F32)]
    for head in range(slab // HD):
        cols = slice(head * HD, (head + 1) * HD)
        (query, query_hat, query_gain), (key, key_hat, key_gain), value = ready(
            head, raw_ref, stats, gains_ref, cosine, sine
        )
        key_ref[...] = key
        grad_key[...] = jnp.zeros_like(grad_key)
        grad_value[...] = jnp.zeros_like(grad_value)
        for first, last, low in ranges(span):
            probs = soften(first, last, query[first:last], key_ref, stats, docs, low)
            grad_out = grad_ref[first:last, cols]
            grad_probs = contract(grad_out, value[low:last], (1, 1))
            inner = jnp.sum(probs * grad_probs, axis=1, keepdims=True)
            grad_scores = (probs * (grad_probs - inner)).astype(BF16)
            grad_query[first:last, :] = jnp.dot(
                grad_scores, key_ref[low:last, :], preferred_element_type=F32
            )
            grad_key[low:last, :] += contract(grad_scores, query[first:last], (0, 0))
            grad_value[low:last, :] += contract(probs.astype(BF16), grad_out, (0, 0))
        grad_values_ref[:, cols] = grad_value[...].astype(BF16)
        for j, (grad, hat, gain) in enumerate(
            ((grad_query, query_hat, query_gain), (grad_key, key_hat, key_gain))
        ):
            grad_norm = turn(grad[...] * HD ** (-0.5), cosine, sine, -1.0)
            grad_gains_ref[j : j + 1, cols] = jnp.sum(grad_norm * hat, axis=0, keepdims=True)
            weighted = grad_norm * gain
            weighted_ref[:, j * slab + head * HD : j * slab + (head + 1) * HD] = weighted
            totals[j] += jnp.sum(weighted * hat, axis=1, keepdims=True)
    sums_ref[...] = by_token(*totals)


def attend_back_call(raw, rows, gains, cosine, sine, grad):
    span, slab = grad.shape
    return pl.pallas_call(
        attend_back_body,
        out_shape=[
            jax.ShapeDtypeStruct((span, 2 * slab), F32),
            jax.ShapeDtypeStruct((span, slab), BF16),
            jax.ShapeDtypeStruct((8, slab), F32),
            jax.ShapeDtypeStruct((8, span), F32),
        ],
        scratch_shapes=[pltpu.VMEM((span, HD), BF16)] + [pltpu.VMEM((span, HD), F32)] * 3,
        compiler_params=pltpu.CompilerParams(vmem_limit_bytes=VMEM_LIMIT),
        cost_estimate=pl.CostEstimate(flops=2000000000, bytes_accessed=8000000, transcendentals=0),
        name="attend_back",
    )(raw, rows, gains, cosine, sine, grad)


def grad_heads_body(order_ref, *refs):
    pairs, (weight_ref, raw_out_ref, hidden_out_ref) = refs[:8], refs[8:]
    slab = pairs[6].shape[1]
    for i in range(2):
        weighted_ref, raw_ref, rows_ref, grad_values_ref = pairs[i::2]
        length = raw_ref.shape[0]
        rows = slice(i * length, (i + 1) * length)
        stats = rows_ref[...].T
        for j in range(2):
            cols = slice(j * slab, (j + 1) * slab)
            inverse = lax.rsqrt(stats[:, j : j + 1] / D + EPS)
            hat = raw_ref[:, cols] * inverse
            mean = stats[:, 3 + j : 4 + j] / D
            raw_out_ref[rows, cols] = (inverse * (weighted_ref[:, cols] - hat * mean)).astype(BF16)
        raw_out_ref[rows, 2 * slab :] = grad_values_ref[...]
    found = contract(raw_out_ref[...], weight_ref[...], (1, 1)).astype(BF16)
    hidden_out_ref[...] = found.reshape(hidden_out_ref.shape)


def grad_heads_call(order, weighted, raw, rows, grad_values, weight):
    span, slab = grad_values.shape
    count = order.shape[0]
    length = span // count
    return pl.pallas_call(
        grad_heads_body,
        out_shape=[
            jax.ShapeDtypeStruct((span, 3 * slab), BF16),
            jax.ShapeDtypeStruct((count, length, D), BF16),
        ],
        grid_spec=pltpu.PrefetchScalarGridSpec(
            num_scalar_prefetch=1,
            grid=(count // 2,),
            in_specs=by_two((length, 2 * slab), 0)
            + by_two((length, 3 * slab), 0)
            + by_two((8, length), 1)
            + by_two((length, slab), 0)
            + [pl.BlockSpec((D, 3 * slab), lambda i, ref: (0, 0), pipeline_mode=pl.Buffered(1))],
            out_specs=[
                pl.BlockSpec((2 * length, 3 * slab), lambda i, ref: (i, 0)),
                pl.BlockSpec((2, length, D), lambda i, ref: (i, 0, 0)),
            ],
        ),
        compiler_params=pltpu.CompilerParams(vmem_limit_bytes=VMEM_LIMIT),
        cost_estimate=pl.CostEstimate(flops=3300000000, bytes_accessed=16000000, transcendentals=0),
        name="grad_heads",
    )(order, weighted, weighted, raw, raw, rows, rows, grad_values, grad_values, weight)


def tie(value, *others):
    return lax.optimization_barrier((value, others))[0]


def cycle(high, low):
    cells = [(0, j) for j in range(low)]
    for i in range(1, high):
        columns = range(low - 1, 0, -1) if i % 2 else range(1, low)
        cells += [(i, j) for j in columns]
    cells += [(i, 0) for i in range(high - 1, 0, -1)]
    return [i * low + j for i, j in cells]


class Ring:
    def __init__(self, count, groups):
        self.count = count
        self.onward, self.backward = [], []
        self.device = {}
        for members in groups:
            for i, member in enumerate(members):
                after = members[(i + 1) % count]
                self.onward.append((member, after))
                self.backward.append((after, member))
                self.device[member] = i

    def gather(self, block, waits=None, other=None, visit=None):
        found, passed = {0: block}, {}
        ahead = behind = block
        fresh = [0]
        for step in range(1, self.count // 2 + 1):
            if waits and step in waits:
                behind = tie(behind, *waits[step])
            if other is not None:
                passed.update({k: other(found[k]) for k in fresh})
            held = [passed[k] for k in fresh if k in passed]
            behind = lax.ppermute(behind, ALL, self.onward)
            if step < (self.count + 1) // 2:
                ahead = lax.ppermute(ahead, ALL, self.backward)
            behind, ahead, *held = lax.optimization_barrier((behind, ahead, *held))
            for k, value in zip(fresh, held):
                passed[k] = value
            fresh = [step]
            found[step] = behind
            if step < (self.count + 1) // 2:
                found[self.count - step] = ahead
                fresh.append(self.count - step)
            if visit is not None and step < self.count // 2:
                waits = {**(waits or {}), step + 1: visit(step, found, passed)}
        found = [found[k] for k in range(self.count)]
        if other is None:
            return found
        last = visit(self.count // 2, found, passed) if visit is not None else ()
        passed.update({k: other(tie(found[k], *last)) for k in fresh})
        return found, [passed[k] for k in range(self.count)]

    def scatter(self, part, visit=None, waits=()):
        half = self.count // 2
        far = self.count - half - 1
        onward = backward = None
        for k in range(half, -1, -1):
            term = part(k).astype(F32) if onward is None else onward.astype(F32) + part(k).astype(F32)
            if k == 0:
                return term if backward is None else term + backward.astype(F32)
            term = term.astype(BF16)
            if waits:
                term = tie(term, *waits)
            onward = lax.ppermute(term, ALL, self.onward)
            if k <= far:
                term = part(self.count - k).astype(F32)
                if backward is not None:
                    term = term + backward.astype(F32)
                backward = lax.ppermute(term.astype(BF16), ALL, self.backward)
                onward, backward = lax.optimization_barrier((onward, backward))
            waits = visit(half - k + 1, onward) if visit is not None else ()


def shards(
    tokens,
    doc_ids,
    expert_ids,
    drop_order,
    w_query,
    w_key,
    w_value,
    w_out,
    w_router,
    gain_attn,
    gain_query,
    gain_key,
    gain_ffn,
    w_gate,
    w_up,
    w_down,
    cotangent,
):
    n_a, n_b, n_e = (lax.axis_size(name) for name in ALL)
    n_c = n_a * n_b
    n_all = n_c * n_e
    group = n_a * n_e
    length = tokens.shape[1]
    span = n_c * length
    slab = D // n_c
    rows = D // n_all
    at_a, at_b, at_e = (lax.axis_index(name) for name in ALL)
    at_c = at_a * n_b + at_b
    expert = at_e * n_a + at_a
    at_all = at_c * n_e + at_e

    walk = cycle(n_a, n_b) if n_b % 2 == 0 and n_a % 2 == 0 else list(range(n_c))
    ctx_ring = Ring(n_c, [[c * n_e + e for c in walk] for e in range(n_e)])
    n_y = n_e // 2
    n_ring = n_a * n_y
    y_walk = cycle(n_a, n_y)
    group_ring = Ring(
        n_ring,
        [
            [((w // n_y) * n_b + b) * n_e + (w % n_y) * 2 + core for w in y_walk]
            for b in range(n_b)
            for core in range(2)
        ],
    )
    swap_cores = [(i, i + 1 - 2 * (i % 2)) for i in range(n_all)]
    table = []
    for i in range(n_all):
        c, e = divmod(i, n_e)
        a, b = divmod(c, n_b)
        p, q = ctx_ring.device[i], group_ring.device[i]
        line = [walk[(p - k) % n_c] for k in range(n_c)]
        for core in (1 - e % 2, e % 2):
            for k in range(n_ring):
                w = y_walk[(q - k) % n_ring]
                line.append((w // n_y) * n_e + (w % n_y) * 2 + core)
        line += [(a + k) % n_a for k in range(n_a)] + [(a - k) % n_a for k in range(n_a)]
        line += [((a - j) % n_a) * n_b + (b + k) % n_b for k in range(n_b) for j in range(n_a)]
        line += [((a + j) % n_a) * n_b + (b + k) % n_b for k in range(n_b) for j in range(n_a)]
        table.append(line)
    line = lax.dynamic_slice_in_dim(jnp.array(table, jnp.int32), at_all, 1, 0)[0]
    cuts = [n_c, 2 * n_ring, n_a, n_a, n_c, n_c]
    ends = [sum(cuts[: i + 1]) for i in range(len(cuts))]
    ctx_spots, group_spots, onward_experts, behind_experts, weight_slabs, grad_slabs = (
        line[end - cut : end] for cut, end in zip(cuts, ends)
    )

    vectors = jnp.stack([gain_attn, gain_query, gain_key, gain_ffn])
    small = jnp.concatenate([w_router.T, vectors]).reshape(-1)
    small = jnp.concatenate([small, doc_ids[0].astype(BF16)])
    small = exchange(jnp.broadcast_to(small[None], (n_all, small.shape[0])), ALL)
    params = small[:, : (EXPERTS + 4) * rows].reshape(n_all, EXPERTS + 4, rows)
    params = params.transpose(1, 0, 2).reshape(EXPERTS + 4, D)
    router_weight = params[:EXPERTS]
    attn_gain, query_gain, key_gain, ffn_gain = params[EXPERTS:].astype(F32)
    documents = pick(small[:, (EXPERTS + 4) * rows :].reshape(n_c, n_e, length), at_e, 1)
    documents = documents.reshape(1, span)
    head_gains = jnp.stack([query_gain, key_gain])
    head_gains = lax.dynamic_slice_in_dim(head_gains, at_c * slab, slab, 1)
    cosine, sine = angles(span)

    def along_a(block, shift):
        return lax.ppermute(block, "a", [(j, (j + shift) % n_a) for j in range(n_a)])

    def along_b(block, shift):
        return lax.ppermute(block, "b", [((j + shift) % n_b, j) for j in range(n_b)])

    packed = pack_call(onward_experts, w_gate, w_up, w_down)
    near = [packed[0]] + [None] * (n_a - 1)
    middle = n_a // 2
    shifts = [j for j in range(1, n_a) if j != middle] + [middle]

    def fetch(j, *after):
        near[j] = along_a(tie(packed[j], *after), j)

    far = {}

    def share(j, *after):
        for k in range(1, n_b):
            far[k, j] = along_b(tie(near[j], *after), k)

    mine = jnp.stack([w_query, w_key, w_value]).reshape(3, rows, n_c, slab)
    mine = mine.transpose(2, 1, 0, 3).reshape(n_c, rows, 3 * slab)
    mine = exchange(mine, CTX)
    chain = list(range(1, n_a))
    blocks = ctx_ring.gather(tokens[0], {2: [packed[0]], 3: [mine]})
    head_weight = lax.all_gather(mine, "exp", axis=1, tiled=True).reshape(D, 3 * slab)
    out_weight = lax.all_gather(w_out, "exp", axis=0, tiled=True)
    ring_order = jnp.roll(ctx_spots[::-1], 1)

    expert_iota = jnp.arange(EXPERTS, dtype=jnp.int32)
    named = jnp.sum(
        (expert_ids[0][:, :, None] == expert_iota[None, None, :]).astype(F32), axis=1
    )
    order = drop_order[0, 0]
    earlier = (order[None, :] < order[:, None]).astype(F32)
    slots = jnp.dot(earlier, named, precision=HIGH, preferred_element_type=F32)
    kept = named * (slots < CAP).astype(F32)
    slot_code = jnp.where(kept > 0, slots, -1.0).astype(BF16)
    lanes = jnp.zeros((length, HD - 2 * EXPERTS), BF16)
    grad_rows_in = cotangent[0]
    grad_output = grad_rows_in.astype(F32)

    hidden_first, raw, sums = heads_call(ctx_spots, blocks, attn_gain[None], head_weight)

    def over_heads(values):
        values = exchange(jnp.broadcast_to(values[None], (n_c,) + values.shape), CTX)
        return jnp.sum(values, axis=0)

    kinds = lax.broadcasted_iota(jnp.int32, (8, span), 0)
    fetch(chain[0], blocks[n_c // 2])
    share(0, blocks[n_c // 2])
    stats = jnp.where(kinds == 2, documents.astype(F32), over_heads(sums))
    stats = tie(stats, near[chain[0]])
    attended = attend_call(raw, stats, head_gains, cosine, sine)
    partial = project_call(ring_order, attended, out_weight)
    middle_ones = chain[1:-1]
    for j in middle_ones:
        fetch(j, near[chain[0]])
    share(chain[0], near[chain[0]])

    def during_project(step, found):
        if step == 1:
            return [near[j] for j in middle_ones] + [far[k, chain[0]] for k in range(1, n_b)]
        if step == 2 and len(chain) > 1:
            fetch(chain[-1], *[near[j] for j in middle_ones])
            for j in middle_ones:
                share(j, near[j])
        return ()

    attended_out = ctx_ring.scatter(lambda k: partial[k], during_project)
    if len(chain) > 1:
        attended_out = tie(attended_out, near[chain[-1]])
    inputs = tokens[0].astype(F32)
    resid = inputs + attended_out
    inv_second = inv_root(resid)
    normed_second = resid * inv_second
    hidden_second = (normed_second * ffn_gain).astype(BF16)
    logits = ein("td,ed->te", hidden_second, router_weight)
    router_probs = jax.nn.softmax(logits, axis=-1)
    combine = (router_probs * kept).astype(BF16)

    block = jnp.concatenate([hidden_second, combine, slot_code, lanes, grad_rows_in], axis=1)
    if len(chain) > 1:
        share(chain[-1], near[chain[-1]])
    parts = near + [far[k, j] for k in range(1, n_b) for j in range(n_a)]
    where = jnp.concatenate([expert[None], weight_slabs])
    quarter = n_ring // 4
    soon = [k % n_ring for k in range(1 - quarter, quarter + 1)]
    late = [k for k in range(n_ring) if k not in soon]
    results = {}

    def during_rows(step, found, passed):
        if step == 1:
            return [far[k, j] for k in range(1, n_b) for j in middle_ones]
        if step == 2:
            return [far[k, chain[-1]] for k in range(1, n_b)]
        if step == quarter + 1:
            results["soon"] = expert_call(
                where, [passed[k] for k in soon] + [found[k] for k in soon], parts
            )
        if step == n_ring // 2:
            return [results["soon"][-1]]
        return ()

    ours, theirs = group_ring.gather(
        block, None, lambda found: lax.ppermute(found, ALL, swap_cores), during_rows
    )
    *given, give, keep = results["soon"]
    keeps = dict(zip(soon, keep))
    gots = dict(zip(soon, lax.ppermute(give, ALL, swap_cores)))
    *kept_here, give, keep = expert_call(
        where, [theirs[k] for k in late] + [ours[k] for k in late], parts
    )
    keeps.update(zip(late, keep))
    gots.update(zip(late, lax.ppermute(give, ALL, swap_cores)))

    def back_part(k):
        i = (n_ring - k) % n_ring
        return keeps[i].astype(F32) + gots[i].astype(F32)

    def along_b_back(block, shift):
        return lax.ppermute(block, "b", [(j, (j + shift) % n_b) for j in range(n_b)])

    saved = [given, kept_here]
    far_sums = sums_call(grad_slabs[n_a:], saved, slab)
    near_sums = sums_call(grad_slabs[:n_a], [[tie(given[0], far_sums[0])] + given[1:], kept_here], slab)
    moved = {}
    last = ()
    for j in [middle] + shifts[:-1]:
        for k in range(1, n_b):
            moved[k, j] = along_b_back(tie(far_sums[(k - 1) * n_a + j], *last), k)
        last = [moved[k, j] for k in range(1, n_b)]

    def owner_sum(j, rows=slice(None)):
        total = near_sums[j][:, rows].astype(F32)
        for k in range(1, n_b):
            total += moved[k, j][:, rows].astype(F32)
        return total.astype(BF16)

    cut = slab // 2
    halves = [slice(0, cut), slice(cut, slab)]
    owned = {}

    def give_back(j, *after):
        done = owned.setdefault(j, [])
        done.append(along_a(tie(owner_sum(j, halves[len(done)]), *after), j))

    def during_back(step, found):
        if step == 1:
            return [far_sums[0]]
        if step == 2:
            return [near_sums[0]] + [moved[k, middle] for k in range(1, n_b)]
        if step == 3:
            give_back(middle)
            return owned[middle] + [moved[k, j] for k in range(1, n_b) for j in shifts[:1]]
        return ()

    grad_back = group_ring.scatter(back_part, during_back)
    if not owned:
        give_back(middle)
    give_back(middle, *owned[middle])
    grad_back = tie(grad_back, *owned[middle][:1])
    mixed = grad_back[:, :D]
    grad_rows = grad_back[:, D : 2 * D]
    grad_combine = grad_back[:, 2 * D : 2 * D + EXPERTS]
    output = (resid + mixed).astype(BF16)

    grad_router_probs = grad_combine * kept
    grad_logits = (
        router_probs
        * (grad_router_probs - jnp.sum(router_probs * grad_router_probs, axis=-1, keepdims=True))
    ).astype(BF16)
    grad_router_full = ein("td,te->de", hidden_second, grad_logits)
    grad_hidden_second = dot(grad_logits, router_weight) + grad_rows
    grad_ffn_gain = jnp.sum(grad_hidden_second * normed_second, axis=0)
    grad_resid = grad_output + norm_back(grad_hidden_second, normed_second, inv_second, ffn_gain)
    grad_attn_out = grad_resid.astype(BF16)
    first = shifts[:1] if n_a > 2 else []
    blocks = ctx_ring.gather(
        grad_attn_out,
        {
            2: owned[middle][1:],
            3: [moved[k, j] for k in range(1, n_b) for j in shifts[1:-1]],
        },
    )
    for j in first:
        give_back(j, blocks[n_c // 2])
    for k in range(1, n_b):
        moved[k, 0] = along_b_back(tie(far_sums[(k - 1) * n_a], blocks[n_c // 2]), k)
    grad_attended, grad_out = project_back_call(ctx_spots, blocks, attended, out_weight)
    owned[0] = [owner_sum(0)]

    stages = []

    def over_exp(values):
        core, at_y = at_e % 2, at_e // 2
        axis = values.ndim - 4
        keep = lax.dynamic_index_in_dim(values, core, axis + 1, False).astype(F32)
        give = lax.dynamic_index_in_dim(values, 1 - core, axis + 1, False)
        keep = keep + lax.ppermute(give, ALL, swap_cores).astype(F32)
        stages.append(keep)
        total = lax.dynamic_index_in_dim(keep, at_y, axis, False)
        for k in range(1, n_y):
            give = lax.dynamic_index_in_dim(keep, (at_y + k) % n_y, axis, False).astype(BF16)
            onward = [(i, i - i % n_e + (i % n_e + 2 * k) % n_e) for i in range(n_all)]
            total = total + lax.ppermute(give, ALL, onward).astype(F32)
        return total

    grad_out = over_exp(grad_out.reshape(n_y, 2, rows, D))

    weighted, grad_values, grad_head_gains, sums = attend_back_call(
        raw, stats, head_gains, cosine, sine, grad_attended
    )
    sums = over_heads(
        tie(sums, *[owned[j][0] for j in first])
    )
    for j in first:
        give_back(j, *owned[j])
    stats = jnp.where(kinds < 3, stats, jnp.roll(sums, 3, axis=0))
    stats = tie(stats, *[owned[j][1] for j in first], *[moved[k, 0] for k in range(1, n_b)])
    for j in shifts[1:-1]:
        give_back(j, *[owned[i][1] for i in first])
        give_back(j, *owned[j])
    grad_raw, grad_hidden = grad_heads_call(ring_order, weighted, raw, stats, grad_values, head_weight)
    grad_heads = ein("td,tf->df", hidden_first.reshape(span, D), grad_raw).astype(BF16)
    grad_heads = over_exp(grad_heads.reshape(n_c, n_y, 2, rows, 3 * slab))
    grad_heads = grad_heads.astype(BF16)

    def during_first(step, found):
        if step == 1:
            return stages[-1:]
        return [grad_heads] + [owned[j][1] for j in shifts[1:-1]] if step == 2 else ()

    waits = [owned[j][0] for j in shifts[1:-1]]
    grad_hidden_first = ctx_ring.scatter(lambda k: grad_hidden[k], during_first, waits)
    grad_heads = exchange(grad_heads, CTX).reshape(n_c, rows, 3, slab)
    grad_hidden_first = tie(grad_hidden_first, grad_heads)
    grad_heads = grad_heads.transpose(2, 1, 0, 3).reshape(3, rows, D).astype(F32)

    grad_gate_sum, grad_up_sum, grad_down_sum = unpack_call(
        behind_experts, [owned[j] for j in range(n_a)]
    )

    inv_first = inv_root(inputs)
    normed_first = inputs * inv_first
    grad_attn_gain = jnp.sum(grad_hidden_first * normed_first, axis=0)
    grad_inputs = grad_resid + norm_back(grad_hidden_first, normed_first, inv_first, attn_gain)

    head_gains = grad_head_gains[:2].reshape(2, 1, n_e, rows)
    here = jnp.arange(n_c).reshape(1, n_c, 1, 1) == at_c
    head_gains = jnp.where(here, head_gains, 0.0).reshape(2, n_all, rows)
    sums = jnp.concatenate(
        [
            grad_router_full.T.reshape(EXPERTS, n_all, rows),
            grad_attn_gain.reshape(1, n_all, rows),
            head_gains,
            grad_ffn_gain.reshape(1, n_all, rows),
        ]
    )
    sums = exchange(sums.transpose(1, 0, 2).reshape(n_all, -1), ALL)
    sums = jnp.sum(sums, axis=0).reshape(EXPERTS + 4, rows)
    return (
        output[None],
        grad_inputs[None],
        grad_heads[0],
        grad_heads[1],
        grad_heads[2],
        grad_out,
        sums[:EXPERTS].T,
        sums[EXPERTS],
        sums[EXPERTS + 1],
        sums[EXPERTS + 2],
        sums[EXPERTS + 3],
        grad_gate_sum,
        grad_up_sum,
        grad_down_sum,
    )


def solution(mesh):
    n_c, n_e = mesh.shape["ctx"], mesh.shape["exp"]
    n_a = EXPERTS // n_e
    fine = Mesh(mesh.devices.reshape(n_a, n_c // n_a, n_e), ALL)
    rows, blocks = P(ALL, None), P("exp", CTX, None)
    return jax.shard_map(
        shards,
        mesh=fine,
        in_specs=(blocks, P("exp", CTX), blocks, blocks)
        + (rows,) * 5
        + (P(ALL),) * 4
        + (blocks, blocks, P("exp", None, CTX), blocks),
        out_specs=(blocks, blocks)
        + (rows,) * 5
        + (P(ALL),) * 4
        + (blocks, blocks, P("exp", None, CTX)),
        check_vma=False,
    )
```
